32 devices in a mesh: seq: 2 (over x), fsdp: 16 (over z, y, core).
Axes of the slice: x: 2, y: 2, z: 4, core: 2. Of those that a mesh axis runs over, the one named last changes fastest.
Arguments:
- tokens: bfloat16 [16, 1024, 1024], P('fsdp', 'seq'), may hold values from -6 to 6
- segments: int32 [16, 1024], P('fsdp'), may hold values from 0 to 2, as said below
- w_query: bfloat16 [1024, 1024], P('fsdp'), may hold values from -0.1875 to 0.1875
- w_key: bfloat16 [1024, 1024], P('fsdp'), may hold values from -0.1875 to 0.1875
- w_value: bfloat16 [1024, 1024], P('fsdp'), may hold values from -0.1875 to 0.1875
- w_gate: bfloat16 [1024, 1024], P('fsdp'), may hold values from -0.1875 to 0.1875
- w_out: bfloat16 [1024, 1024], P('fsdp'), may hold values from -0.1875 to 0.1875
- w_sglu_in: bfloat16 [1024, 5632], P('fsdp'), may hold values from -0.1875 to 0.1875
- w_sglu_down: bfloat16 [1024, 2816], P('fsdp'), may hold values from -0.109375 to 0.109375
- cotangent: bfloat16 [16, 1024, 1024], P('fsdp', 'seq'), may hold values from -6 to 6
Outputs:
- output: bfloat16 [16, 1024, 1024], P('fsdp', 'seq')
- input_grad: float32 [16, 1024, 1024], P('fsdp', 'seq')
- grad_query: float32 [1024, 1024], P('fsdp')
- grad_key: float32 [1024, 1024], P('fsdp')
- grad_value: float32 [1024, 1024], P('fsdp')
- grad_gate: float32 [1024, 1024], P('fsdp')
- grad_out: float32 [1024, 1024], P('fsdp')
- grad_sglu_in: float32 [1024, 5632], P('fsdp')
- grad_sglu_down: float32 [1024, 2816], P('fsdp')
The draws below stay inside these ranges and needn't reach their ends.
Inputs may be any that keep to these rules, and one draw needn't show every extreme that they name: `segments`: in each sequence the numbers never fall, and each of 0, 1 and 2 covers at least 204 positions in a row.
All inputs are finite; a program needn't handle non-finite values.
Results may differ from the reference program's by a relative error of at most 0.014.
Values may be sent and summed in bfloat16 or wider, within the bound.
No kernel may reach another device: no remote copies, remote signals or barrier semaphores. Data moves between devices by JAX's collectives and lax.ppermute only.
A program may use at most 256 MiB of HBM per device.

```python
import math
import jax
import jax.numpy as jnp
from jax import lax

D = 1024
HEADS = 8
HEAD_DIM = 128
FF = 2816
LENGTH = 1024
SEQS = 16


def draw_segments(key, part):
    first_key = jax.random.fold_in(key, 11)
    second_key = jax.random.fold_in(key, 23)
    shortest = LENGTH // 5
    first_cut = jax.random.randint(first_key, (SEQS, 1), shortest, LENGTH - 2 * shortest + 1, dtype=jnp.int32)
    offsets = jax.random.randint(second_key, (SEQS, 1), 0, 1 << 20, dtype=jnp.int32)
    room = LENGTH - shortest + 1 - (first_cut + shortest)
    second_cut = first_cut + shortest + offsets % room
    places = jnp.arange(LENGTH, dtype=jnp.int32)[None, :]
    return (places >= first_cut).astype(jnp.int32) + (places >= second_cut).astype(jnp.int32)


def spiked(values, rng, source, target, shards_of, factor):
    owner, partner = [(jnp.arange(values.shape[dim]) // (values.shape[dim] // shards_of)).reshape([-1 if axis == dim else 1 for axis in range(values.ndim)]) for dim in (source, target)]
    chosen = jax.random.permutation(rng, shards_of)[partner]
    strong = (owner == chosen) | (owner == (partner + shards_of // 2) % shards_of)
    return jnp.where(strong, factor * values, values)


def levels(key, shape, cuts, least, largest):
    factor_of, own = 1.0, jax.random.fold_in(key, 6)
    for axis_at, parts in cuts:
        draws = jnp.exp(jax.random.uniform(jax.random.fold_in(own, axis_at), (parts,), jnp.float32, least / len(cuts), largest / len(cuts)))
        factor_of = factor_of * jnp.repeat(draws, shape[axis_at] // parts).reshape([-1 if axis == axis_at else 1 for axis in range(len(shape))])
    return factor_of


def centred(key, extent, deviation, reach, pieces=(), kind=jnp.bfloat16):
    values = deviation * jax.random.normal(key, extent, jnp.float32)
    if pieces:
        values = values * levels(key, extent, pieces, -0.22, 0.18)
    return jnp.clip(values, -reach, reach).astype(kind)


def bell_draw_with(key, dims, spread, reach, shards, heavy, kind=jnp.bfloat16):
    drawn = spread * jax.random.normal(key, dims, jnp.float32)
    if shards:
        drawn = drawn * levels(key, dims, shards, -0.22, 0.18)
    return jnp.clip(spiked(drawn, jax.random.fold_in(key, 3), *heavy), -reach, reach).astype(kind)


def setup_inputs(seed: int = 0) -> dict:
    streams_of = jax.random.split(jax.random.key(seed), 11)
    return {
        "tokens": bell_draw_with(streams_of[0], (SEQS, LENGTH, D), 1.0, 6.0, ((0, 16), (1, 2)), (0, 2, 16, 2.0)),
        "segments": draw_segments(jax.random.fold_in(streams_of[10], 71), 0),
        "w_query": centred(streams_of[2], (D, D), D ** -0.5, 0.1875, ((0, 16),)),
        "w_key": centred(streams_of[3], (D, D), D ** -0.5, 0.1875, ((0, 16),)),
        "w_value": centred(streams_of[4], (D, D), D ** -0.5, 0.1875, ((0, 16),)),
        "w_gate": centred(streams_of[5], (D, D), D ** -0.5, 0.1875, ((0, 16),)),
        "w_out": centred(streams_of[6], (D, D), D ** -0.5, 0.1875, ((0, 16),)),
        "w_sglu_in": centred(streams_of[7], (D, 2 * FF), D ** -0.5, 0.1875, ((0, 16),)),
        "w_sglu_down": centred(streams_of[8], (D, FF), FF ** -0.5, 0.109375, ((0, 16),)),
        "cotangent": centred(streams_of[9], (SEQS, LENGTH, D), 1.0, 6.0, ((0, 16), (1, 2))),
    }


@jax.custom_vjp
def low(v):
    return lax.optimization_barrier(v.astype(jnp.bfloat16)).astype(jnp.float32)

@jax.custom_vjp
def low_back(v):
    return v

def low_keep(v):
    return (low(v), None)

def low_pass(kept, grad):
    return (grad,)

def back_keep(v):
    return (v, None)

def back_low(kept, grad):
    return (low(grad),)
low.defvjp(low_keep, low_pass)
low_back.defvjp(back_keep, back_low)
EPSILON = 1e-06
HIGHEST = lax.Precision.HIGHEST

def matmul(left, right):
    return jnp.dot(left, right, preferred_element_type=jnp.float32, precision=HIGHEST)

def simple_norm(values):
    return values * lax.rsqrt(lax.optimization_barrier(jnp.mean(values * values, axis=-1, keepdims=True)) + EPSILON)

def swish(values):
    return values * jax.nn.sigmoid(values)

def decay_table(seg_ids, head_count, head_first):
    length = seg_ids.shape[0]
    places = jnp.arange(length, dtype=jnp.int32)
    distance = (places[:, None] - places[None, :]).astype(jnp.float32)
    allowed = (places[:, None] >= places[None, :]) & (seg_ids[:, None] == seg_ids[None, :])
    head_ids = (head_first + jnp.arange(head_count, dtype=jnp.int32)).astype(jnp.float32)
    slopes = 0.25 * jnp.exp2(-0.5 * (head_ids + 1.0))
    decayed = jnp.exp(-slopes[:, None, None] * jnp.maximum(distance, 0.0)[None])
    return jnp.where(allowed[None], decayed, 0.0)

def mixer_core(query, keys, value_heads, seg_ids):
    decay = decay_table(seg_ids, HEADS, 0)
    product = low_back(jnp.einsum('ihd,jhd->hij', query, keys, precision=HIGHEST))
    scores = low(product * decay)
    return jnp.einsum('hij,jhd->ihd', scores, value_heads, precision=HIGHEST)

def layer(inputs, w_query, w_key, w_value, w_gate, w_out, w_sglu_in, w_sglu_down, seg_ids):
    group, length, width = inputs.shape
    normed_in = low(simple_norm(inputs))
    query = low_back(low(swish(low_back(matmul(normed_in, w_query)))))
    keys = low_back(low(swish(low_back(matmul(normed_in, w_key)))))
    value_heads = low_back(low(matmul(normed_in, w_value)))
    gate_pre = low_back(matmul(normed_in, w_gate))
    head_shape = (group, length, HEADS, HEAD_DIM)
    attended = jax.vmap(mixer_core)(query.reshape(head_shape), keys.reshape(head_shape), value_heads.reshape(head_shape), seg_ids)
    attended = low_back(low(attended.reshape(group, length, width)))
    gated = low(simple_norm(attended) * gate_pre)
    hidden_in = inputs + low_back(matmul(gated, w_out))
    normed_mid = low(simple_norm(hidden_in))
    both_parts = low_back(matmul(normed_mid, w_sglu_in))
    hidden = low(both_parts[..., :FF] * both_parts[..., FF:])
    down_part = low_back(jnp.einsum('glf,df->gld', hidden, w_sglu_down, precision=HIGHEST))
    return hidden_in + down_part

def reference(tokens, segments, w_query, w_key, w_value, w_gate, w_out, w_sglu_in, w_sglu_down, cotangent):
    seq_count, length, width = tokens.shape
    group = math.gcd(seq_count, max(1, 4096 // length))
    weights = tuple((w.astype(jnp.float32) for w in (w_query, w_key, w_value, w_gate, w_out, w_sglu_in, w_sglu_down)))
    inputs = tokens.astype(jnp.float32).reshape(seq_count // group, group, length, width)
    seg_groups = segments.reshape(seq_count // group, group, length)
    cot_groups = cotangent.astype(jnp.float32).reshape(seq_count // group, group, length, width)

    def one_group(totals, item):
        group_in, group_seg, group_cot = item

        def forward(values, *params):
            return layer(values, *params, group_seg)
        result, pull = jax.vjp(forward, group_in, *weights)
        grads = pull(group_cot)
        totals = tuple((t + g for t, g in zip(totals, grads[1:])))
        return (totals, (result, grads[0]))
    zeros = tuple((jnp.zeros(w.shape, jnp.float32) for w in weights))
    totals, (results, in_grads) = lax.scan(one_group, zeros, (inputs, seg_groups, cot_groups))
    output = results.reshape(tokens.shape).astype(jnp.bfloat16)
    input_grad = in_grads.reshape(tokens.shape)
    return (output, input_grad, totals[0], totals[1], totals[2], totals[3], totals[4], totals[5], totals[6])
```

```python
import functools

import jax
import jax.numpy as jnp
from jax import lax
from jax.experimental import pallas as pl
from jax.experimental.pallas import tpu as pltpu
from jax.sharding import Mesh
from jax.sharding import PartitionSpec as P

HEAD_DIM = 128
EPSILON = 1e-06
FAR = 1e9
F32 = jnp.float32
BF16 = jnp.bfloat16


def dot(left, right):
    return jnp.dot(left, right, preferred_element_type=F32)


def dot_nt(left, right):
    return lax.dot_general(left, right, (((1,), (1,)), ((), ())), preferred_element_type=F32)


def dot_tn(left, right):
    return lax.dot_general(left, right, (((0,), (0,)), ((), ())), preferred_element_type=F32)


def row_factor(values):
    return lax.rsqrt(jnp.mean(values * values, axis=-1, keepdims=True) + EPSILON)


def norm_back(values, factor, upstream):
    normed = values * factor
    return factor * (upstream - normed * jnp.mean(upstream * normed, axis=-1, keepdims=True))


def sds(shape, kind):
    return jax.ShapeDtypeStruct(shape, kind)


def full(shape):
    return pl.BlockSpec(shape, lambda *_: (0,) * len(shape))


def cost(flops, nbytes):
    return pl.CostEstimate(flops=int(flops), bytes_accessed=int(nbytes), transcendentals=0)


def slope_of(head):
    return 0.25 * 2.0 ** (-0.5 * (head + 1))


def kv_kernel(heads, normed_ref, w_ref, dist_ref, key_ref, slope_ref, value_ref, state_ref):
    step = pl.program_id(0)
    width = normed_ref.shape[1]

    def column(j):
        return pl.ds(pl.multiple_of(j * 256, 256), 256)

    @pl.when(step == 0)
    def _():
        def body(j, carry):
            pre = dot(normed_ref[...], w_ref[:, column(j)])
            sig = jax.nn.sigmoid(pre)
            key_ref[:, column(j)] = (pre * sig).astype(BF16)
            slope_ref[:, column(j)] = (sig * (1.0 + pre * (1.0 - sig))).astype(BF16)
            return carry

        lax.fori_loop(0, width // 256, body, 0)

    @pl.when(step == 1)
    def _():
        def body(j, carry):
            value_ref[:, column(j)] = dot(normed_ref[...], w_ref[:, column(j)]).astype(BF16)
            return carry

        lax.fori_loop(0, width // 256, body, 0)
        for head in range(heads):
            cols = slice(head * HEAD_DIM, (head + 1) * HEAD_DIM)
            weight = jnp.exp(-slope_of(head) * dist_ref[...])
            scaled = (key_ref[:, cols].astype(F32) * weight).astype(BF16)
            state_ref[cols, :] = dot_tn(scaled, value_ref[:, cols]).astype(BF16)


def project_kv(normed, weights, cut_dist):
    rows, width = normed.shape
    heads = width // HEAD_DIM
    act = sds((rows, width), BF16)
    return pl.pallas_call(
        functools.partial(kv_kernel, heads),
        grid=(2,),
        in_specs=[
            full((rows, width)),
            pl.BlockSpec((width, width), lambda i: (0, i + 1)),
            full((rows, 1)),
        ],
        out_specs=[full((rows, width))] * 3 + [full((width, HEAD_DIM))],
        out_shape=[act, act, act, sds((width, HEAD_DIM), BF16)],
        cost_estimate=cost(4 * rows * width * width, 4 * width * width + 8 * rows * width),
        name="project_kv",
    )(normed, weights, cut_dist)


def qu_kernel(normed_ref, w_ref, query_ref, slope_ref, gate_ref):
    step = pl.program_id(0)
    width = normed_ref.shape[1]

    def column(j):
        return pl.ds(pl.multiple_of(j * 256, 256), 256)

    @pl.when(step == 0)
    def _():
        def body(j, carry):
            pre = dot(normed_ref[...], w_ref[:, column(j)])
            sig = jax.nn.sigmoid(pre)
            query_ref[:, column(j)] = (pre * sig).astype(BF16)
            slope_ref[:, column(j)] = (sig * (1.0 + pre * (1.0 - sig))).astype(BF16)
            return carry

        lax.fori_loop(0, width // 256, body, 0)

    @pl.when(step == 1)
    def _():
        def body(j, carry):
            gate_ref[:, column(j)] = dot(normed_ref[...], w_ref[:, column(j)]).astype(BF16)
            return carry

        lax.fori_loop(0, width // 256, body, 0)


def project_qu(normed, weights):
    rows, width = normed.shape
    act = sds((rows, width), BF16)
    return pl.pallas_call(
        qu_kernel,
        grid=(2,),
        in_specs=[full((rows, width)), pl.BlockSpec((width, width), lambda i: (0, 3 * i))],
        out_specs=[full((rows, width))] * 3,
        out_shape=[act, act, act],
        cost_estimate=cost(4 * rows * width * width, 4 * width * width + 8 * rows * width),
        name="project_qu",
    )(normed, weights)


def distance_tables(seg_col, seg_row, dist_ref):
    rows = seg_col.shape[0]
    span = lax.broadcasted_iota(jnp.int32, (rows, rows), 0) - lax.broadcasted_iota(
        jnp.int32, (rows, rows), 1
    )
    allowed = (span >= 0) & (seg_col == seg_row)
    dist_ref[...] = jnp.where(allowed, span.astype(F32), FAR)


def attend_kernel(slopes, q_ref, k_ref, v_ref, col_ref, row_ref, out_ref, dist_ref):
    head = pl.program_id(0)

    @pl.when(head == 0)
    def _():
        distance_tables(col_ref[...], row_ref[...], dist_ref)

    slope = slopes[head]
    rows = q_ref.shape[0]
    half = rows // 2
    for block in range(2):
        low, high = block * half, (block + 1) * half
        decay = jnp.exp(-slope * dist_ref[low:high, :high])
        scores = (dot_nt(q_ref[low:high, :], k_ref[:high, :]) * decay).astype(BF16)
        out_ref[low:high, :] = dot(scores, v_ref[:high, :])


def attend_local(slopes, query, key, value, seg_col, seg_row):
    rows, width = query.shape
    heads = width // HEAD_DIM
    by_head = pl.BlockSpec((rows, HEAD_DIM), lambda h, _: (0, h))
    return pl.pallas_call(
        attend_kernel,
        grid_spec=pltpu.PrefetchScalarGridSpec(
            num_scalar_prefetch=1,
            grid=(heads,),
            in_specs=[by_head] * 3 + [full((rows, 1)), full((1, rows))],
            out_specs=by_head,
            scratch_shapes=[pltpu.VMEM((rows, rows), F32)],
        ),
        out_shape=sds((rows, width), F32),
        cost_estimate=cost(3 * rows * rows * width, 10 * rows * width),
        name="attend_local",
    )(slopes, query, key, value, seg_col, seg_row)


def mix_kernel(heads, att_ref, q_ref, u_ref, x_ref, state_ref, dist_ref, w_ref, att_out, gated_out, hidden_out, normed_out):
    for head in range(heads):
        cols = slice(head * HEAD_DIM, (head + 1) * HEAD_DIM)
        weight = jnp.exp(-slope_of(head) * dist_ref[...])
        scaled = (q_ref[:, cols].astype(F32) * weight).astype(BF16)
        att_out[:, cols] = (att_ref[:, cols] + dot(scaled, state_ref[cols, :])).astype(BF16)
    attended = att_out[...].astype(F32)
    gated = (attended * row_factor(attended) * u_ref[...].astype(F32)).astype(BF16)
    gated_out[...] = gated
    hidden = x_ref[...].astype(F32) + dot(gated, w_ref[...])
    hidden_out[...] = hidden
    normed_out[...] = (hidden * row_factor(hidden)).astype(BF16)


def mix_out(att, query, gate, tokens, state, cut_dist, weights):
    rows, width = query.shape
    heads = width // HEAD_DIM
    part = rows // 2
    by_rows = pl.BlockSpec((part, width), lambda i: (i, 0))
    return pl.pallas_call(
        functools.partial(mix_kernel, heads),
        grid=(2,),
        in_specs=[by_rows] * 4
        + [
            full((width, HEAD_DIM)),
            pl.BlockSpec((part, 1), lambda i: (i, 0)),
            pl.BlockSpec((width, width), lambda i: (0, 4)),
        ],
        out_specs=[by_rows] * 4,
        out_shape=[sds((rows, width), kind) for kind in (BF16, BF16, F32, BF16)],
        cost_estimate=cost(2 * rows * width * (width + HEAD_DIM), 2 * width * width + 20 * rows * width),
        name="mix_out",
    )(att, query, gate, tokens, state, cut_dist, weights)


def ff_kernel(first, normed_ref, grad_ref, w_ref, *refs):
    acts_ref, out_ref, back_ref, wg, wu, wd, gate, up, sem = refs[-9:]
    part = wg.shape[1]
    width = normed_ref.shape[1]
    copies = []
    for i, buf in enumerate((wg, wu, wd)):
        copies.append(
            pltpu.make_async_copy(w_ref.at[:, first + i * part : first + (i + 1) * part], buf, sem.at[i])
        )
        copies[-1].start()
    whole = part // 256

    def sweep(body):
        def step(j, carry):
            body(pl.ds(pl.multiple_of(j * 256, 256), 256), None)
            return carry

        lax.fori_loop(0, whole, step, 0)
        if part % 256:
            body(slice(whole * 256, part), None)

    copies[0].wait()

    def gate_part(cols, _):
        gate[:, cols] = dot(normed_ref[...], wg[:, cols])

    sweep(gate_part)
    copies[1].wait()

    def up_part(cols, _):
        up[:, cols] = dot(normed_ref[...], wu[:, cols])

    sweep(up_part)
    copies[2].wait()

    def shifted(cols, i):
        if isinstance(cols, slice):
            return slice(cols.start + i * part, cols.stop + i * part)
        return pl.ds(pl.multiple_of(cols.start + i * part, 128), cols.size)

    def down_part(cols, _):
        d_hidden = dot(grad_ref[...], wd[:, cols])
        acts_ref[:, shifted(cols, 0)] = (d_hidden * up[:, cols]).astype(BF16)
        acts_ref[:, shifted(cols, 1)] = (d_hidden * gate[:, cols]).astype(BF16)
        acts_ref[:, shifted(cols, 2)] = (gate[:, cols] * up[:, cols]).astype(BF16)

    sweep(down_part)

    def rows_step(j, carry):
        block = pl.ds(pl.multiple_of(j * 256, 256), 256)
        back = dot_nt(acts_ref[:, :part], wg[block, :]) + dot_nt(acts_ref[:, part : 2 * part], wu[block, :])
        back_ref[:, block] = back.astype(back_ref.dtype)
        return carry

    lax.fori_loop(0, width // 256, rows_step, 0)

    def out_step(j, carry):
        block = pl.ds(pl.multiple_of(j * 256, 256), 256)
        out_ref[:, block] = dot_nt(acts_ref[:, 2 * part :], wd[block, :]).astype(out_ref.dtype)
        return carry

    lax.fori_loop(0, width // 256, out_step, 0)


def feed_forward(first, part, kind, place, places, normed, grad, weights, acts=None):
    rows, width = normed.shape
    operands = [normed, grad, weights]
    in_specs = [full((rows, width))] * 2 + [pl.BlockSpec(memory_space=pl.ANY)]
    aliases = {}
    if acts is not None:
        operands.append(acts)
        in_specs.append(pl.BlockSpec(memory_space=pl.ANY))
        aliases = {3: 0}
    return pl.pallas_call(
        functools.partial(ff_kernel, first),
        grid=(1,),
        in_specs=in_specs,
        out_specs=[
            pl.BlockSpec((rows, 3 * part), lambda i: (place, 0)),
            full((rows, width)),
            full((rows, width)),
        ],
        out_shape=[
            sds((places * rows, 3 * part), BF16),
            sds((rows, width), kind),
            sds((rows, width), kind),
        ],
        scratch_shapes=[pltpu.VMEM((width, part), BF16)] * 3
        + [pltpu.VMEM((rows, part), F32)] * 2
        + [pltpu.SemaphoreType.DMA((3,))],
        input_output_aliases=aliases,
        cost_estimate=cost(12 * rows * width * part, 6 * width * part + 6 * rows * part + 12 * rows * width),
        name="feed_forward",
    )(*operands)


def unmix_kernel(heads, hidden_ref, own_ref, other_ref, grad_ref, u_ref, att_ref, q_ref, dist_ref, w_ref, d_hidden_out, d_mix_out, d_u_out, d_att_out, state_out, total):
    step = pl.program_id(0)
    hidden = hidden_ref[...]
    upstream = own_ref[...] + other_ref[...].astype(F32)
    d_hidden = grad_ref[...].astype(F32) + norm_back(hidden, row_factor(hidden), upstream)
    d_hidden_out[...] = d_hidden
    d_mix = d_hidden.astype(BF16)
    d_mix_out[...] = d_mix
    d_gated = dot_nt(d_mix, w_ref[...])
    attended = att_ref[...].astype(F32)
    factor = row_factor(attended)
    d_u_out[...] = (d_gated * (attended * factor)).astype(BF16)
    d_att_out[...] = norm_back(attended, factor, d_gated * u_ref[...].astype(F32)).astype(BF16)

    @pl.when(step == 0)
    def _():
        total[...] = jnp.zeros_like(total)

    for head in range(heads):
        cols = slice(head * HEAD_DIM, (head + 1) * HEAD_DIM)
        weight = jnp.exp(-slope_of(head) * dist_ref[...])
        scaled = (q_ref[:, cols].astype(F32) * weight).astype(BF16)
        total[cols, :] += dot_tn(scaled, d_att_out[:, cols])

    @pl.when(step == pl.num_programs(0) - 1)
    def _():
        state_out[...] = total[...].astype(BF16)


def unmix(hidden, back_own, back_other, grad, gate, attended, query, cut_dist, weights):
    rows, width = query.shape
    heads = width // HEAD_DIM
    part = rows // 2
    by_rows = pl.BlockSpec((part, width), lambda i: (i, 0))
    return pl.pallas_call(
        functools.partial(unmix_kernel, heads),
        grid=(2,),
        in_specs=[by_rows] * 7
        + [
            pl.BlockSpec((part, 1), lambda i: (i, 0)),
            pl.BlockSpec((width, width), lambda i: (0, 4)),
        ],
        out_specs=[by_rows] * 4 + [full((width, HEAD_DIM))],
        out_shape=[sds((rows, width), kind) for kind in (F32, BF16, BF16, BF16)]
        + [sds((width, HEAD_DIM), BF16)],
        scratch_shapes=[pltpu.VMEM((width, HEAD_DIM), F32)],
        cost_estimate=cost(2 * rows * width * (width + HEAD_DIM), 2 * width * width + 26 * rows * width),
        name="unmix",
    )(hidden, back_own, back_other, grad, gate, attended, query, cut_dist, weights)


def attend_back_kernel(slopes, q_ref, k_ref, v_ref, d_ref, sq_ref, state_ref, cut_ref, col_ref, row_ref, dq_ref, dk_ref, dv_ref, dist_ref, turned_ref):
    head = pl.program_id(0)
    rows = q_ref.shape[0]
    half = rows // 2

    @pl.when(head == 0)
    def _():
        distance_tables(col_ref[...], row_ref[...], dist_ref)
        turned_ref[...] = dist_ref[...].T

    slope = slopes[head]
    cut = jnp.exp(-slope * cut_ref[...])
    for block in range(2):
        low, high = block * half, (block + 1) * half
        decay = jnp.exp(-slope * dist_ref[low:high, :high])
        d_prod = (dot_nt(d_ref[low:high, :], v_ref[:high, :]) * decay).astype(BF16)
        d_query = dot(d_prod, k_ref[:high, :]) + cut[low:high] * dot_nt(d_ref[low:high, :], state_ref[...])
        dq_ref[low:high, :] = (d_query * sq_ref[low:high, :].astype(F32)).astype(BF16)
    for block in range(2):
        low, high = block * half, (block + 1) * half
        decay = jnp.exp(-slope * turned_ref[low:high, low:])
        scores = (dot_nt(k_ref[low:high, :], q_ref[low:, :]) * decay).astype(BF16)
        dv_ref[low:high, :] = dot(scores, d_ref[low:, :])
        d_prod = (dot_nt(v_ref[low:high, :], d_ref[low:, :]) * decay).astype(BF16)
        dk_ref[low:high, :] = dot(d_prod, q_ref[low:, :])


def attend_back(slopes, query, key, value, d_att, q_slope, state, cut_dist, seg_col, seg_row):
    rows, width = query.shape
    heads = width // HEAD_DIM
    by_head = pl.BlockSpec((rows, HEAD_DIM), lambda h, _: (0, h))
    return pl.pallas_call(
        attend_back_kernel,
        grid_spec=pltpu.PrefetchScalarGridSpec(
            num_scalar_prefetch=1,
            grid=(heads,),
            in_specs=[by_head] * 5
            + [
                pl.BlockSpec((HEAD_DIM, HEAD_DIM), lambda h, _: (h, 0)),
                full((rows, 1)),
                full((rows, 1)),
                full((1, rows)),
            ],
            out_specs=[by_head] * 3,
            scratch_shapes=[pltpu.VMEM((rows, rows), F32)] * 2,
        ),
        out_shape=[sds((rows, width), kind) for kind in (BF16, F32, F32)],
        cost_estimate=cost(9 * rows * rows * width, 20 * rows * width),
        name="attend_back",
    )(slopes, query, key, value, d_att, q_slope, state, cut_dist, seg_col, seg_row)


def join_kernel(slopes, dq_ref, dk_ref, dv_ref, k_ref, v_ref, sk_ref, state_ref, cut_ref, out_ref):
    slope = slopes[pl.program_id(0)]
    cut = jnp.exp(-slope * cut_ref[...])
    out_ref[:, :HEAD_DIM] = dq_ref[...]
    d_key = dk_ref[...] + cut * dot_nt(v_ref[...], state_ref[...])
    out_ref[:, HEAD_DIM : 2 * HEAD_DIM] = (d_key * sk_ref[...].astype(F32)).astype(BF16)
    d_value = dv_ref[...] + cut * dot(k_ref[...], state_ref[...])
    out_ref[:, 2 * HEAD_DIM :] = d_value.astype(BF16)


def join_back(slopes, dq, dk, dv, key, value, k_slope, state, cut_dist):
    rows, width = key.shape
    heads = width // HEAD_DIM
    by_head = pl.BlockSpec((rows, HEAD_DIM), lambda h, _: (0, h))
    return pl.pallas_call(
        join_kernel,
        grid_spec=pltpu.PrefetchScalarGridSpec(
            num_scalar_prefetch=1,
            grid=(heads,),
            in_specs=[by_head] * 6
            + [pl.BlockSpec((HEAD_DIM, HEAD_DIM), lambda h, _: (h, 0)), full((rows, 1))],
            out_specs=pl.BlockSpec((rows, 3 * HEAD_DIM), lambda h, _: (0, h)),
        ),
        out_shape=sds((rows, 3 * width), BF16),
        cost_estimate=cost(4 * rows * HEAD_DIM * width, 22 * rows * width),
        name="join_back",
    )(slopes, dq, dk, dv, key, value, k_slope, state, cut_dist)


def input_kernel(heads, dqkv_ref, du_ref, w_ref, dh_ref, x_ref, out_ref, packed, total):
    step = pl.program_id(0)
    width = x_ref.shape[1]
    for which in range(3):

        @pl.when(step == which)
        def _(which=which):
            for head in range(heads):
                source = (3 * head + which) * HEAD_DIM
                packed[:, head * HEAD_DIM : (head + 1) * HEAD_DIM] = dqkv_ref[:, source : source + HEAD_DIM]

    @pl.when(step == 3)
    def _():
        packed[...] = du_ref[...]

    @pl.when(step == 0)
    def _():
        total[...] = jnp.zeros_like(total)

    def body(j, carry):
        block = pl.ds(pl.multiple_of(j * 256, 256), 256)
        total[:, block] += dot_nt(packed[...], w_ref[block, :])
        return carry

    lax.fori_loop(0, width // 256, body, 0)

    @pl.when(step == 3)
    def _():
        inputs = x_ref[...].astype(F32)
        out_ref[...] = dh_ref[...] + norm_back(inputs, row_factor(inputs), total[...])


def input_grad_of(dqkv, du, weights, d_hidden, tokens):
    rows, width = tokens.shape
    heads = width // HEAD_DIM
    return pl.pallas_call(
        functools.partial(input_kernel, heads),
        grid=(4,),
        in_specs=[
            full((rows, 3 * width)),
            full((rows, width)),
            pl.BlockSpec((width, width), lambda i: (0, i)),
            full((rows, width)),
            full((rows, width)),
        ],
        out_specs=full((rows, width)),
        out_shape=sds((rows, width), F32),
        scratch_shapes=[pltpu.VMEM((rows, width), BF16), pltpu.VMEM((rows, width), F32)],
        cost_estimate=cost(8 * rows * width * width, 8 * width * width + 18 * rows * width),
        name="input_grad",
    )(dqkv, du, weights, d_hidden, tokens)


def swap(values, axis, bit=1):
    size = lax.axis_size(axis)
    return lax.ppermute(values, axis, [(i, i ^ bit) for i in range(size)])


def pick(values, place, axis):
    return lax.dynamic_index_in_dim(values, place, axis, keepdims=False)


def scatter_rows(parts):
    group = lax.axis_size("zy")
    bits = group.bit_length() - 1
    index, core = lax.axis_index("zy"), lax.axis_index("core")
    rows = parts[0].shape[0] // (2 * group)
    terms = [[part.reshape((2,) * (bits + 1) + (rows, part.shape[1]))] for part in parts]
    left = list(range(bits - 1, -1, -1)) + ["core"]
    for bit in ["core"] + [0] * (bits > 0) + list(range(bits - 1, 0, -1)):
        axis = left.index(bit)
        mine = core if bit == "core" else (index >> bit) & 1
        sent = [
            functools.reduce(jnp.add, [pick(t, 1 - mine, axis).astype(F32) for t in term])
            for term in terms
        ]
        sent = (sent[0] if len(sent) == 1 else jnp.concatenate(sent, -1)).astype(BF16)
        got = swap(sent, "core") if bit == "core" else swap(sent, "zy", 1 << bit)
        kept = [[pick(t, mine, axis) for t in term] for term in terms]
        at = 0
        for term in kept:
            wide = term[0].shape[-1]
            term.append(got[..., at : at + wide])
            at += wide
        terms = kept
        left.remove(bit)
    sums = [functools.reduce(jnp.add, [t.astype(F32) for t in term]) for term in terms]
    return (sums[0] if len(sums) == 1 else jnp.concatenate(sums, -1)).astype(BF16)


def on_device(tokens, segments, w_query, w_key, w_value, w_gate, w_out, w_sglu_in, w_sglu_down, cotangent):
    rows, width = tokens.shape[1:]
    heads = width // HEAD_DIM
    planes = lax.axis_size("seq")
    plane = lax.axis_index("seq")
    ff = w_sglu_down.shape[1]
    part = ff // planes
    inputs, grad_tok = tokens[0], cotangent[0]

    slopes = jnp.array([slope_of(head) for head in range(heads)], F32)
    segs = lax.dynamic_slice_in_dim(segments[0], plane * rows, rows)
    edge = segments[0, rows - 1]
    places = jnp.arange(rows, dtype=jnp.int32)
    same = segs == edge
    from_cut = jnp.where(same, (places + 1).astype(F32), FAR)[:, None]
    to_cut = jnp.where(same, (rows - 1 - places).astype(F32), FAR)[:, None]
    seg_col, seg_row = segs[:, None], segs[None, :]

    def ff_cols(values, first):
        return lax.dynamic_slice_in_dim(values, first + plane * part, part, axis=1)

    shard = jnp.concatenate(
        [w_query, w_key, w_value, w_gate, w_out]
        + [ff_cols(w_sglu_in, 0), ff_cols(w_sglu_in, ff), ff_cols(w_sglu_down, 0)],
        axis=1,
    )
    weights = lax.all_gather(shard, ("zy", "core"), axis=0, tiled=True)
    first = 5 * width

    grad_other = swap(grad_tok, "seq")
    x32 = inputs.astype(F32)
    normed_in = (x32 * row_factor(x32)).astype(BF16)

    key, k_slope, value, state = project_kv(normed_in, weights, to_cut)
    state = lax.ppermute(state, "seq", [(i, i + 1) for i in range(planes - 1)])
    query, q_slope, gate = project_qu(normed_in, weights)
    att = attend_local(slopes, query, key, value, seg_col, seg_row)
    attended, gated, hidden, normed = mix_out(att, query, gate, inputs, state, from_cut, weights)

    normed_other = swap(normed, "seq")
    acts, out_own, back_own = feed_forward(first, part, F32, 0, planes, normed, grad_tok, weights)
    acts, out_sent, back_sent = feed_forward(
        first, part, BF16, 1, planes, normed_other, grad_other, weights, acts
    )
    back_other = swap(back_sent, "seq")
    out_other = swap(out_sent, "seq")
    output = (hidden + out_own + out_other.astype(F32)).astype(BF16)

    normed_both = jnp.concatenate([normed, normed_other], 0)
    grad_both = jnp.concatenate([grad_tok, grad_other], 0)
    g_down = dot_tn(grad_both, acts[:, 2 * part :]).astype(BF16)
    g_in = dot_tn(normed_both, acts[:, : 2 * part]).astype(BF16)
    down_sum = scatter_rows([g_down])
    in_sum = scatter_rows([g_in])

    d_hidden, d_mix, d_u, d_att, back_state = unmix(
        hidden, back_own, back_other, grad_tok, gate, attended, query, from_cut, weights
    )
    back_state = lax.ppermute(back_state, "seq", [(i + 1, i) for i in range(planes - 1)])
    g_out = dot_tn(gated, d_mix).astype(BF16)
    g_gate = dot_tn(normed_in, d_u).astype(BF16)
    mix_sum = scatter_rows([g_out, g_gate])
    dq, dk, dv = attend_back(
        slopes, query, key, value, d_att, q_slope, state, from_cut, seg_col, seg_row
    )
    dqkv = join_back(slopes, dq, dk, dv, key, value, k_slope, back_state, to_cut)
    g_qkv = dot_tn(normed_in, dqkv).astype(BF16)
    qkv_sum = scatter_rows([g_qkv])
    input_grad = input_grad_of(dqkv, d_u, weights, d_hidden, inputs)

    def both_planes(values):
        other = swap(values, "seq")
        low = jnp.where(plane == 0, values, other).astype(F32)
        high = jnp.where(plane == 0, other, values).astype(F32)
        return low, high

    low, high = both_planes(in_sum)
    grad_in = jnp.concatenate([low[:, :part], high[:, :part], low[:, part:], high[:, part:]], 1)
    grad_down = jnp.concatenate(both_planes(down_sum), 1)
    mix_total = mix_sum.astype(F32) + swap(mix_sum, "seq").astype(F32)
    qkv_total = qkv_sum.astype(F32) + swap(qkv_sum, "seq").astype(F32)
    qkv_total = qkv_total.reshape(-1, heads, 3, HEAD_DIM)
    grads = [qkv_total[:, :, i].reshape(-1, width) for i in range(3)]
    return (
        output[None],
        input_grad[None],
        *grads,
        mix_total[:, width:],
        mix_total[:, :width],
        grad_in,
        grad_down,
    )


def solution(mesh):
    planes, group = mesh.devices.shape
    devices = mesh.devices.reshape(planes, group // 2, 2)
    split = Mesh(devices, ("seq", "zy", "core"))
    rows = ("zy", "core")
    tok = P(rows, "seq", None)
    mat = P(rows, None)
    return jax.shard_map(
        on_device,
        mesh=split,
        in_specs=(tok,) + (mat,) * 8 + (tok,),
        out_specs=(tok, tok) + (mat,) * 7,
        check_vma=False,
    )
```

```python
import functools

import jax
import jax.numpy as jnp
from jax import lax
from jax.experimental import pallas as pl
from jax.experimental.pallas import tpu as pltpu
from jax.sharding import Mesh
from jax.sharding import PartitionSpec as P

HEAD_DIM = 128
EPSILON = 1e-06
FAR = 1e9
F32 = jnp.float32
BF16 = jnp.bfloat16


def dot(left, right):
    return jnp.dot(left, right, preferred_element_type=F32)


def dot_nt(left, right):
    return lax.dot_general(left, right, (((1,), (1,)), ((), ())), preferred_element_type=F32)


def dot_tn(left, right):
    return lax.dot_general(left, right, (((0,), (0,)), ((), ())), preferred_element_type=F32)


def row_factor(values):
    return lax.rsqrt(jnp.mean(values * values, axis=-1, keepdims=True) + EPSILON)


def norm_back(values, factor, upstream):
    normed = values * factor
    return factor * (upstream - normed * jnp.mean(upstream * normed, axis=-1, keepdims=True))


def sds(shape, kind):
    return jax.ShapeDtypeStruct(shape, kind)


def full(shape):
    return pl.BlockSpec(shape, lambda *_: (0,) * len(shape))


def vmem():
    return pl.BlockSpec(memory_space=pltpu.VMEM)


def hbm():
    return pl.BlockSpec(memory_space=pltpu.HBM)


def fetch(w_ref, firsts, bufs, sem):
    copies = []
    for i, (first, buf) in enumerate(zip(firsts, bufs, strict=True)):
        copies.append(pltpu.make_async_copy(w_ref.at[:, first : first + buf.shape[1]], buf, sem.at[i]))
        copies[-1].start()
    return copies


def cost(micros):
    return pl.CostEstimate(flops=int(micros * 1.1e9), bytes_accessed=0, transcendentals=0)


def run(kernel, operands, in_specs, deps=(), scalars=0, grid=(1,), scratch=(), **options):
    given = len(operands)

    def body(*refs):
        kernel(*refs[:given], *refs[given + len(deps) :])

    return pl.pallas_call(
        body,
        grid_spec=pltpu.PrefetchScalarGridSpec(
            num_scalar_prefetch=scalars,
            grid=grid,
            in_specs=list(in_specs) + [pl.BlockSpec(memory_space=pl.ANY)] * len(deps),
            out_specs=options.pop("out_specs"),
            scratch_shapes=list(scratch),
        ),
        **options,
    )(*operands, *deps)


def room(mebibytes):
    return pltpu.CompilerParams(vmem_limit_bytes=mebibytes << 20)


def slope_of(head):
    return 0.25 * 2.0 ** (-0.5 * (head + 1))


def shard_kernel(plane_ref, *refs):
    out_ref = refs[-1]
    at = 0
    for ref in refs[:-1]:
        out_ref[:, at : at + ref.shape[1]] = ref[...]
        at += ref.shape[1]


def gather_shard(plane, part, mixer, w_in, w_down):
    rows = w_in.shape[0]
    planes = w_down.shape[1] // part
    wide = sum(w.shape[1] for w in mixer) + 3 * part
    return run(
        shard_kernel,
        (jnp.reshape(plane, (1,)), *mixer, w_in, w_in, w_down),
        scalars=1,
        in_specs=[pl.BlockSpec(w.shape, lambda i, p: (0, 0)) for w in mixer]
        + [
            pl.BlockSpec((rows, part), lambda i, p: (0, p[0])),
            pl.BlockSpec((rows, part), lambda i, p: (0, p[0] + planes)),
            pl.BlockSpec((rows, part), lambda i, p: (0, p[0])),
        ],
        out_specs=pl.BlockSpec((rows, wide), lambda i, p: (0, 0)),
        out_shape=sds((rows, wide), BF16),
        compiler_params=room(8),
        name="gather_shard",
    )


def swish_parts(pre):
    sig = jax.nn.sigmoid(pre)
    return (pre * sig).astype(BF16), (sig * (1.0 + pre * (1.0 - sig))).astype(BF16)


def kv_kernel(heads, normed_ref, w_ref, dist_ref, key_ref, slope_ref, value_ref, state_ref, wk, wv, sem):
    width = normed_ref.shape[1]
    copies = fetch(w_ref, (width, 2 * width), (wk, wv), sem)
    copies[0].wait()
    for low in range(0, width, 256):
        cols = slice(low, low + 256)
        key_ref[:, cols], slope_ref[:, cols] = swish_parts(dot(normed_ref[...], wk[:, cols]))
    copies[1].wait()
    for low in range(0, width, 256):
        cols = slice(low, low + 256)
        value_ref[:, cols] = dot(normed_ref[...], wv[:, cols]).astype(BF16)
    for head in range(heads):
        cols = slice(head * HEAD_DIM, (head + 1) * HEAD_DIM)
        weight = jnp.exp(-slope_of(head) * dist_ref[...])
        scaled = (key_ref[:, cols].astype(F32) * weight).astype(BF16)
        state_ref[cols, :] = dot_tn(scaled, value_ref[:, cols]).astype(BF16)


def project_kv(normed, weights, cut_dist, deps=()):
    rows, width = normed.shape
    heads = width // HEAD_DIM
    act = sds((rows, width), BF16)
    return run(
        functools.partial(kv_kernel, heads),
        (normed, weights, cut_dist),
        deps=deps,
        in_specs=[vmem(), hbm(), vmem()],
        out_specs=[vmem()] * 4,
        out_shape=[act, act, act, sds((width, HEAD_DIM), BF16)],
        scratch=[pltpu.VMEM((width, width), BF16)] * 2 + [pltpu.SemaphoreType.DMA((2,))],
        cost_estimate=cost(0.2),
        compiler_params=room(8),
        name="project_kv",
    )


def qu_kernel(normed_ref, w_ref, query_ref, slope_ref, gate_ref, wq, wu, sem):
    width = normed_ref.shape[1]
    copies = fetch(w_ref, (0, 3 * width), (wq, wu), sem)
    copies[0].wait()
    for low in range(0, width, 256):
        cols = slice(low, low + 256)
        query_ref[:, cols], slope_ref[:, cols] = swish_parts(dot(normed_ref[...], wq[:, cols]))
    copies[1].wait()
    for low in range(0, width, 256):
        cols = slice(low, low + 256)
        gate_ref[:, cols] = dot(normed_ref[...], wu[:, cols]).astype(BF16)


def project_qu(normed, weights):
    rows, width = normed.shape
    act = sds((rows, width), BF16)
    return run(
        qu_kernel,
        (normed, weights),
        in_specs=[vmem(), hbm()],
        out_specs=[vmem()] * 3,
        out_shape=[act, act, act],
        scratch=[pltpu.VMEM((width, width), BF16)] * 2 + [pltpu.SemaphoreType.DMA((2,))],
        cost_estimate=cost(0.2),
        compiler_params=room(8),
        name="project_qu",
    )


def distance_tables(seg_col, seg_row, dist_ref):
    rows = seg_col.shape[0]
    span = lax.broadcasted_iota(jnp.int32, (rows, rows), 0) - lax.broadcasted_iota(
        jnp.int32, (rows, rows), 1
    )
    allowed = (span >= 0) & (seg_col == seg_row)
    dist_ref[...] = jnp.where(allowed, span.astype(F32), FAR)


def attend_kernel(heads, q_ref, k_ref, v_ref, col_ref, row_ref, out_ref, dist_ref):
    distance_tables(col_ref[...], row_ref[...], dist_ref)
    rows = q_ref.shape[0]
    half = rows // 2
    for head in range(heads):
        cols = slice(head * HEAD_DIM, (head + 1) * HEAD_DIM)
        for block in range(2):
            low, high = block * half, (block + 1) * half
            decay = jnp.exp(-slope_of(head) * dist_ref[low:high, :high])
            scores = (dot_nt(q_ref[low:high, cols], k_ref[:high, cols]) * decay).astype(BF16)
            out_ref[low:high, cols] = dot(scores, v_ref[:high, cols])


def attend_local(query, key, value, seg_col, seg_row):
    rows, width = query.shape
    return run(
        functools.partial(attend_kernel, width // HEAD_DIM),
        (query, key, value, seg_col, seg_row),
        in_specs=[vmem()] * 5,
        out_specs=vmem(),
        out_shape=sds((rows, width), F32),
        scratch=[pltpu.VMEM((rows, rows), F32)],
        cost_estimate=cost(0.2),
        compiler_params=room(5),
        name="attend_local",
    )


def mix_kernel(heads, att_ref, q_ref, u_ref, x_ref, state_ref, dist_ref, w_ref, att_out, gated_out, hidden_out, normed_out, top_out, bottom_out, wo, sem):
    width = q_ref.shape[1]
    rows = q_ref.shape[0]
    copies = fetch(w_ref, (4 * width,), (wo,), sem)
    for head in range(heads):
        cols = slice(head * HEAD_DIM, (head + 1) * HEAD_DIM)
        weight = jnp.exp(-slope_of(head) * dist_ref[...])
        scaled = (q_ref[:, cols].astype(F32) * weight).astype(BF16)
        att_out[:, cols] = (att_ref[:, cols] + dot(scaled, state_ref[cols, :])).astype(BF16)
    copies[0].wait()
    for low in range(0, rows, 256):
        part = slice(low, low + 256)
        attended = att_out[part, :].astype(F32)
        gated = (attended * row_factor(attended) * u_ref[part, :].astype(F32)).astype(BF16)
        gated_out[part, :] = gated
        hidden = x_ref[part, :].astype(F32) + dot(gated, wo[...])
        hidden_out[part, :] = hidden
        normed = (hidden * row_factor(hidden)).astype(BF16)
        normed_out[part, :] = normed
        half_out, at = (top_out, low) if 2 * low < rows else (bottom_out, low - rows // 2)
        half_out[at : at + 256, :] = normed


def mix_out(att, query, gate, tokens, state, cut_dist, weights):
    rows, width = query.shape
    return run(
        functools.partial(mix_kernel, width // HEAD_DIM),
        (att, query, gate, tokens, state, cut_dist, weights),
        in_specs=[vmem()] * 6 + [hbm()],
        out_specs=[vmem()] * 6,
        out_shape=[sds((rows, width), kind) for kind in (BF16, BF16, F32, BF16)]
        + [sds((rows // 2, width), BF16)] * 2,
        scratch=[pltpu.VMEM((width, width), BF16), pltpu.SemaphoreType.DMA((1,))],
        cost_estimate=cost(0.2),
        compiler_params=room(7),
        name="mix_out",
    )


def ff_kernel(first, place, grad_first, normed_ref, grad_ref, w_ref, *refs):
    acts_ref, back_ref, wg, wu, wd, sem = refs[-6:]
    part = wg.shape[1]
    rows, width = normed_ref.shape
    here = slice(place, place + rows)
    blocks = [slice(low, min(low + 256, part)) for low in range(0, part, 256)]
    copies = []
    for block, cols in enumerate(blocks):
        for which, buf in enumerate((wg, wu, wd)):
            source = slice(first + which * part + cols.start, first + which * part + cols.stop)
            copies.append(
                pltpu.make_async_copy(w_ref.at[:, source], buf.at[:, cols], sem.at[3 * block + which])
            )
            copies[-1].start()
    for block, cols in enumerate(blocks):
        for copy in copies[3 * block : 3 * block + 3]:
            copy.wait()
        gate = dot(normed_ref[...], wg[:, cols])
        up = dot(normed_ref[...], wu[:, cols])
        d_hidden = dot(grad_ref[grad_first : grad_first + rows, :], wd[:, cols])
        for which, value in enumerate((d_hidden * up, d_hidden * gate, gate * up)):
            acts_ref[here, which * part + cols.start : which * part + cols.stop] = value.astype(BF16)
    for low in range(0, width, 256):
        block = slice(low, low + 256)
        back = dot_nt(acts_ref[here, :part], wg[block, :]) + dot_nt(acts_ref[here, part : 2 * part], wu[block, :])
        back_ref[:, block] = back.astype(back_ref.dtype)


def feed_forward(first, part, kind, place, total, normed, grad_first, grad, weights, acts=None, deps=()):
    rows, width = normed.shape
    operands = [normed, grad, weights]
    in_specs = [vmem(), vmem(), hbm()]
    options = {}
    if acts is not None:
        operands.append(acts)
        in_specs.append(vmem())
        options["input_output_aliases"] = {3: 0}
    return run(
        functools.partial(ff_kernel, first, place, grad_first),
        operands,
        deps=deps,
        in_specs=in_specs,
        out_specs=[vmem()] * 2,
        out_shape=[
            sds((total, 3 * part), BF16),
            sds((rows, width), kind),
        ],
        scratch=[pltpu.VMEM((width, part), BF16)] * 3
        + [pltpu.SemaphoreType.DMA((3 * -(-part // 256),))],
        cost_estimate=cost(0.2),
        compiler_params=room(18),
        name="feed_forward",
        **options,
    )


def down_kernel(first, acts_ref, w_ref, own_ref, other_ref, wd, sem):
    part = wd.shape[1]
    rows, width = own_ref.shape
    copies = fetch(w_ref, (first + 2 * part,), (wd,), sem)
    copies[0].wait()
    for low in range(0, width, 256):
        block = slice(low, low + 256)
        own_ref[:, block] = dot_nt(acts_ref[:rows, 2 * part :], wd[block, :])
        other_ref[:, block] = dot_nt(acts_ref[rows:, 2 * part :], wd[block, :]).astype(BF16)


def down_project(first, part, acts, weights, deps=()):
    width = weights.shape[0]
    rows = acts.shape[0] // 2
    return run(
        functools.partial(down_kernel, first),
        (acts, weights),
        deps=deps,
        in_specs=[vmem(), hbm()],
        out_specs=[vmem()] * 2,
        out_shape=[sds((rows, width), F32), sds((rows, width), BF16)],
        scratch=[pltpu.VMEM((width, part), BF16), pltpu.SemaphoreType.DMA((1,))],
        cost_estimate=cost(0.2),
        compiler_params=room(7),
        name="down_project",
    )


def add_kernel(hidden_ref, own_ref, other_ref, out_ref):
    out_ref[...] = (hidden_ref[...] + own_ref[...] + other_ref[...].astype(F32)).astype(BF16)


def add_output(hidden, own, other, deps):
    return run(
        add_kernel,
        (hidden, own, other),
        deps=deps,
        in_specs=[vmem()] * 3,
        out_specs=vmem(),
        out_shape=sds(hidden.shape, BF16),
        cost_estimate=cost(1),
        compiler_params=room(4),
        name="add_output",
    )


def fold_kernel(kept_ref, late_ref, soon_ref, out_ref):
    half = late_ref.shape[0]
    out_ref[:half, :] = (kept_ref[:half, :].astype(F32) + late_ref[...].astype(F32)).astype(BF16)
    out_ref[half:, :] = (kept_ref[half:, :].astype(F32) + soon_ref[...].astype(F32)).astype(BF16)


def fold(kept, late, soon):
    return run(
        fold_kernel,
        (kept, late, soon),
        in_specs=[vmem()] * 3,
        out_specs=vmem(),
        out_shape=sds(kept.shape, BF16),
        cost_estimate=cost(0.2),
        compiler_params=room(4),
        name="fold",
    )


def unmix_kernel(heads, hidden_ref, own_ref, top_ref, bottom_ref, grad_ref, u_ref, att_ref, q_ref, dist_ref, w_ref, d_hidden_out, d_mixer_out, d_att_out, state_out, wo, sem):
    rows, width = q_ref.shape
    copies = fetch(w_ref, (4 * width,), (wo,), sem)
    for low in range(0, rows, 256):
        part = slice(low, low + 256)
        hidden = hidden_ref[part, :]
        half_ref, at = (top_ref, low) if 2 * low < rows else (bottom_ref, low - rows // 2)
        upstream = own_ref[part, :] + half_ref[at : at + 256, :].astype(F32)
        d_hidden = grad_ref[part, :].astype(F32) + norm_back(hidden, row_factor(hidden), upstream)
        d_hidden_out[part, :] = d_hidden
        d_mixer_out[part, :width] = d_hidden.astype(BF16)
    copies[0].wait()
    for low in range(0, rows, 256):
        part = slice(low, low + 256)
        d_gated = dot_nt(d_mixer_out[part, :width], wo[...])
        attended = att_ref[part, :].astype(F32)
        factor = row_factor(attended)
        d_mixer_out[part, width:] = (d_gated * (attended * factor)).astype(BF16)
        d_att_out[part, :] = norm_back(attended, factor, d_gated * u_ref[part, :].astype(F32)).astype(BF16)
    for head in range(heads):
        cols = slice(head * HEAD_DIM, (head + 1) * HEAD_DIM)
        weight = jnp.exp(-slope_of(head) * dist_ref[...])
        scaled = (q_ref[:, cols].astype(F32) * weight).astype(BF16)
        state_out[cols, :] = dot_tn(scaled, d_att_out[:, cols]).astype(BF16)


def unmix(hidden, back_own, back_top, back_bottom, grad, gate, attended, query, cut_dist, weights, deps=()):
    rows, width = query.shape
    return run(
        functools.partial(unmix_kernel, width // HEAD_DIM),
        (hidden, back_own, back_top, back_bottom, grad, gate, attended, query, cut_dist, weights),
        deps=deps,
        in_specs=[vmem()] * 9 + [hbm()],
        out_specs=[vmem()] * 4,
        out_shape=[
            sds((rows, width), F32),
            sds((rows, 2 * width), BF16),
            sds((rows, width), BF16),
            sds((width, HEAD_DIM), BF16),
        ],
        scratch=[pltpu.VMEM((width, width), BF16), pltpu.SemaphoreType.DMA((1,))],
        cost_estimate=cost(60),
        compiler_params=room(8),
        name="unmix",
    )


def attend_back_kernel(heads, q_ref, k_ref, v_ref, d_ref, sq_ref, state_ref, cut_ref, col_ref, row_ref, dq_ref, dk_ref, dv_ref, dist_ref, turned_ref):
    rows = q_ref.shape[0]
    half = rows // 2
    distance_tables(col_ref[...], row_ref[...], dist_ref)
    turned_ref[...] = dist_ref[...].T
    for head in range(heads):
        cols = slice(head * HEAD_DIM, (head + 1) * HEAD_DIM)
        slope = slope_of(head)
        cut = jnp.exp(-slope * cut_ref[...])
        for block in range(2):
            low, high = block * half, (block + 1) * half
            decay = jnp.exp(-slope * dist_ref[low:high, :high])
            d_prod = (dot_nt(d_ref[low:high, cols], v_ref[:high, cols]) * decay).astype(BF16)
            d_query = dot(d_prod, k_ref[:high, cols])
            d_query += cut[low:high] * dot_nt(d_ref[low:high, cols], state_ref[cols, :])
            dq_ref[low:high, cols] = (d_query * sq_ref[low:high, cols].astype(F32)).astype(BF16)
        for block in range(2):
            low, high = block * half, (block + 1) * half
            decay = jnp.exp(-slope * turned_ref[low:high, low:])
            scores = (dot_nt(k_ref[low:high, cols], q_ref[low:, cols]) * decay).astype(BF16)
            dv_ref[low:high, cols] = dot(scores, d_ref[low:, cols])
            d_prod = (dot_nt(v_ref[low:high, cols], d_ref[low:, cols]) * decay).astype(BF16)
            dk_ref[low:high, cols] = dot(d_prod, q_ref[low:, cols])


def attend_back(query, key, value, d_att, q_slope, state, cut_dist, seg_col, seg_row, deps=()):
    rows, width = query.shape
    return run(
        functools.partial(attend_back_kernel, width // HEAD_DIM),
        (query, key, value, d_att, q_slope, state, cut_dist, seg_col, seg_row),
        deps=deps,
        in_specs=[vmem()] * 9,
        out_specs=[vmem()] * 3,
        out_shape=[sds((rows, width), kind) for kind in (BF16, F32, F32)],
        scratch=[pltpu.VMEM((rows, rows), F32)] * 2,
        cost_estimate=cost(0.2),
        compiler_params=room(7),
        name="attend_back",
    )


def join_kernel(heads, dq_ref, dk_ref, dv_ref, k_ref, v_ref, sk_ref, state_ref, cut_ref, out_ref):
    for head in range(heads):
        cols = slice(head * HEAD_DIM, (head + 1) * HEAD_DIM)
        cut = jnp.exp(-slope_of(head) * cut_ref[...])
        group = heads // 2 * HEAD_DIM
        at = head // (heads // 2) * 3 * group + head % (heads // 2) * HEAD_DIM
        out_ref[:, at : at + HEAD_DIM] = dq_ref[:, cols]
        d_key = dk_ref[:, cols] + cut * dot_nt(v_ref[:, cols], state_ref[cols, :])
        out_ref[:, at + group : at + group + HEAD_DIM] = (d_key * sk_ref[:, cols].astype(F32)).astype(BF16)
        d_value = dv_ref[:, cols] + cut * dot(k_ref[:, cols], state_ref[cols, :])
        out_ref[:, at + 2 * group : at + 2 * group + HEAD_DIM] = d_value.astype(BF16)


def join_back(dq, dk, dv, key, value, k_slope, state, cut_dist, deps=()):
    rows, width = key.shape
    return run(
        functools.partial(join_kernel, width // HEAD_DIM),
        (dq, dk, dv, key, value, k_slope, state, cut_dist),
        deps=deps,
        in_specs=[vmem()] * 8,
        out_specs=vmem(),
        out_shape=sds((rows, 3 * width), BF16),
        cost_estimate=cost(0.2),
        compiler_params=room(4),
        name="join_back",
    )


def input_kernel(dqkv_ref, dmix_ref, w_ref, dh_ref, x_ref, out_ref, *refs):
    bufs, sem = refs[:4], refs[4]
    rows, width = x_ref.shape
    half = width // 2
    copies = fetch(w_ref, [i * width for i in range(4)], bufs, sem)
    for copy in copies:
        copy.wait()
    for low in range(0, rows, 256):
        part = slice(low, low + 256)
        total = dot_nt(dmix_ref[part, width:], bufs[3][...])
        for i in range(3):
            for side in range(2):
                at = side * 3 * half + i * half
                total += dot_nt(dqkv_ref[part, at : at + half], bufs[i][:, side * half : (side + 1) * half])
        inputs = x_ref[part, :].astype(F32)
        out_ref[part, :] = dh_ref[part, :] + norm_back(inputs, row_factor(inputs), total)


def input_grad_of(dqkv, d_mixer, weights, d_hidden, tokens, deps=()):
    rows, width = tokens.shape
    return run(
        input_kernel,
        (dqkv, d_mixer, weights, d_hidden, tokens),
        deps=deps,
        in_specs=[vmem(), vmem(), hbm(), vmem(), vmem()],
        out_specs=vmem(),
        out_shape=sds((rows, width), F32),
        scratch=[pltpu.VMEM((width, width), BF16)] * 4
        + [pltpu.SemaphoreType.DMA((4,))],
        cost_estimate=cost(0.2),
        compiler_params=room(14),
        name="input_grad",
    )


def grad_kernel(jobs, wide, first, table, *refs):
    right_ref, late_ref, soon_ref, keep_ref, turned = refs[-5:]
    width = turned.shape[0]
    half = width // 2
    rows = width // table.shape[0]
    loaded = None
    for block, job in enumerate(jobs):
        if job != loaded:
            loaded = job
            start = 0
            for source in refs[job[0] : job[0] + job[1]]:
                tokens = source.shape[0]
                for at in range(0, width, 128):
                    flat = source[:, at : at + 128].T
                    for sub in range(128 // rows):
                        place = pl.multiple_of(table[at // rows + sub] * rows, rows)
                        turned[pl.ds(place, rows), start : start + tokens] = flat[sub * rows : (sub + 1) * rows]
                start += tokens
        def columns(cols, source):
            right = right_ref[:, source]
            keep_ref[:, cols] = dot(turned[:half, :], right).astype(BF16)
            sent = dot(turned[half:, :], right).astype(BF16)
            late_ref[:, cols] = sent[: half // 2]
            soon_ref[:, cols] = sent[half // 2 :]

        if wide * len(jobs) <= 2048:
            for low in range(block * wide, (block + 1) * wide, 256):
                columns(slice(low, low + 256), slice(first + low, first + low + 256))
            continue

        def body(j, carry, block=block, columns=columns):
            low = pl.multiple_of(block * wide + j * 256, 128)
            columns(pl.ds(low, 256), pl.ds(pl.multiple_of(first + low, 128), 256))
            return carry

        lax.fori_loop(0, wide // 256, body, 0)
        if wide % 256:
            low, high = (block + 1) * wide - wide % 256, (block + 1) * wide
            columns(slice(low, high), slice(first + low, first + high))


def weight_grads(axes, stacks, jobs, right, span=None, deps=()):
    tokens, columns = right.shape
    if span is not None:
        columns = span[1] - span[0]
    wide = columns // len(jobs)
    width = stacks[0].shape[1]
    bits = lax.axis_size("zy").bit_length() - 1
    natural = list(range(bits - 1, -1, -1)) + ["core"] + (["seq"] if "seq" in axes else [])
    leaving = list(axes) + [axis for axis in natural if axis not in axes]
    owner = jnp.arange(2 ** len(natural), dtype=jnp.int32)
    place = jnp.zeros_like(owner)
    for rank, axis in enumerate(leaving):
        bit = (owner >> (len(natural) - 1 - natural.index(axis))) & 1
        if axis in axes:
            bit = bit ^ place_on(axis)
        place = place + (bit << (len(leaving) - 1 - rank))
    return run(
        functools.partial(grad_kernel, jobs, wide, 0 if span is None else span[0]),
        (place, *stacks, right),
        scalars=1,
        deps=deps,
        in_specs=[vmem()] * (len(stacks) + 1),
        out_specs=[vmem()] * 3,
        out_shape=[sds((width // parts, columns), BF16) for parts in (4, 4, 2)],
        scratch=[pltpu.VMEM((width, tokens), BF16)],
        cost_estimate=cost(0.2),
        compiler_params=room(8 if columns > 3 * width else 6),
        name="weight_grads",
    )


def place_on(axis):
    if isinstance(axis, int):
        return (lax.axis_index("zy") >> axis) & 1
    return lax.axis_index(axis)


def swap(values, axis):
    if isinstance(axis, int):
        size = lax.axis_size("zy")
        return lax.ppermute(values, "zy", [(i, i ^ (1 << axis)) for i in range(size)])
    return lax.ppermute(values, axis, [(i, i ^ 1) for i in range(lax.axis_size(axis))])


def tie(value, *earlier):
    return lax.optimization_barrier((value, *earlier))[0]


class RowSums:
    def __init__(self, axes, late, soon, kept):
        self.axes, self.kept, self.sent = list(axes), kept, (soon, late)
        self.rows = kept.shape[0]
        self.terms = None

    def take(self, *earlier):
        axis = self.axes.pop(0)
        if self.terms is None:
            soon, late = (swap(each, axis) for each in self.sent)
            self.rows //= 2
            soon = tie(soon, *earlier)
            self.terms = [self.kept, late]
            self.sent = (self.kept[self.rows :].astype(F32) + soon.astype(F32)).astype(BF16)
            return self.sent
        got = swap(self.sent, axis)
        self.terms.append(tie(got, *earlier) if earlier else got)
        if not self.axes:
            return self.total(0, self.rows)
        self.rows //= 2
        self.sent = self.total(self.rows, 2 * self.rows)
        return self.sent

    def total(self, low, high):
        return functools.reduce(jnp.add, [t[low:high].astype(F32) for t in self.terms]).astype(BF16)


def on_device(tokens, segments, w_query, w_key, w_value, w_gate, w_out, w_sglu_in, w_sglu_down, cotangent):
    rows, width = tokens.shape[1:]
    heads = width // HEAD_DIM
    planes = lax.axis_size("seq")
    plane = lax.axis_index("seq")
    ff = w_sglu_down.shape[1]
    part = ff // planes
    inputs, grad_tok = tokens[0], cotangent[0]
    bits = lax.axis_size("zy").bit_length() - 1
    zy = [0] + list(range(bits - 1, 0, -1))

    segs = lax.dynamic_slice_in_dim(segments[0], plane * rows, rows)
    edge = segments[0, rows - 1]
    places = jnp.arange(rows, dtype=jnp.int32)
    same = segs == edge
    from_cut = jnp.where(same, (places + 1).astype(F32), FAR)[:, None]
    to_cut = jnp.where(same, (rows - 1 - places).astype(F32), FAR)[:, None]
    seg_col, seg_row = segs[:, None], segs[None, :]

    shard = gather_shard(plane, part, (w_query, w_key, w_value, w_gate, w_out), w_sglu_in, w_sglu_down)
    weights = pltpu.with_memory_space_constraint(
        lax.all_gather(shard, ("zy", "core"), axis=0, tiled=True), pltpu.HBM
    )
    first = 5 * width

    grad_other = swap(grad_tok, "seq")
    x32 = inputs.astype(F32)
    normed_in = (x32 * row_factor(x32)).astype(BF16)

    key, k_slope, value, state = project_kv(normed_in, weights, to_cut, (grad_other,))
    state = lax.ppermute(state, "seq", [(i, i + 1) for i in range(planes - 1)])
    query, q_slope, gate = project_qu(normed_in, weights)
    att = attend_local(query, key, value, seg_col, seg_row)
    attended, gated, hidden, normed, *sides = mix_out(
        att, query, gate, inputs, state, from_cut, weights
    )

    top, bottom = (swap(side, "seq") for side in sides)
    half = rows // 2
    block = functools.partial(feed_forward, first, part)
    acts, back_own = block(F32, 0, planes * rows, normed, 0, grad_tok, weights)
    acts, back_top = block(BF16, rows, planes * rows, top, 0, grad_other, weights, acts)
    back_top = swap(back_top, "seq")
    acts, back_bottom = block(BF16, rows + half, planes * rows, bottom, half, grad_other, weights, acts)
    back_bottom = swap(back_bottom, "seq")

    late_ff, soon_ff, kept_ff = weight_grads(
        ["core"],
        (normed, top, bottom, grad_tok, grad_other),
        [(0, 3), (0, 3), (3, 2)],
        acts,
        None,
        (back_top,),
    )
    d_hidden, d_mixer, d_att, back_state = unmix(
        hidden, back_own, back_top, back_bottom, grad_tok, gate, attended, query, from_cut, weights, (soon_ff,)
    )
    back_state = lax.ppermute(back_state, "seq", [(i + 1, i) for i in range(planes - 1)])
    soon_ff, late_ff = (tie(swap(each, "core"), d_mixer) for each in (soon_ff, late_ff))
    ff_part = fold(kept_ff, late_ff, soon_ff)
    ff_sum = lax.psum_scatter(ff_part, "zy", scatter_dimension=0, tiled=True)

    low_axes = ["core", "seq"] + zy
    high_axes = ["core", 0, "seq"] + zy[1:]
    grads_mix = weight_grads(low_axes, (gated, normed_in), [(0, 1), (1, 1)], d_mixer, None, (ff_part, back_state))
    mixed = RowSums(low_axes, *grads_mix)
    latest = [grads_mix[0]]

    def step(*sums):
        for each in sums:
            latest[:] = [each.take(*latest)]
        return latest[0]

    dq, dk, dv = attend_back(
        query, key, value, d_att, q_slope, state, from_cut, seg_col, seg_row, (step(mixed),)
    )
    dqkv = join_back(dq, dk, dv, key, value, k_slope, back_state, to_cut)

    cut = heads // 2 * 3 * HEAD_DIM
    grads_low = weight_grads(low_axes, (normed_in,), [(0, 1)], dqkv, (0, cut))
    low_heads = RowSums(low_axes, *grads_low)
    grads_high = weight_grads(high_axes, (normed_in,), [(0, 1)], dqkv, (cut, 2 * cut), (grads_low[0],))
    high_heads = RowSums(high_axes, *grads_high)
    latest[:] = [grads_high[0]]
    step(mixed, low_heads, high_heads)
    out_own, out_sent = down_project(first, part, acts, weights, (latest[0],))
    out_other = swap(out_sent, "seq")
    input_grad = input_grad_of(dqkv, d_mixer, weights, d_hidden, inputs, (out_own,))
    latest[:] = [input_grad]
    step(mixed, low_heads, high_heads)
    ff_sum = tie(ff_sum, *latest)
    latest[:] = [ff_sum]
    while any(each.axes for each in (low_heads, high_heads, mixed)):
        for each in (mixed, low_heads, high_heads):
            if each.axes:
                step(each)
    low_sum, high_sum, mixed_sum = (each.total(0, each.rows) for each in (low_heads, high_heads, mixed))
    output = add_output(hidden, out_own, out_other, (mixed_sum,))

    def both_planes(values):
        other = swap(values, "seq")
        low = jnp.where(plane == 0, values, other).astype(F32)
        high = jnp.where(plane == 0, other, values).astype(F32)
        return low, high

    low, high = both_planes(ff_sum)
    grad_in = jnp.concatenate(
        [low[:, :part], high[:, :part], low[:, part : 2 * part], high[:, part : 2 * part]], 1
    )
    grad_down = jnp.concatenate([low[:, 2 * part :], high[:, 2 * part :]], 1)
    mix_total = jnp.concatenate(both_planes(mixed_sum), 0)
    sides = jnp.concatenate(both_planes(jnp.concatenate([low_sum, high_sum], 1)), 0)
    wide = width // 2
    grads = [
        jnp.concatenate([sides[:, i * wide : (i + 1) * wide], sides[:, (3 + i) * wide : (4 + i) * wide]], 1)
        for i in range(3)
    ]
    return (
        output[None],
        input_grad[None],
        *grads,
        mix_total[:, width:],
        mix_total[:, :width],
        grad_in,
        grad_down,
    )


def solution(mesh):
    planes, group = mesh.devices.shape
    devices = mesh.devices.reshape(planes, group // 2, 2)
    split = Mesh(devices, ("seq", "zy", "core"))
    rows = ("zy", "core")
    tok = P(rows, "seq", None)
    mat = P(rows, None)
    return jax.shard_map(
        on_device,
        mesh=split,
        in_specs=(tok,) + (mat,) * 8 + (tok,),
        out_specs=(tok, tok) + (mat,) * 7,
        check_vma=False,
    )
```

```python
import functools

import jax
import jax.numpy as jnp
from jax import lax
from jax.experimental import pallas as pl
from jax.experimental.pallas import tpu as pltpu
from jax.sharding import Mesh
from jax.sharding import PartitionSpec as P

HEAD_DIM = 128
EPSILON = 1e-06
FAR = 1e9
F32 = jnp.float32
BF16 = jnp.bfloat16


def dot(left, right):
    return jnp.dot(left, right, preferred_element_type=F32)


def dot_nt(left, right):
    return lax.dot_general(left, right, (((1,), (1,)), ((), ())), preferred_element_type=F32)


def dot_tn(left, right):
    return lax.dot_general(left, right, (((0,), (0,)), ((), ())), preferred_element_type=F32)


def row_factor(values):
    return lax.rsqrt(jnp.mean(values * values, axis=-1, keepdims=True) + EPSILON)


def norm_back(values, factor, upstream):
    normed = values * factor
    return factor * (upstream - normed * jnp.mean(upstream * normed, axis=-1, keepdims=True))


def sds(shape, kind):
    return jax.ShapeDtypeStruct(shape, kind)


def full(shape):
    return pl.BlockSpec(shape, lambda *_: (0,) * len(shape))


def vmem():
    return pl.BlockSpec(memory_space=pltpu.VMEM)


def hbm():
    return pl.BlockSpec(memory_space=pltpu.HBM)


def fetch(w_ref, firsts, bufs, sem):
    copies = []
    for i, (first, buf) in enumerate(zip(firsts, bufs, strict=True)):
        copies.append(pltpu.make_async_copy(w_ref.at[:, first : first + buf.shape[1]], buf, sem.at[i]))
        copies[-1].start()
    return copies


def cost(micros):
    return pl.CostEstimate(flops=int(micros * 1.1e9), bytes_accessed=0, transcendentals=0)


def run(kernel, operands, in_specs, deps=(), scalars=0, grid=(1,), scratch=(), **options):
    given = len(operands)

    def body(*refs):
        kernel(*refs[:given], *refs[given + len(deps) :])

    return pl.pallas_call(
        body,
        grid_spec=pltpu.PrefetchScalarGridSpec(
            num_scalar_prefetch=scalars,
            grid=grid,
            in_specs=list(in_specs) + [pl.BlockSpec(memory_space=pl.ANY)] * len(deps),
            out_specs=options.pop("out_specs"),
            scratch_shapes=list(scratch),
        ),
        **options,
    )(*operands, *deps)


def room(mebibytes):
    return pltpu.CompilerParams(vmem_limit_bytes=mebibytes << 20)


def slope_of(head):
    return 0.25 * 2.0 ** (-0.5 * (head + 1))


def shard_kernel(plane_ref, *refs):
    out_ref, flag_ref = refs[-2:]
    flag_ref[...] = jnp.full(flag_ref.shape, plane_ref[0] == 0, F32)
    at = 0
    for ref in refs[:-2]:
        out_ref[:, at : at + ref.shape[1]] = ref[...]
        at += ref.shape[1]


def gather_shard(plane, part, mixer, w_in, w_down):
    rows = w_in.shape[0]
    planes = w_down.shape[1] // part
    wide = sum(w.shape[1] for w in mixer) + 3 * part
    return run(
        shard_kernel,
        (jnp.reshape(plane, (1,)), *mixer, w_in, w_in, w_down),
        scalars=1,
        in_specs=[pl.BlockSpec(w.shape, lambda i, p: (0, 0)) for w in mixer]
        + [
            pl.BlockSpec((rows, part), lambda i, p: (0, p[0])),
            pl.BlockSpec((rows, part), lambda i, p: (0, p[0] + planes)),
            pl.BlockSpec((rows, part), lambda i, p: (0, p[0])),
        ],
        out_specs=[pl.BlockSpec((rows, wide), lambda i, p: (0, 0)), pl.BlockSpec((rows, 128), lambda i, p: (0, 0))],
        out_shape=[sds((rows, wide), BF16), sds((rows, 128), F32)],
        compiler_params=room(8),
        name="gather_shard",
    )


def swish_parts(pre):
    sig = jax.nn.sigmoid(pre)
    return (pre * sig).astype(BF16), (sig * (1.0 + pre * (1.0 - sig))).astype(BF16)


def kv_kernel(heads, normed_ref, w_ref, dist_ref, key_ref, slope_ref, value_ref, state_ref, wk, wv, sem):
    width = normed_ref.shape[1]
    copies = fetch(w_ref, (width, 2 * width), (wk, wv), sem)
    copies[0].wait()
    for low in range(0, width, 256):
        cols = slice(low, low + 256)
        key_ref[:, cols], slope_ref[:, cols] = swish_parts(dot(normed_ref[...], wk[:, cols]))
    copies[1].wait()
    for low in range(0, width, 256):
        cols = slice(low, low + 256)
        value_ref[:, cols] = dot(normed_ref[...], wv[:, cols]).astype(BF16)
    for head in range(heads):
        cols = slice(head * HEAD_DIM, (head + 1) * HEAD_DIM)
        weight = jnp.exp(-slope_of(head) * dist_ref[...])
        scaled = (key_ref[:, cols].astype(F32) * weight).astype(BF16)
        state_ref[cols, :] = dot_tn(scaled, value_ref[:, cols]).astype(BF16)


def project_kv(normed, weights, cut_dist, deps=()):
    rows, width = normed.shape
    heads = width // HEAD_DIM
    act = sds((rows, width), BF16)
    return run(
        functools.partial(kv_kernel, heads),
        (normed, weights, cut_dist),
        deps=deps,
        in_specs=[vmem(), hbm(), vmem()],
        out_specs=[vmem()] * 4,
        out_shape=[act, act, act, sds((width, HEAD_DIM), BF16)],
        scratch=[pltpu.VMEM((width, width), BF16)] * 2 + [pltpu.SemaphoreType.DMA((2,))],
        cost_estimate=cost(0.2),
        compiler_params=room(12),
        name="project_kv",
    )


def qu_kernel(normed_ref, w_ref, query_ref, slope_ref, gate_ref, wq, wu, sem):
    width = normed_ref.shape[1]
    copies = fetch(w_ref, (0, 3 * width), (wq, wu), sem)
    copies[0].wait()
    for low in range(0, width, 256):
        cols = slice(low, low + 256)
        query_ref[:, cols], slope_ref[:, cols] = swish_parts(dot(normed_ref[...], wq[:, cols]))
    copies[1].wait()
    for low in range(0, width, 256):
        cols = slice(low, low + 256)
        gate_ref[:, cols] = dot(normed_ref[...], wu[:, cols]).astype(BF16)


def project_qu(normed, weights):
    rows, width = normed.shape
    act = sds((rows, width), BF16)
    return run(
        qu_kernel,
        (normed, weights),
        in_specs=[vmem(), hbm()],
        out_specs=[vmem()] * 3,
        out_shape=[act, act, act],
        scratch=[pltpu.VMEM((width, width), BF16)] * 2 + [pltpu.SemaphoreType.DMA((2,))],
        cost_estimate=cost(0.2),
        compiler_params=room(12),
        name="project_qu",
    )


def distance_tables(seg_col, seg_row, dist_ref):
    rows = seg_col.shape[0]
    span = lax.broadcasted_iota(jnp.int32, (rows, rows), 0) - lax.broadcasted_iota(
        jnp.int32, (rows, rows), 1
    )
    allowed = (span >= 0) & (seg_col == seg_row)
    dist_ref[...] = jnp.where(allowed, span.astype(F32), FAR)


def attend_kernel(heads, q_ref, k_ref, v_ref, col_ref, row_ref, out_ref, dist_ref):
    distance_tables(col_ref[...], row_ref[...], dist_ref)
    rows = q_ref.shape[0]
    half = rows // 2
    for head in range(heads):
        cols = slice(head * HEAD_DIM, (head + 1) * HEAD_DIM)
        for block in range(2):
            low, high = block * half, (block + 1) * half
            decay = jnp.exp(-slope_of(head) * dist_ref[low:high, :high])
            scores = (dot_nt(q_ref[low:high, cols], k_ref[:high, cols]) * decay).astype(BF16)
            out_ref[low:high, cols] = dot(scores, v_ref[:high, cols])


def attend_local(query, key, value, seg_col, seg_row):
    rows, width = query.shape
    return run(
        functools.partial(attend_kernel, width // HEAD_DIM),
        (query, key, value, seg_col, seg_row),
        in_specs=[vmem()] * 5,
        out_specs=vmem(),
        out_shape=sds((rows, width), F32),
        scratch=[pltpu.VMEM((rows, rows), F32)],
        cost_estimate=cost(0.2),
        compiler_params=room(10),
        name="attend_local",
    )


def mix_kernel(heads, att_ref, q_ref, u_ref, x_ref, state_ref, dist_ref, w_ref, att_out, gated_out, hidden_out, normed_out, top_out, bottom_out, wo, sem):
    width = q_ref.shape[1]
    rows = q_ref.shape[0]
    copies = fetch(w_ref, (4 * width,), (wo,), sem)
    for head in range(heads):
        cols = slice(head * HEAD_DIM, (head + 1) * HEAD_DIM)
        weight = jnp.exp(-slope_of(head) * dist_ref[...])
        scaled = (q_ref[:, cols].astype(F32) * weight).astype(BF16)
        att_out[:, cols] = (att_ref[:, cols] + dot(scaled, state_ref[cols, :])).astype(BF16)
    copies[0].wait()
    for low in range(0, rows, 256):
        part = slice(low, low + 256)
        attended = att_out[part, :].astype(F32)
        gated = (attended * row_factor(attended) * u_ref[part, :].astype(F32)).astype(BF16)
        gated_out[part, :] = gated
        hidden = x_ref[part, :].astype(F32) + dot(gated, wo[...])
        hidden_out[part, :] = hidden
        normed = (hidden * row_factor(hidden)).astype(BF16)
        normed_out[part, :] = normed
        half_out, at = (top_out, low) if 2 * low < rows else (bottom_out, low - rows // 2)
        half_out[at : at + 256, :] = normed


def mix_out(att, query, gate, tokens, state, cut_dist, weights):
    rows, width = query.shape
    return run(
        functools.partial(mix_kernel, width // HEAD_DIM),
        (att, query, gate, tokens, state, cut_dist, weights),
        in_specs=[vmem()] * 6 + [hbm()],
        out_specs=[vmem()] * 6,
        out_shape=[sds((rows, width), kind) for kind in (BF16, BF16, F32, BF16)]
        + [sds((rows // 2, width), BF16)] * 2,
        scratch=[pltpu.VMEM((width, width), BF16), pltpu.SemaphoreType.DMA((1,))],
        cost_estimate=cost(0.2),
        compiler_params=room(12),
        name="mix_out",
    )


def ff_kernel(first, grad_first, normed_ref, grad_ref, w_ref, acts_ref, back_ref, wg, wu, wd, sem):
    part = wg.shape[1]
    rows, width = normed_ref.shape
    blocks = [slice(low, min(low + 256, part)) for low in range(0, part, 256)]
    copies = []
    for block, cols in enumerate(blocks):
        for which, buf in enumerate((wg, wu, wd)):
            source = slice(first + which * part + cols.start, first + which * part + cols.stop)
            copies.append(
                pltpu.make_async_copy(w_ref.at[:, source], buf.at[:, cols], sem.at[3 * block + which])
            )
            copies[-1].start()
    for block, cols in enumerate(blocks):
        for copy in copies[3 * block : 3 * block + 3]:
            copy.wait()
        gate = dot(normed_ref[...], wg[:, cols])
        up = dot(normed_ref[...], wu[:, cols])
        d_hidden = dot(grad_ref[grad_first : grad_first + rows, :], wd[:, cols])
        for which, value in enumerate((d_hidden * up, d_hidden * gate, gate * up)):
            acts_ref[:, which * part + cols.start : which * part + cols.stop] = value.astype(BF16)
    for low in range(0, width, 256):
        block = slice(low, low + 256)
        back = dot_nt(acts_ref[:, :part], wg[block, :]) + dot_nt(acts_ref[:, part : 2 * part], wu[block, :])
        back_ref[:, block] = back.astype(back_ref.dtype)


def feed_forward(first, part, kind, normed, grad_first, grad, weights, deps=()):
    rows, width = normed.shape
    return run(
        functools.partial(ff_kernel, first, grad_first),
        (normed, grad, weights),
        deps=deps,
        in_specs=[vmem(), vmem(), hbm()],
        out_specs=[vmem()] * 2,
        out_shape=[sds((rows, 3 * part), BF16), sds((rows, width), kind)],
        scratch=[pltpu.VMEM((width, part), BF16)] * 3
        + [pltpu.SemaphoreType.DMA((3 * -(-part // 256),))],
        cost_estimate=cost(0.2),
        compiler_params=room(22),
        name="feed_forward",
    )


def down_kernel(first, own_acts, top_acts, bottom_acts, w_ref, own_ref, other_ref, wd, sem):
    part = wd.shape[1]
    width = own_ref.shape[1]
    half = top_acts.shape[0]
    copies = fetch(w_ref, (first + 2 * part,), (wd,), sem)
    copies[0].wait()
    for low in range(0, width, 256):
        block = slice(low, low + 256)
        own_ref[:, block] = dot_nt(own_acts[:, 2 * part :], wd[block, :])
        other_ref[:half, block] = dot_nt(top_acts[:, 2 * part :], wd[block, :]).astype(BF16)
        other_ref[half:, block] = dot_nt(bottom_acts[:, 2 * part :], wd[block, :]).astype(BF16)


def down_project(first, part, acts, weights, deps=()):
    width = weights.shape[0]
    rows = acts[0].shape[0]
    return run(
        functools.partial(down_kernel, first),
        (*acts, weights),
        deps=deps,
        in_specs=[vmem()] * 3 + [hbm()],
        out_specs=[vmem()] * 2,
        out_shape=[sds((rows, width), F32), sds((rows, width), BF16)],
        scratch=[pltpu.VMEM((width, part), BF16), pltpu.SemaphoreType.DMA((1,))],
        cost_estimate=cost(0.2),
        compiler_params=room(12),
        name="down_project",
    )


def add_kernel(hidden_ref, own_ref, other_ref, out_ref):
    out_ref[...] = (hidden_ref[...] + own_ref[...] + other_ref[...].astype(F32)).astype(BF16)


def add_output(hidden, own, other, deps):
    return run(
        add_kernel,
        (hidden, own, other),
        deps=deps,
        in_specs=[vmem()] * 3,
        out_specs=vmem(),
        out_shape=sds(hidden.shape, BF16),
        cost_estimate=cost(1),
        compiler_params=room(8),
        name="add_output",
    )


def fold_kernel(kept_ref, late_ref, soon_ref, out_ref):
    half = late_ref.shape[0]
    out_ref[:half, :] = (kept_ref[:half, :].astype(F32) + late_ref[...].astype(F32)).astype(BF16)
    out_ref[half:, :] = (kept_ref[half:, :].astype(F32) + soon_ref[...].astype(F32)).astype(BF16)


def fold(kept, late, soon):
    return run(
        fold_kernel,
        (kept, late, soon),
        in_specs=[vmem()] * 3,
        out_specs=vmem(),
        out_shape=sds(kept.shape, BF16),
        cost_estimate=cost(0.2),
        compiler_params=room(8),
        name="fold",
    )


def unmix_kernel(heads, hidden_ref, own_ref, top_ref, bottom_ref, grad_ref, u_ref, att_ref, q_ref, dist_ref, w_ref, d_hidden_out, d_mixer_out, d_att_out, state_out, wo, sem):
    rows, width = q_ref.shape
    copies = fetch(w_ref, (4 * width,), (wo,), sem)
    for low in range(0, rows, 256):
        part = slice(low, low + 256)
        hidden = hidden_ref[part, :]
        half_ref, at = (top_ref, low) if 2 * low < rows else (bottom_ref, low - rows // 2)
        upstream = own_ref[part, :] + half_ref[at : at + 256, :].astype(F32)
        d_hidden = grad_ref[part, :].astype(F32) + norm_back(hidden, row_factor(hidden), upstream)
        d_hidden_out[part, :] = d_hidden
        d_mixer_out[part, :width] = d_hidden.astype(BF16)
    copies[0].wait()
    for low in range(0, rows, 256):
        part = slice(low, low + 256)
        d_gated = dot_nt(d_mixer_out[part, :width], wo[...])
        attended = att_ref[part, :].astype(F32)
        factor = row_factor(attended)
        d_mixer_out[part, width:] = (d_gated * (attended * factor)).astype(BF16)
        d_att_out[part, :] = norm_back(attended, factor, d_gated * u_ref[part, :].astype(F32)).astype(BF16)
    for head in range(heads):
        cols = slice(head * HEAD_DIM, (head + 1) * HEAD_DIM)
        weight = jnp.exp(-slope_of(head) * dist_ref[...])
        scaled = (q_ref[:, cols].astype(F32) * weight).astype(BF16)
        state_out[cols, :] = dot_tn(scaled, d_att_out[:, cols]).astype(BF16)


def unmix(hidden, back_own, back_top, back_bottom, grad, gate, attended, query, cut_dist, weights, deps=()):
    rows, width = query.shape
    return run(
        functools.partial(unmix_kernel, width // HEAD_DIM),
        (hidden, back_own, back_top, back_bottom, grad, gate, attended, query, cut_dist, weights),
        deps=deps,
        in_specs=[vmem()] * 9 + [hbm()],
        out_specs=[vmem()] * 4,
        out_shape=[
            sds((rows, width), F32),
            sds((rows, 2 * width), BF16),
            sds((rows, width), BF16),
            sds((width, HEAD_DIM), BF16),
        ],
        scratch=[pltpu.VMEM((width, width), BF16), pltpu.SemaphoreType.DMA((1,))],
        cost_estimate=cost(60),
        compiler_params=room(14),
        name="unmix",
    )


def attend_back_kernel(heads, q_ref, k_ref, v_ref, d_ref, sq_ref, state_ref, cut_ref, col_ref, row_ref, dq_ref, dk_ref, dv_ref, dist_ref, turned_ref):
    rows = q_ref.shape[0]
    half = rows // 2
    distance_tables(col_ref[...], row_ref[...], dist_ref)
    turned_ref[...] = dist_ref[...].T
    for head in range(heads):
        cols = slice(head * HEAD_DIM, (head + 1) * HEAD_DIM)
        slope = slope_of(head)
        cut = jnp.exp(-slope * cut_ref[...])
        for block in range(2):
            low, high = block * half, (block + 1) * half
            decay = jnp.exp(-slope * dist_ref[low:high, :high])
            d_prod = (dot_nt(d_ref[low:high, cols], v_ref[:high, cols]) * decay).astype(BF16)
            d_query = dot(d_prod, k_ref[:high, cols])
            d_query += cut[low:high] * dot_nt(d_ref[low:high, cols], state_ref[cols, :])
            dq_ref[low:high, cols] = (d_query * sq_ref[low:high, cols].astype(F32)).astype(BF16)
        for block in range(2):
            low, high = block * half, (block + 1) * half
            decay = jnp.exp(-slope * turned_ref[low:high, low:])
            scores = (dot_nt(k_ref[low:high, cols], q_ref[low:, cols]) * decay).astype(BF16)
            dv_ref[low:high, cols] = dot(scores, d_ref[low:, cols])
            d_prod = (dot_nt(v_ref[low:high, cols], d_ref[low:, cols]) * decay).astype(BF16)
            dk_ref[low:high, cols] = dot(d_prod, q_ref[low:, cols])


def attend_back(query, key, value, d_att, q_slope, state, cut_dist, seg_col, seg_row, deps=()):
    rows, width = query.shape
    return run(
        functools.partial(attend_back_kernel, width // HEAD_DIM),
        (query, key, value, d_att, q_slope, state, cut_dist, seg_col, seg_row),
        deps=deps,
        in_specs=[vmem()] * 9,
        out_specs=[vmem()] * 3,
        out_shape=[sds((rows, width), kind) for kind in (BF16, F32, F32)],
        scratch=[pltpu.VMEM((rows, rows), F32)] * 2,
        cost_estimate=cost(0.2),
        compiler_params=room(12),
        name="attend_back",
    )


def join_kernel(heads, dq_ref, dk_ref, dv_ref, k_ref, v_ref, sk_ref, state_ref, cut_ref, out_ref):
    for head in range(heads):
        cols = slice(head * HEAD_DIM, (head + 1) * HEAD_DIM)
        cut = jnp.exp(-slope_of(head) * cut_ref[...])
        group = heads // 2 * HEAD_DIM
        at = head // (heads // 2) * 3 * group + head % (heads // 2) * HEAD_DIM
        out_ref[:, at : at + HEAD_DIM] = dq_ref[:, cols]
        d_key = dk_ref[:, cols] + cut * dot_nt(v_ref[:, cols], state_ref[cols, :])
        out_ref[:, at + group : at + group + HEAD_DIM] = (d_key * sk_ref[:, cols].astype(F32)).astype(BF16)
        d_value = dv_ref[:, cols] + cut * dot(k_ref[:, cols], state_ref[cols, :])
        out_ref[:, at + 2 * group : at + 2 * group + HEAD_DIM] = d_value.astype(BF16)


def join_back(dq, dk, dv, key, value, k_slope, state, cut_dist, deps=()):
    rows, width = key.shape
    return run(
        functools.partial(join_kernel, width // HEAD_DIM),
        (dq, dk, dv, key, value, k_slope, state, cut_dist),
        deps=deps,
        in_specs=[vmem()] * 8,
        out_specs=vmem(),
        out_shape=sds((rows, 3 * width), BF16),
        cost_estimate=cost(0.2),
        compiler_params=room(8),
        name="join_back",
    )


def input_kernel(dqkv_ref, dmix_ref, w_ref, dh_ref, x_ref, out_ref, *refs):
    bufs, sem = refs[:4], refs[4]
    rows, width = x_ref.shape
    half = width // 2
    copies = fetch(w_ref, [i * width for i in range(4)], bufs, sem)
    for copy in copies:
        copy.wait()
    for low in range(0, rows, 256):
        part = slice(low, low + 256)
        total = dot_nt(dmix_ref[part, width:], bufs[3][...])
        for i in range(3):
            for side in range(2):
                at = side * 3 * half + i * half
                total += dot_nt(dqkv_ref[part, at : at + half], bufs[i][:, side * half : (side + 1) * half])
        inputs = x_ref[part, :].astype(F32)
        out_ref[part, :] = dh_ref[part, :] + norm_back(inputs, row_factor(inputs), total)


def input_grad_of(dqkv, d_mixer, weights, d_hidden, tokens, deps=()):
    rows, width = tokens.shape
    return run(
        input_kernel,
        (dqkv, d_mixer, weights, d_hidden, tokens),
        deps=deps,
        in_specs=[vmem(), vmem(), hbm(), vmem(), vmem()],
        out_specs=vmem(),
        out_shape=sds((rows, width), F32),
        scratch=[pltpu.VMEM((width, width), BF16)] * 4
        + [pltpu.SemaphoreType.DMA((4,))],
        cost_estimate=cost(0.2),
        compiler_params=room(18),
        name="input_grad",
    )


def grad_kernel(jobs, wide, first, table, *refs):
    late_ref, soon_ref, keep_ref, turned = refs[-4:]
    rights = refs[max(job[0] + job[1] for job in jobs) : -4]
    width = turned.shape[0]
    half = width // 2
    rows = width // table.shape[0]
    loaded = None
    for block, job in enumerate(jobs):
        if job != loaded:
            loaded = job
            start = 0
            for source in refs[job[0] : job[0] + job[1]]:
                tokens = source.shape[0]
                for at in range(0, width, 128):
                    flat = source[:, at : at + 128].T
                    for sub in range(128 // rows):
                        place = pl.multiple_of(table[at // rows + sub] * rows, rows)
                        turned[pl.ds(place, rows), start : start + tokens] = flat[sub * rows : (sub + 1) * rows]
                start += tokens
        def columns(cols, source):
            right = jnp.concatenate([ref[:, source] for ref in rights], 0)
            keep_ref[:, cols] = dot(turned[:half, :], right).astype(BF16)
            sent = dot(turned[half:, :], right).astype(BF16)
            late_ref[:, cols] = sent[: half // 2]
            soon_ref[:, cols] = sent[half // 2 :]

        if wide * len(jobs) <= 2048:
            for low in range(block * wide, (block + 1) * wide, 256):
                columns(slice(low, low + 256), slice(first + low, first + low + 256))
            continue

        def body(j, carry, block=block, columns=columns):
            low = pl.multiple_of(block * wide + j * 256, 128)
            columns(pl.ds(low, 256), pl.ds(pl.multiple_of(first + low, 128), 256))
            return carry

        lax.fori_loop(0, wide // 256, body, 0)
        if wide % 256:
            low, high = (block + 1) * wide - wide % 256, (block + 1) * wide
            columns(slice(low, high), slice(first + low, first + high))


def places_of(axes):
    bits = lax.axis_size("zy").bit_length() - 1
    natural = list(range(bits - 1, -1, -1)) + ["core"] + (["seq"] if "seq" in axes else [])
    leaving = list(axes) + [axis for axis in natural if axis not in axes]
    owner = jnp.arange(2 ** len(natural), dtype=jnp.int32)
    place = jnp.zeros_like(owner)
    for rank, axis in enumerate(leaving):
        bit = (owner >> (len(natural) - 1 - natural.index(axis))) & 1
        if axis in axes:
            bit = bit ^ place_on(axis)
        place = place + (bit << (len(leaving) - 1 - rank))
    return place


def weight_grads(place, stacks, jobs, rights, span=None, deps=()):
    tokens, columns = sum(right.shape[0] for right in rights), rights[0].shape[1]
    if span is not None:
        columns = span[1] - span[0]
    wide = columns // len(jobs)
    width = stacks[0].shape[1]
    return run(
        functools.partial(grad_kernel, jobs, wide, 0 if span is None else span[0]),
        (place, *stacks, *rights),
        scalars=1,
        deps=deps,
        in_specs=[vmem()] * (len(stacks) + len(rights)),
        out_specs=[vmem()] * 3,
        out_shape=[sds((width // parts, columns), BF16) for parts in (4, 4, 2)],
        scratch=[pltpu.VMEM((width, tokens), BF16)],
        cost_estimate=cost(0.2),
        compiler_params=room(14 if columns > 3 * width else 12),
        name="weight_grads",
    )


def place_on(axis):
    if isinstance(axis, int):
        return (lax.axis_index("zy") >> axis) & 1
    return lax.axis_index(axis)


def swap(values, axis):
    if isinstance(axis, int):
        size = lax.axis_size("zy")
        return lax.ppermute(values, "zy", [(i, i ^ (1 << axis)) for i in range(size)])
    return lax.ppermute(values, axis, [(i, i ^ 1) for i in range(lax.axis_size(axis))])


def tie(value, *earlier):
    return lax.optimization_barrier((value, *earlier))[0]


class RowSums:
    def __init__(self, axes, late, soon, kept):
        self.axes, self.kept, self.sent = list(axes), kept, (soon, late)
        self.rows = kept.shape[0]
        self.terms = None

    def take(self, *earlier):
        axis = self.axes.pop(0)
        if self.terms is None:
            soon, late = (swap(each, axis) for each in self.sent)
            self.rows //= 2
            soon = tie(soon, *earlier)
            self.terms = [self.kept, late]
            self.sent = (self.kept[self.rows :].astype(F32) + soon.astype(F32)).astype(BF16)
            return self.sent
        got = swap(self.sent, axis)
        self.terms.append(tie(got, *earlier) if earlier else got)
        if not self.axes:
            return self.total(0, self.rows)
        self.rows //= 2
        self.sent = self.total(self.rows, 2 * self.rows)
        return self.sent

    def total(self, low, high):
        return functools.reduce(jnp.add, [t[low:high].astype(F32) for t in self.terms]).astype(BF16)


def on_device(tokens, segments, w_query, w_key, w_value, w_gate, w_out, w_sglu_in, w_sglu_down, cotangent):
    rows, width = tokens.shape[1:]
    heads = width // HEAD_DIM
    planes = lax.axis_size("seq")
    plane = lax.axis_index("seq")
    ff = w_sglu_down.shape[1]
    part = ff // planes
    inputs, grad_tok = tokens[0], cotangent[0]
    bits = lax.axis_size("zy").bit_length() - 1
    zy = [0] + list(range(bits - 1, 0, -1))

    segs = lax.dynamic_slice_in_dim(segments[0], plane * rows, rows)
    edge = segments[0, rows - 1]
    places = jnp.arange(rows, dtype=jnp.int32)
    same = segs == edge
    from_cut = jnp.where(same, (places + 1).astype(F32), FAR)[:, None]
    to_cut = jnp.where(same, (rows - 1 - places).astype(F32), FAR)[:, None]
    seg_col, seg_row = segs[:, None], segs[None, :]

    shard, on_first = gather_shard(plane, part, (w_query, w_key, w_value, w_gate, w_out), w_sglu_in, w_sglu_down)
    weights = pltpu.with_memory_space_constraint(
        lax.all_gather(shard, ("zy", "core"), axis=0, tiled=True), pltpu.HBM
    )
    first = 5 * width

    low_axes = ["core", "seq"] + zy
    high_axes = ["core", 0, "seq"] + zy[1:]
    ff_places, low_places, high_places = (places_of(axes) for axes in (["core"], low_axes, high_axes))

    grad_other = swap(grad_tok, "seq")
    x32 = inputs.astype(F32)
    normed_in = (x32 * row_factor(x32)).astype(BF16)

    key, k_slope, value, state = project_kv(
        normed_in, weights, to_cut, (grad_other, ff_places, low_places, high_places)
    )
    state = lax.ppermute(state, "seq", [(i, i + 1) for i in range(planes - 1)])
    query, q_slope, gate = project_qu(normed_in, weights)
    att = attend_local(query, key, value, seg_col, seg_row)
    attended, gated, hidden, normed, *sides = mix_out(
        att, query, gate, inputs, state, from_cut, weights
    )

    top, bottom = (swap(side, "seq") for side in sides)
    half = rows // 2
    block = functools.partial(feed_forward, first, part)
    own_acts, back_own = block(F32, normed, 0, grad_tok, weights)
    top_acts, back_top = block(BF16, top, 0, grad_other, weights, (back_own,))
    back_top = swap(back_top, "seq")
    bottom_acts, back_bottom = block(BF16, bottom, half, grad_other, weights, (top_acts,))
    back_bottom = swap(back_bottom, "seq")
    acts = (own_acts, top_acts, bottom_acts)

    late_ff, soon_ff, kept_ff = weight_grads(
        ff_places,
        (normed, top, bottom, grad_tok, grad_other),
        [(0, 3), (0, 3), (3, 2)],
        acts,
    )
    d_hidden, d_mixer, d_att, back_state = unmix(
        hidden, back_own, back_top, back_bottom, grad_tok, gate, attended, query, from_cut, weights, (soon_ff,)
    )
    back_state = lax.ppermute(back_state, "seq", [(i + 1, i) for i in range(planes - 1)])
    soon_ff, late_ff = (tie(swap(each, "core"), d_mixer) for each in (soon_ff, late_ff))
    ff_part = fold(kept_ff, late_ff, soon_ff)
    ff_sum = lax.psum_scatter(ff_part, "zy", scatter_dimension=0, tiled=True)

    grads_mix = weight_grads(low_places, (gated, normed_in), [(0, 1), (1, 1)], (d_mixer,), None, (ff_part,))
    mixed = RowSums(low_axes, *grads_mix)
    latest = [grads_mix[0]]

    def step(*sums):
        for each in sums:
            latest[:] = [each.take(*latest)]
        return latest[0]

    dq, dk, dv = attend_back(
        query, key, value, d_att, q_slope, state, from_cut, seg_col, seg_row, (grads_mix[0],)
    )
    latest[:] = [dq, back_state]
    dqkv = join_back(dq, dk, dv, key, value, k_slope, back_state, to_cut, (step(mixed),))

    cut = heads // 2 * 3 * HEAD_DIM
    grads_low = weight_grads(low_places, (normed_in,), [(0, 1)], (dqkv,), (0, cut))
    low_heads = RowSums(low_axes, *grads_low)
    grads_high = weight_grads(high_places, (normed_in,), [(0, 1)], (dqkv,), (cut, 2 * cut), (grads_low[0],))
    high_heads = RowSums(high_axes, *grads_high)
    latest[:] = [grads_high[0]]
    out_own, out_sent = down_project(first, part, acts, weights, (latest[0],))
    latest[:] = [out_own]
    step(mixed, low_heads, high_heads)
    input_grad = input_grad_of(dqkv, d_mixer, weights, d_hidden, inputs, (latest[0],))
    latest[:] = [input_grad]
    out_other = swap(tie(out_sent, step(mixed, low_heads)), "seq")
    output = add_output(hidden, out_own, out_other, (step(high_heads),))
    latest[:] = [output]
    step(mixed, low_heads, high_heads)
    ff_sum = tie(ff_sum, *latest)
    latest[:] = [ff_sum]
    while any(each.axes for each in (low_heads, high_heads, mixed)):
        for each in (mixed, low_heads, high_heads):
            if each.axes:
                step(each)
    low_sum, high_sum, mixed_sum = (each.total(0, each.rows) for each in (low_heads, high_heads, mixed))

    def both_planes(values):
        other = swap(values, "seq")
        mine = on_first[: values.shape[0], :1] > 0.5
        low = jnp.where(mine, values, other).astype(F32)
        high = jnp.where(mine, other, values).astype(F32)
        return low, high

    low, high = both_planes(ff_sum)
    grad_in = jnp.concatenate(
        [low[:, :part], high[:, :part], low[:, part : 2 * part], high[:, part : 2 * part]], 1
    )
    grad_down = jnp.concatenate([low[:, 2 * part :], high[:, 2 * part :]], 1)
    mix_total = jnp.concatenate(both_planes(mixed_sum), 0)
    sides = jnp.concatenate(both_planes(jnp.concatenate([low_sum, high_sum], 1)), 0)
    wide = width // 2
    grads = [
        jnp.concatenate([sides[:, i * wide : (i + 1) * wide], sides[:, (3 + i) * wide : (4 + i) * wide]], 1)
        for i in range(3)
    ]
    return (
        output[None],
        input_grad[None],
        *grads,
        mix_total[:, width:],
        mix_total[:, :width],
        grad_in,
        grad_down,
    )


def solution(mesh):
    planes, group = mesh.devices.shape
    devices = mesh.devices.reshape(planes, group // 2, 2)
    split = Mesh(devices, ("seq", "zy", "core"))
    rows = ("zy", "core")
    tok = P(rows, "seq", None)
    mat = P(rows, None)
    return jax.shard_map(
        on_device,
        mesh=split,
        in_specs=(tok,) + (mat,) * 8 + (tok,),
        out_specs=(tok, tok) + (mat,) * 7,
        check_vma=False,
    )
```

```python
import functools

import jax
import jax.numpy as jnp
from jax import lax
from jax.experimental import pallas as pl
from jax.experimental.pallas import tpu as pltpu
from jax.sharding import Mesh
from jax.sharding import PartitionSpec as P

HEAD_DIM = 128
EPSILON = 1e-06
FAR = 1e9
F32 = jnp.float32
BF16 = jnp.bfloat16


def dot(left, right):
    return jnp.dot(left, right, preferred_element_type=F32)


def dot_nt(left, right):
    return lax.dot_general(left, right, (((1,), (1,)), ((), ())), preferred_element_type=F32)


def dot_tn(left, right):
    return lax.dot_general(left, right, (((0,), (0,)), ((), ())), preferred_element_type=F32)


def row_factor(values):
    return lax.rsqrt(jnp.mean(values * values, axis=-1, keepdims=True) + EPSILON)


def norm_back(values, factor, upstream):
    normed = values * factor
    return factor * (upstream - normed * jnp.mean(upstream * normed, axis=-1, keepdims=True))


def sds(shape, kind):
    return jax.ShapeDtypeStruct(shape, kind)


def full(shape):
    return pl.BlockSpec(shape, lambda *_: (0,) * len(shape))


def vmem():
    return pl.BlockSpec(memory_space=pltpu.VMEM)


def hbm():
    return pl.BlockSpec(memory_space=pltpu.HBM)


def fetch(w_ref, firsts, bufs, sem):
    copies = []
    for i, (first, buf) in enumerate(zip(firsts, bufs, strict=True)):
        copies.append(pltpu.make_async_copy(w_ref.at[:, first : first + buf.shape[1]], buf, sem.at[i]))
        copies[-1].start()
    return copies


def cost(micros):
    return pl.CostEstimate(flops=int(micros * 1.1e9), bytes_accessed=0, transcendentals=0)


def run(kernel, operands, in_specs, deps=(), scalars=0, grid=(1,), scratch=(), **options):
    given = len(operands)

    def body(*refs):
        kernel(*refs[:given], *refs[given + len(deps) :])

    return pl.pallas_call(
        body,
        grid_spec=pltpu.PrefetchScalarGridSpec(
            num_scalar_prefetch=scalars,
            grid=grid,
            in_specs=list(in_specs) + [pl.BlockSpec(memory_space=pl.ANY)] * len(deps),
            out_specs=options.pop("out_specs"),
            scratch_shapes=list(scratch),
        ),
        **options,
    )(*operands, *deps)


def room(mebibytes):
    return pltpu.CompilerParams(vmem_limit_bytes=mebibytes << 20)


def slope_of(head):
    return 0.25 * 2.0 ** (-0.5 * (head + 1))


def shard_kernel(plane_ref, *refs):
    out_ref = refs[-1]
    at = 0
    for ref in refs[:-1]:
        out_ref[:, at : at + ref.shape[1]] = ref[...]
        at += ref.shape[1]


def gather_shard(plane, part, mixer, w_in, w_down):
    rows = w_in.shape[0]
    planes = w_down.shape[1] // part
    wide = sum(w.shape[1] for w in mixer) + 3 * part
    return run(
        shard_kernel,
        (jnp.reshape(plane, (1,)), *mixer, w_in, w_in, w_down),
        scalars=1,
        in_specs=[pl.BlockSpec(w.shape, lambda i, p: (0, 0)) for w in mixer]
        + [
            pl.BlockSpec((rows, part), lambda i, p: (0, p[0])),
            pl.BlockSpec((rows, part), lambda i, p: (0, p[0] + planes)),
            pl.BlockSpec((rows, part), lambda i, p: (0, p[0])),
        ],
        out_specs=pl.BlockSpec((rows, wide), lambda i, p: (0, 0)),
        out_shape=sds((rows, wide), BF16),
        compiler_params=room(8),
        name="gather_shard",
    )


def swish_parts(pre):
    sig = jax.nn.sigmoid(pre)
    return (pre * sig).astype(BF16), (sig * (1.0 + pre * (1.0 - sig))).astype(BF16)


def kv_kernel(heads, normed_ref, w_ref, dist_ref, key_ref, slope_ref, value_ref, state_ref, wk, wv, sem):
    width = normed_ref.shape[1]
    copies = fetch(w_ref, (width, 2 * width), (wk, wv), sem)
    copies[0].wait()
    for low in range(0, width, 256):
        cols = slice(low, low + 256)
        key_ref[:, cols], slope_ref[:, cols] = swish_parts(dot(normed_ref[...], wk[:, cols]))
    copies[1].wait()
    for low in range(0, width, 256):
        cols = slice(low, low + 256)
        value_ref[:, cols] = dot(normed_ref[...], wv[:, cols]).astype(BF16)
    for head in range(heads):
        cols = slice(head * HEAD_DIM, (head + 1) * HEAD_DIM)
        weight = jnp.exp(-slope_of(head) * dist_ref[...])
        scaled = (key_ref[:, cols].astype(F32) * weight).astype(BF16)
        state_ref[cols, :] = dot_tn(scaled, value_ref[:, cols]).astype(BF16)


def project_kv(normed, weights, cut_dist, deps=()):
    rows, width = normed.shape
    heads = width // HEAD_DIM
    act = sds((rows, width), BF16)
    return run(
        functools.partial(kv_kernel, heads),
        (normed, weights, cut_dist),
        deps=deps,
        in_specs=[vmem(), hbm(), vmem()],
        out_specs=[vmem()] * 4,
        out_shape=[act, act, act, sds((width, HEAD_DIM), BF16)],
        scratch=[pltpu.VMEM((width, width), BF16)] * 2 + [pltpu.SemaphoreType.DMA((2,))],
        cost_estimate=cost(0.2),
        compiler_params=room(12),
        name="project_kv",
    )


def qu_kernel(normed_ref, w_ref, query_ref, slope_ref, gate_ref, wq, wu, sem):
    width = normed_ref.shape[1]
    copies = fetch(w_ref, (0, 3 * width), (wq, wu), sem)
    copies[0].wait()
    for low in range(0, width, 256):
        cols = slice(low, low + 256)
        query_ref[:, cols], slope_ref[:, cols] = swish_parts(dot(normed_ref[...], wq[:, cols]))
    copies[1].wait()
    for low in range(0, width, 256):
        cols = slice(low, low + 256)
        gate_ref[:, cols] = dot(normed_ref[...], wu[:, cols]).astype(BF16)


def project_qu(normed, weights):
    rows, width = normed.shape
    act = sds((rows, width), BF16)
    return run(
        qu_kernel,
        (normed, weights),
        in_specs=[vmem(), hbm()],
        out_specs=[vmem()] * 3,
        out_shape=[act, act, act],
        scratch=[pltpu.VMEM((width, width), BF16)] * 2 + [pltpu.SemaphoreType.DMA((2,))],
        cost_estimate=cost(0.2),
        compiler_params=room(12),
        name="project_qu",
    )


def distance_tables(seg_col, seg_row, dist_ref):
    rows = seg_col.shape[0]
    span = lax.broadcasted_iota(jnp.int32, (rows, rows), 0) - lax.broadcasted_iota(
        jnp.int32, (rows, rows), 1
    )
    allowed = (span >= 0) & (seg_col == seg_row)
    dist_ref[...] = jnp.where(allowed, span.astype(F32), FAR)


def attend_kernel(heads, q_ref, k_ref, v_ref, col_ref, row_ref, out_ref, dist_ref):
    distance_tables(col_ref[...], row_ref[...], dist_ref)
    rows = q_ref.shape[0]
    half = rows // 2
    for head in range(heads):
        cols = slice(head * HEAD_DIM, (head + 1) * HEAD_DIM)
        for block in range(2):
            low, high = block * half, (block + 1) * half
            decay = jnp.exp(-slope_of(head) * dist_ref[low:high, :high])
            scores = (dot_nt(q_ref[low:high, cols], k_ref[:high, cols]) * decay).astype(BF16)
            out_ref[low:high, cols] = dot(scores, v_ref[:high, cols])


def attend_local(query, key, value, seg_col, seg_row):
    rows, width = query.shape
    return run(
        functools.partial(attend_kernel, width // HEAD_DIM),
        (query, key, value, seg_col, seg_row),
        in_specs=[vmem()] * 5,
        out_specs=vmem(),
        out_shape=sds((rows, width), F32),
        scratch=[pltpu.VMEM((rows, rows), F32)],
        cost_estimate=cost(0.2),
        compiler_params=room(10),
        name="attend_local",
    )


def mix_kernel(heads, att_ref, q_ref, u_ref, x_ref, state_ref, dist_ref, w_ref, att_out, gated_out, hidden_out, normed_out, top_out, bottom_out, wo, sem):
    width = q_ref.shape[1]
    rows = q_ref.shape[0]
    copies = fetch(w_ref, (4 * width,), (wo,), sem)
    for head in range(heads):
        cols = slice(head * HEAD_DIM, (head + 1) * HEAD_DIM)
        weight = jnp.exp(-slope_of(head) * dist_ref[...])
        scaled = (q_ref[:, cols].astype(F32) * weight).astype(BF16)
        att_out[:, cols] = (att_ref[:, cols] + dot(scaled, state_ref[cols, :])).astype(BF16)
    copies[0].wait()
    for low in range(0, rows, 256):
        part = slice(low, low + 256)
        attended = att_out[part, :].astype(F32)
        gated = (attended * row_factor(attended) * u_ref[part, :].astype(F32)).astype(BF16)
        gated_out[part, :] = gated
        hidden = x_ref[part, :].astype(F32) + dot(gated, wo[...])
        hidden_out[part, :] = hidden
        normed = (hidden * row_factor(hidden)).astype(BF16)
        normed_out[part, :] = normed
        half_out, at = (top_out, low) if 2 * low < rows else (bottom_out, low - rows // 2)
        half_out[at : at + 256, :] = normed


def mix_out(att, query, gate, tokens, state, cut_dist, weights):
    rows, width = query.shape
    return run(
        functools.partial(mix_kernel, width // HEAD_DIM),
        (att, query, gate, tokens, state, cut_dist, weights),
        in_specs=[vmem()] * 6 + [hbm()],
        out_specs=[vmem()] * 6,
        out_shape=[sds((rows, width), kind) for kind in (BF16, BF16, F32, BF16)]
        + [sds((rows // 2, width), BF16)] * 2,
        scratch=[pltpu.VMEM((width, width), BF16), pltpu.SemaphoreType.DMA((1,))],
        cost_estimate=cost(0.2),
        compiler_params=room(12),
        name="mix_out",
    )


def ff_kernel(grad_first, copies, normed_ref, grad_ref, wg, wu, wd, acts_ref, back_ref):
    part = wg.shape[1]
    rows, width = normed_ref.shape
    for block, low in enumerate(range(0, part, 256)):
        cols = slice(low, min(low + 256, part))
        for copy in copies[3 * block : 3 * block + 3]:
            copy.wait()
        gate = dot(normed_ref[...], wg[:, cols])
        up = dot(normed_ref[...], wu[:, cols])
        d_hidden = dot(grad_ref[grad_first : grad_first + rows, :], wd[:, cols])
        for which, value in enumerate((d_hidden * up, d_hidden * gate, gate * up)):
            acts_ref[:, which * part + cols.start : which * part + cols.stop] = value.astype(BF16)
    for low in range(0, width, 256):
        block = slice(low, low + 256)
        back = dot_nt(acts_ref[:, :part], wg[block, :]) + dot_nt(acts_ref[:, part : 2 * part], wu[block, :])
        back_ref[:, block] = back.astype(back_ref.dtype)


def first_ff_kernel(first, normed_ref, grad_ref, w_ref, acts_ref, back_ref, wg, wu, wd, sem):
    part = wg.shape[1]
    copies = []
    for low in range(0, part, 256):
        high = min(low + 256, part)
        for which, buf in enumerate((wg, wu, wd)):
            source = slice(first + which * part + low, first + which * part + high)
            copies.append(
                pltpu.make_async_copy(w_ref.at[:, source], buf.at[:, low:high], sem.at[len(copies)])
            )
            copies[-1].start()
    ff_kernel(0, copies, normed_ref, grad_ref, wg, wu, wd, acts_ref, back_ref)


def feed_forward(first, part, normed, grad, weights):
    rows, width = normed.shape
    acts, back, *fetched = run(
        functools.partial(first_ff_kernel, first),
        (normed, grad, weights),
        in_specs=[vmem(), vmem(), hbm()],
        out_specs=[vmem()] * 5,
        out_shape=[sds((rows, 3 * part), BF16), sds((rows, width), F32)] + [sds((width, part), BF16)] * 3,
        scratch=[pltpu.SemaphoreType.DMA((3 * -(-part // 256),))],
        cost_estimate=cost(0.2),
        compiler_params=room(22),
        name="feed_forward",
    )
    return acts, back, fetched


def feed_forward_more(normed, grad_first, grad, fetched, deps=()):
    rows, width = normed.shape
    part = fetched[0].shape[1]
    return run(
        functools.partial(ff_kernel, grad_first, ()),
        (normed, grad, *fetched),
        deps=deps,
        in_specs=[vmem()] * 5,
        out_specs=[vmem()] * 2,
        out_shape=[sds((rows, 3 * part), BF16), sds((rows, width), BF16)],
        cost_estimate=cost(0.2),
        compiler_params=room(22),
        name="feed_forward_more",
    )


def down_kernel(first, own_acts, other_acts, w_ref, own_ref, other_ref, wd, sem):
    part = wd.shape[1]
    width = own_ref.shape[1]
    copies = fetch(w_ref, (first + 2 * part,), (wd,), sem)
    copies[0].wait()
    for low in range(0, width, 256):
        block = slice(low, low + 256)
        own_ref[:, block] = dot_nt(own_acts[:, 2 * part :], wd[block, :])
        other_ref[:, block] = dot_nt(other_acts[:, 2 * part :], wd[block, :]).astype(BF16)


def down_project(first, part, own_acts, other_acts, weights, deps=()):
    width = weights.shape[0]
    return run(
        functools.partial(down_kernel, first),
        (own_acts, other_acts, weights),
        deps=deps,
        in_specs=[vmem()] * 2 + [hbm()],
        out_specs=[vmem()] * 2,
        out_shape=[sds((own_acts.shape[0], width), F32), sds((other_acts.shape[0], width), BF16)],
        scratch=[pltpu.VMEM((width, part), BF16), pltpu.SemaphoreType.DMA((1,))],
        cost_estimate=cost(0.2),
        compiler_params=room(12),
        name="down_project",
    )


def down_more_kernel(acts_ref, wd, out_ref):
    part = wd.shape[1]
    for low in range(0, out_ref.shape[1], 256):
        block = slice(low, low + 256)
        out_ref[:, block] = dot_nt(acts_ref[:, 2 * part :], wd[block, :]).astype(BF16)


def down_more(acts, wd):
    return run(
        down_more_kernel,
        (acts, wd),
        in_specs=[vmem()] * 2,
        out_specs=vmem(),
        out_shape=sds((acts.shape[0], wd.shape[0]), BF16),
        cost_estimate=cost(0.2),
        compiler_params=room(12),
        name="down_more",
    )


def add_kernel(hidden_ref, own_ref, top_ref, bottom_ref, out_ref):
    half = top_ref.shape[0]
    for rows, other in ((slice(0, half), top_ref), (slice(half, 2 * half), bottom_ref)):
        out_ref[rows, :] = (hidden_ref[rows, :] + own_ref[rows, :] + other[...].astype(F32)).astype(BF16)


def add_output(hidden, own, top, bottom, deps):
    return run(
        add_kernel,
        (hidden, own, top, bottom),
        deps=deps,
        in_specs=[vmem()] * 4,
        out_specs=vmem(),
        out_shape=sds(hidden.shape, BF16),
        cost_estimate=cost(1),
        compiler_params=room(8),
        name="add_output",
    )


def fold_kernel(kept_ref, late_ref, soon_ref, out_ref):
    half = late_ref.shape[0]
    out_ref[:half, :] = (kept_ref[:half, :].astype(F32) + late_ref[...].astype(F32)).astype(BF16)
    out_ref[half:, :] = (kept_ref[half:, :].astype(F32) + soon_ref[...].astype(F32)).astype(BF16)


def fold(kept, late, soon, deps):
    return run(
        fold_kernel,
        (kept, late, soon),
        deps=deps,
        in_specs=[vmem()] * 3,
        out_specs=vmem(),
        out_shape=sds(kept.shape, BF16),
        cost_estimate=cost(0.2),
        compiler_params=room(8),
        name="fold",
    )


def unmix_kernel(heads, hidden_ref, own_ref, top_ref, bottom_ref, grad_ref, u_ref, att_ref, q_ref, dist_ref, w_ref, d_hidden_out, d_mixer_out, d_att_out, state_out, wo, sem):
    rows, width = q_ref.shape
    copies = fetch(w_ref, (4 * width,), (wo,), sem)
    for low in range(0, rows, 256):
        part = slice(low, low + 256)
        hidden = hidden_ref[part, :]
        half_ref, at = (top_ref, low) if 2 * low < rows else (bottom_ref, low - rows // 2)
        upstream = own_ref[part, :] + half_ref[at : at + 256, :].astype(F32)
        d_hidden = grad_ref[part, :].astype(F32) + norm_back(hidden, row_factor(hidden), upstream)
        d_hidden_out[part, :] = d_hidden
        d_mixer_out[part, :width] = d_hidden.astype(BF16)
    copies[0].wait()
    for low in range(0, rows, 256):
        part = slice(low, low + 256)
        d_gated = dot_nt(d_mixer_out[part, :width], wo[...])
        attended = att_ref[part, :].astype(F32)
        factor = row_factor(attended)
        d_mixer_out[part, width:] = (d_gated * (attended * factor)).astype(BF16)
        d_att_out[part, :] = norm_back(attended, factor, d_gated * u_ref[part, :].astype(F32)).astype(BF16)
    for head in range(heads):
        cols = slice(head * HEAD_DIM, (head + 1) * HEAD_DIM)
        weight = jnp.exp(-slope_of(head) * dist_ref[...])
        scaled = (q_ref[:, cols].astype(F32) * weight).astype(BF16)
        state_out[cols, :] = dot_tn(scaled, d_att_out[:, cols]).astype(BF16)


def unmix(hidden, back_own, back_top, back_bottom, grad, gate, attended, query, cut_dist, weights, deps=()):
    rows, width = query.shape
    return run(
        functools.partial(unmix_kernel, width // HEAD_DIM),
        (hidden, back_own, back_top, back_bottom, grad, gate, attended, query, cut_dist, weights),
        deps=deps,
        in_specs=[vmem()] * 9 + [hbm()],
        out_specs=[vmem()] * 4,
        out_shape=[
            sds((rows, width), F32),
            sds((rows, 2 * width), BF16),
            sds((rows, width), BF16),
            sds((width, HEAD_DIM), BF16),
        ],
        scratch=[pltpu.VMEM((width, width), BF16), pltpu.SemaphoreType.DMA((1,))],
        cost_estimate=cost(60),
        compiler_params=room(14),
        name="unmix",
    )


def attend_back_kernel(heads, q_ref, k_ref, v_ref, d_ref, sq_ref, state_ref, cut_ref, col_ref, row_ref, dq_ref, dk_ref, dv_ref, dist_ref, turned_ref):
    rows = q_ref.shape[0]
    half = rows // 2
    distance_tables(col_ref[...], row_ref[...], dist_ref)
    turned_ref[...] = dist_ref[...].T
    for head in range(heads):
        cols = slice(head * HEAD_DIM, (head + 1) * HEAD_DIM)
        slope = slope_of(head)
        cut = jnp.exp(-slope * cut_ref[...])
        for block in range(2):
            low, high = block * half, (block + 1) * half
            decay = jnp.exp(-slope * dist_ref[low:high, :high])
            d_prod = (dot_nt(d_ref[low:high, cols], v_ref[:high, cols]) * decay).astype(BF16)
            d_query = dot(d_prod, k_ref[:high, cols])
            d_query += cut[low:high] * dot_nt(d_ref[low:high, cols], state_ref[cols, :])
            dq_ref[low:high, cols] = (d_query * sq_ref[low:high, cols].astype(F32)).astype(BF16)
        for block in range(2):
            low, high = block * half, (block + 1) * half
            decay = jnp.exp(-slope * turned_ref[low:high, low:])
            scores = (dot_nt(k_ref[low:high, cols], q_ref[low:, cols]) * decay).astype(BF16)
            dv_ref[low:high, cols] = dot(scores, d_ref[low:, cols])
            d_prod = (dot_nt(v_ref[low:high, cols], d_ref[low:, cols]) * decay).astype(BF16)
            dk_ref[low:high, cols] = dot(d_prod, q_ref[low:, cols])


def attend_back(query, key, value, d_att, q_slope, state, cut_dist, seg_col, seg_row, deps=()):
    rows, width = query.shape
    return run(
        functools.partial(attend_back_kernel, width // HEAD_DIM),
        (query, key, value, d_att, q_slope, state, cut_dist, seg_col, seg_row),
        deps=deps,
        in_specs=[vmem()] * 9,
        out_specs=[vmem()] * 3,
        out_shape=[sds((rows, width), kind) for kind in (BF16, F32, F32)],
        scratch=[pltpu.VMEM((rows, rows), F32)] * 2,
        cost_estimate=cost(0.2),
        compiler_params=room(12),
        name="attend_back",
    )


def join_kernel(heads, dq_ref, dk_ref, dv_ref, k_ref, v_ref, sk_ref, state_ref, cut_ref, out_ref):
    for head in range(heads):
        cols = slice(head * HEAD_DIM, (head + 1) * HEAD_DIM)
        cut = jnp.exp(-slope_of(head) * cut_ref[...])
        group = heads // 2 * HEAD_DIM
        at = head // (heads // 2) * 3 * group + head % (heads // 2) * HEAD_DIM
        out_ref[:, at : at + HEAD_DIM] = dq_ref[:, cols]
        d_key = dk_ref[:, cols] + cut * dot_nt(v_ref[:, cols], state_ref[cols, :])
        out_ref[:, at + group : at + group + HEAD_DIM] = (d_key * sk_ref[:, cols].astype(F32)).astype(BF16)
        d_value = dv_ref[:, cols] + cut * dot(k_ref[:, cols], state_ref[cols, :])
        out_ref[:, at + 2 * group : at + 2 * group + HEAD_DIM] = d_value.astype(BF16)


def join_back(dq, dk, dv, key, value, k_slope, state, cut_dist, deps=()):
    rows, width = key.shape
    return run(
        functools.partial(join_kernel, width // HEAD_DIM),
        (dq, dk, dv, key, value, k_slope, state, cut_dist),
        deps=deps,
        in_specs=[vmem()] * 8,
        out_specs=vmem(),
        out_shape=sds((rows, 3 * width), BF16),
        cost_estimate=cost(0.2),
        compiler_params=room(8),
        name="join_back",
    )


def input_kernel(dqkv_ref, dmix_ref, w_ref, dh_ref, x_ref, out_ref, *refs):
    bufs, sem = refs[:4], refs[4]
    rows, width = x_ref.shape
    half = width // 2
    copies = fetch(w_ref, [i * width for i in range(4)], bufs, sem)
    for copy in copies:
        copy.wait()
    for low in range(0, rows, 256):
        part = slice(low, low + 256)
        total = dot_nt(dmix_ref[part, width:], bufs[3][...])
        for i in range(3):
            for side in range(2):
                at = side * 3 * half + i * half
                total += dot_nt(dqkv_ref[part, at : at + half], bufs[i][:, side * half : (side + 1) * half])
        inputs = x_ref[part, :].astype(F32)
        out_ref[part, :] = dh_ref[part, :] + norm_back(inputs, row_factor(inputs), total)


def input_grad_of(dqkv, d_mixer, weights, d_hidden, tokens, deps=()):
    rows, width = tokens.shape
    return run(
        input_kernel,
        (dqkv, d_mixer, weights, d_hidden, tokens),
        deps=deps,
        in_specs=[vmem(), vmem(), hbm(), vmem(), vmem()],
        out_specs=vmem(),
        out_shape=sds((rows, width), F32),
        scratch=[pltpu.VMEM((width, width), BF16)] * 4
        + [pltpu.SemaphoreType.DMA((4,))],
        cost_estimate=cost(0.2),
        compiler_params=room(18),
        name="input_grad",
    )


def grad_kernel(jobs, wide, first, table, *refs):
    late_ref, soon_ref, keep_ref, turned = refs[-4:]
    rights = refs[max(job[0] + job[1] for job in jobs) : -4]
    width = turned.shape[0]
    half = width // 2
    rows = width // table.shape[0]
    loaded = None
    for block, job in enumerate(jobs):
        if job != loaded:
            loaded = job
            start = 0
            for source in refs[job[0] : job[0] + job[1]]:
                tokens = source.shape[0]
                for at in range(0, width, 128):
                    flat = source[:, at : at + 128].T
                    for sub in range(128 // rows):
                        place = pl.multiple_of(table[at // rows + sub] * rows, rows)
                        turned[pl.ds(place, rows), start : start + tokens] = flat[sub * rows : (sub + 1) * rows]
                start += tokens
        def columns(cols, source):
            right = jnp.concatenate([ref[:, source] for ref in rights], 0)
            keep_ref[:, cols] = dot(turned[:half, :], right).astype(BF16)
            sent = dot(turned[half:, :], right).astype(BF16)
            late_ref[:, cols] = sent[: half // 2]
            soon_ref[:, cols] = sent[half // 2 :]

        if wide * len(jobs) <= 2048:
            for low in range(block * wide, (block + 1) * wide, 256):
                columns(slice(low, low + 256), slice(first + low, first + low + 256))
            continue

        def body(j, carry, block=block, columns=columns):
            low = pl.multiple_of(block * wide + j * 256, 128)
            columns(pl.ds(low, 256), pl.ds(pl.multiple_of(first + low, 128), 256))
            return carry

        lax.fori_loop(0, wide // 256, body, 0)
        if wide % 256:
            low, high = (block + 1) * wide - wide % 256, (block + 1) * wide
            columns(slice(low, high), slice(first + low, first + high))


def places_of(axes):
    bits = lax.axis_size("zy").bit_length() - 1
    natural = list(range(bits - 1, -1, -1)) + ["core"] + (["seq"] if "seq" in axes else [])
    leaving = list(axes) + [axis for axis in natural if axis not in axes]
    owner = jnp.arange(2 ** len(natural), dtype=jnp.int32)
    place = jnp.zeros_like(owner)
    for rank, axis in enumerate(leaving):
        bit = (owner >> (len(natural) - 1 - natural.index(axis))) & 1
        if axis in axes:
            bit = bit ^ place_on(axis)
        place = place + (bit << (len(leaving) - 1 - rank))
    return place


def weight_grads(place, stacks, jobs, rights, span=None, deps=()):
    tokens, columns = sum(right.shape[0] for right in rights), rights[0].shape[1]
    if span is not None:
        columns = span[1] - span[0]
    wide = columns // len(jobs)
    width = stacks[0].shape[1]
    return run(
        functools.partial(grad_kernel, jobs, wide, 0 if span is None else span[0]),
        (place, *stacks, *rights),
        scalars=1,
        deps=deps,
        in_specs=[vmem()] * (len(stacks) + len(rights)),
        out_specs=[vmem()] * 3,
        out_shape=[sds((width // parts, columns), BF16) for parts in (4, 4, 2)],
        scratch=[pltpu.VMEM((width, tokens), BF16)],
        cost_estimate=cost(0.2),
        compiler_params=room(14 if columns > 3 * width else 12),
        name="weight_grads",
    )


def place_on(axis):
    if isinstance(axis, int):
        return (lax.axis_index("zy") >> axis) & 1
    return lax.axis_index(axis)


def swap(values, axis):
    if isinstance(axis, int):
        size = lax.axis_size("zy")
        return lax.ppermute(values, "zy", [(i, i ^ (1 << axis)) for i in range(size)])
    return lax.ppermute(values, axis, [(i, i ^ 1) for i in range(lax.axis_size(axis))])


def tie(value, *earlier):
    return lax.optimization_barrier((value, *earlier))[0]


class RowSums:
    def __init__(self, axes, late, soon, kept):
        self.axes, self.kept, self.sent = list(axes), kept, (soon, late)
        self.rows = kept.shape[0]
        self.terms = None

    def take(self, *earlier):
        axis = self.axes.pop(0)
        if self.terms is None:
            soon, late = (swap(each, axis) for each in self.sent)
            self.rows //= 2
            soon = tie(soon, *earlier)
            self.terms = [self.kept, late]
            self.sent = (self.kept[self.rows :].astype(F32) + soon.astype(F32)).astype(BF16)
            return self.sent
        got = swap(self.sent, axis)
        self.terms.append(tie(got, *earlier) if earlier else got)
        if not self.axes:
            return self.total(0, self.rows)
        self.rows //= 2
        self.sent = self.total(self.rows, 2 * self.rows)
        return self.sent

    def total(self, low, high):
        return functools.reduce(jnp.add, [t[low:high].astype(F32) for t in self.terms]).astype(BF16)


def mixer_grads_kernel(plane_ref, low_ref, low_other, high_ref, high_other, mix_ref, mix_other, query_ref, key_ref, value_ref, gate_ref, out_ref):
    rows = low_ref.shape[0]
    width = query_ref.shape[1]
    wide = width // 2
    own, other = (low_ref, high_ref, mix_ref), (low_other, high_other, mix_other)
    for plane in range(2):

        @pl.when(plane_ref[0] == plane)
        def _(plane=plane):
            for place, (low, high, mix) in ((plane, own), (1 - plane, other)):
                here = slice(place * rows, (place + 1) * rows)
                for i, ref in enumerate((query_ref, key_ref, value_ref)):
                    ref[here, :wide] = low[:, i * wide : (i + 1) * wide].astype(F32)
                    ref[here, wide:] = high[:, i * wide : (i + 1) * wide].astype(F32)
                out_ref[here, :] = mix[:, :width].astype(F32)
                gate_ref[here, :] = mix[:, width:].astype(F32)


def mixer_grads(plane, sums, width, deps):
    rows = 2 * sums[0].shape[0]
    arrays = [each for own in sums for each in (own, swap(own, "seq"))]
    return run(
        mixer_grads_kernel,
        (plane, *arrays),
        deps=deps,
        scalars=1,
        in_specs=[full(array.shape) for array in arrays],
        out_specs=[full((rows, width))] * 5,
        out_shape=[sds((rows, width), F32)] * 5,
        cost_estimate=cost(0.2),
        compiler_params=room(8),
        name="mixer_grads",
    )


def ff_grads_kernel(plane_ref, own_ref, other_ref, in_ref, down_ref):
    part = own_ref.shape[1] // 3
    for plane in range(2):

        @pl.when(plane_ref[0] == plane)
        def _(plane=plane):
            for place, ref in ((plane, own_ref), (1 - plane, other_ref)):
                for which, out in enumerate((in_ref, in_ref, down_ref)):
                    at = (place if which == 2 else 2 * which + place) * part
                    out[:, at : at + part] = ref[:, which * part : (which + 1) * part].astype(F32)


def ff_grads(plane, own, other):
    rows, columns = own.shape
    part = columns // 3
    return run(
        ff_grads_kernel,
        (plane, own, other),
        scalars=1,
        in_specs=[full(own.shape)] * 2,
        out_specs=[full((rows, 4 * part)), full((rows, 2 * part))],
        out_shape=[sds((rows, 4 * part), F32), sds((rows, 2 * part), F32)],
        cost_estimate=cost(0.2),
        compiler_params=room(10),
        name="ff_grads",
    )


def on_device(tokens, segments, w_query, w_key, w_value, w_gate, w_out, w_sglu_in, w_sglu_down, cotangent):
    rows, width = tokens.shape[1:]
    heads = width // HEAD_DIM
    planes = lax.axis_size("seq")
    plane = lax.axis_index("seq")
    ff = w_sglu_down.shape[1]
    part = ff // planes
    inputs, grad_tok = tokens[0], cotangent[0]
    bits = lax.axis_size("zy").bit_length() - 1
    zy = [0] + list(range(bits - 1, 0, -1))

    segs = lax.dynamic_slice_in_dim(segments[0], plane * rows, rows)
    edge = segments[0, rows - 1]
    places = jnp.arange(rows, dtype=jnp.int32)
    same = segs == edge
    from_cut = jnp.where(same, (places + 1).astype(F32), FAR)[:, None]
    to_cut = jnp.where(same, (rows - 1 - places).astype(F32), FAR)[:, None]
    seg_col, seg_row = segs[:, None], segs[None, :]

    shard = gather_shard(plane, part, (w_query, w_key, w_value, w_gate, w_out), w_sglu_in, w_sglu_down)
    weights = pltpu.with_memory_space_constraint(
        lax.all_gather(shard, ("zy", "core"), axis=0, tiled=True), pltpu.HBM
    )
    first = 5 * width

    low_axes = ["core", "seq"] + zy
    high_axes = low_axes
    ff_places, low_places, high_places = (places_of(axes) for axes in (["core"], low_axes, high_axes))

    grad_other = swap(grad_tok, "seq")
    x32 = inputs.astype(F32)
    normed_in = (x32 * row_factor(x32)).astype(BF16)

    key, k_slope, value, state = project_kv(
        normed_in, weights, to_cut, (grad_other, ff_places, low_places, high_places)
    )
    state = lax.ppermute(state, "seq", [(i, i + 1) for i in range(planes - 1)])
    query, q_slope, gate = project_qu(normed_in, weights)
    att = attend_local(query, key, value, seg_col, seg_row)
    attended, gated, hidden, normed, *sides = mix_out(
        att, query, gate, inputs, state, from_cut, weights
    )

    top, bottom = (swap(side, "seq") for side in sides)
    half = rows // 2
    own_acts, back_own, fetched = feed_forward(first, part, normed, grad_tok, weights)
    top_acts, back_top = feed_forward_more(top, 0, grad_other, fetched, (back_own,))
    back_top = swap(back_top, "seq")
    out_top = down_more(top_acts, fetched[2])
    bottom_acts, back_bottom = feed_forward_more(bottom, half, grad_other, fetched, (out_top,))
    back_bottom = swap(back_bottom, "seq")
    acts = (own_acts, top_acts, bottom_acts)

    late_ff, soon_ff, kept_ff = weight_grads(
        ff_places,
        (normed, top, bottom, grad_tok, grad_other),
        [(0, 3), (0, 3), (3, 2)],
        acts,
    )
    out_top = swap(tie(out_top, soon_ff), "seq")
    d_hidden, d_mixer, d_att, back_state = unmix(
        hidden, back_own, back_top, back_bottom, grad_tok, gate, attended, query, from_cut, weights, (soon_ff,)
    )
    back_state = lax.ppermute(back_state, "seq", [(i + 1, i) for i in range(planes - 1)])
    soon_ff, late_ff = (tie(swap(tie(each, back_top), "core"), d_mixer) for each in (soon_ff, late_ff))
    ff_part = fold(kept_ff, late_ff, soon_ff, (out_top,))
    ff_sum = lax.psum_scatter(ff_part, "zy", scatter_dimension=0, tiled=True)

    grads_mix = weight_grads(low_places, (gated, normed_in), [(0, 1), (1, 1)], (d_mixer,), None, (ff_part,))
    mixed = RowSums(low_axes, *grads_mix)
    latest = [grads_mix[0]]

    def step(*sums):
        for each in sums:
            latest[:] = [each.take(*latest)]
        return latest[0]

    dq, dk, dv = attend_back(
        query, key, value, d_att, q_slope, state, from_cut, seg_col, seg_row, (grads_mix[0],)
    )
    latest[:] = [dq, back_state]
    dqkv = join_back(dq, dk, dv, key, value, k_slope, back_state, to_cut, (step(mixed),))

    cut = heads // 2 * 3 * HEAD_DIM
    grads_low = weight_grads(low_places, (normed_in,), [(0, 1)], (dqkv,), (0, cut))
    low_heads = RowSums(low_axes, *grads_low)
    grads_high = weight_grads(high_places, (normed_in,), [(0, 1)], (dqkv,), (cut, 2 * cut), (grads_low[0],))
    high_heads = RowSums(high_axes, *grads_high)
    latest[:] = [grads_high[0]]
    out_own, out_bottom = down_project(first, part, own_acts, bottom_acts, weights, (latest[0],))
    latest[:] = [out_own]
    step(mixed, low_heads, high_heads)
    input_grad = input_grad_of(dqkv, d_mixer, weights, d_hidden, inputs, (latest[0],))
    latest[:] = [input_grad]
    out_bottom = swap(tie(out_bottom, step(mixed, low_heads, high_heads)), "seq")
    step(mixed, low_heads)
    output = add_output(hidden, out_own, out_top, out_bottom, (step(high_heads),))
    latest[:] = [output]
    ff_sum = tie(ff_sum, *latest)
    latest[:] = [ff_sum]
    while any(each.axes for each in (low_heads, high_heads, mixed)):
        for each in (mixed, low_heads, high_heads):
            if each.axes:
                step(each)
    low_sum, high_sum, mixed_sum = (each.total(0, each.rows) for each in (low_heads, high_heads, mixed))

    which = jnp.reshape(plane, (1,))
    grad_in, grad_down = ff_grads(which, ff_sum, swap(ff_sum, "seq"))
    *grads, grad_gate, grad_out = mixer_grads(which, (low_sum, high_sum, mixed_sum), width, (grad_down,))
    return (
        output[None],
        input_grad[None],
        *grads,
        grad_gate,
        grad_out,
        grad_in,
        grad_down,
    )


def solution(mesh):
    planes, group = mesh.devices.shape
    devices = mesh.devices.reshape(planes, group // 2, 2)
    split = Mesh(devices, ("seq", "zy", "core"))
    rows = ("zy", "core")
    tok = P(rows, "seq", None)
    mat = P(rows, None)
    return jax.shard_map(
        on_device,
        mesh=split,
        in_specs=(tok,) + (mat,) * 8 + (tok,),
        out_specs=(tok, tok) + (mat,) * 7,
        check_vma=False,
    )
```

```python
import functools

import jax
import jax.numpy as jnp
from jax import lax
from jax.experimental import pallas as pl
from jax.experimental.pallas import tpu as pltpu
from jax.sharding import Mesh
from jax.sharding import PartitionSpec as P

HEAD_DIM = 128
EPSILON = 1e-06
FAR = 1e9
F32 = jnp.float32
BF16 = jnp.bfloat16


def dot(left, right):
    return jnp.dot(left, right, preferred_element_type=F32)


def dot_nt(left, right):
    return lax.dot_general(left, right, (((1,), (1,)), ((), ())), preferred_element_type=F32)


def dot_tn(left, right):
    return lax.dot_general(left, right, (((0,), (0,)), ((), ())), preferred_element_type=F32)


def row_factor(values):
    return lax.rsqrt(jnp.mean(values * values, axis=-1, keepdims=True) + EPSILON)


def norm_back(values, factor, upstream):
    normed = values * factor
    return factor * (upstream - normed * jnp.mean(upstream * normed, axis=-1, keepdims=True))


def sds(shape, kind):
    return jax.ShapeDtypeStruct(shape, kind)


def full(shape):
    return pl.BlockSpec(shape, lambda *_: (0,) * len(shape))


def vmem():
    return pl.BlockSpec(memory_space=pltpu.VMEM)


def hbm():
    return pl.BlockSpec(memory_space=pltpu.HBM)


def fetch(w_ref, firsts, bufs, sem):
    copies = []
    for i, (first, buf) in enumerate(zip(firsts, bufs, strict=True)):
        copies.append(pltpu.make_async_copy(w_ref.at[:, first : first + buf.shape[1]], buf, sem.at[i]))
        copies[-1].start()
    return copies


def cost(micros):
    return pl.CostEstimate(flops=int(micros * 1.1e9), bytes_accessed=0, transcendentals=0)


def run(kernel, operands, in_specs, deps=(), scalars=0, grid=(1,), scratch=(), **options):
    given = len(operands)

    def body(*refs):
        kernel(*refs[:given], *refs[given + len(deps) :])

    return pl.pallas_call(
        body,
        grid_spec=pltpu.PrefetchScalarGridSpec(
            num_scalar_prefetch=scalars,
            grid=grid,
            in_specs=list(in_specs) + [pl.BlockSpec(memory_space=pl.ANY)] * len(deps),
            out_specs=options.pop("out_specs"),
            scratch_shapes=list(scratch),
        ),
        **options,
    )(*operands, *deps)


def room(mebibytes):
    return pltpu.CompilerParams(vmem_limit_bytes=mebibytes << 20)


def slope_of(head):
    return 0.25 * 2.0 ** (-0.5 * (head + 1))


def shard_kernel(plane_ref, *refs):
    out_ref = refs[-1]
    at = 0
    for ref in refs[:-1]:
        out_ref[:, at : at + ref.shape[1]] = ref[...]
        at += ref.shape[1]


def gather_shard(plane, part, mixer, w_in, w_down):
    rows = w_in.shape[0]
    planes = w_down.shape[1] // part
    wide = sum(w.shape[1] for w in mixer) + 3 * part
    return run(
        shard_kernel,
        (jnp.reshape(plane, (1,)), *mixer, w_in, w_in, w_down),
        scalars=1,
        in_specs=[pl.BlockSpec(w.shape, lambda i, p: (0, 0)) for w in mixer]
        + [
            pl.BlockSpec((rows, part), lambda i, p: (0, p[0])),
            pl.BlockSpec((rows, part), lambda i, p: (0, p[0] + planes)),
            pl.BlockSpec((rows, part), lambda i, p: (0, p[0])),
        ],
        out_specs=pl.BlockSpec((rows, wide), lambda i, p: (0, 0)),
        out_shape=sds((rows, wide), BF16),
        compiler_params=room(8),
        name="gather_shard",
    )


def swish_parts(pre):
    sig = jax.nn.sigmoid(pre)
    return (pre * sig).astype(BF16), (sig * (1.0 + pre * (1.0 - sig))).astype(BF16)


def kv_kernel(heads, normed_ref, w_ref, dist_ref, key_ref, slope_ref, value_ref, state_ref, wk, wv, sem):
    width = normed_ref.shape[1]
    copies = fetch(w_ref, (width, 2 * width), (wk, wv), sem)
    copies[0].wait()
    for low in range(0, width, 256):
        cols = slice(low, low + 256)
        key_ref[:, cols], slope_ref[:, cols] = swish_parts(dot(normed_ref[...], wk[:, cols]))
    copies[1].wait()
    for low in range(0, width, 256):
        cols = slice(low, low + 256)
        value_ref[:, cols] = dot(normed_ref[...], wv[:, cols]).astype(BF16)
    for head in range(heads):
        cols = slice(head * HEAD_DIM, (head + 1) * HEAD_DIM)
        weight = jnp.exp(-slope_of(head) * dist_ref[...])
        scaled = (key_ref[:, cols].astype(F32) * weight).astype(BF16)
        state_ref[cols, :] = dot_tn(scaled, value_ref[:, cols]).astype(BF16)


def project_kv(normed, weights, cut_dist, deps=()):
    rows, width = normed.shape
    heads = width // HEAD_DIM
    act = sds((rows, width), BF16)
    return run(
        functools.partial(kv_kernel, heads),
        (normed, weights, cut_dist),
        deps=deps,
        in_specs=[vmem(), hbm(), vmem()],
        out_specs=[vmem()] * 4,
        out_shape=[act, act, act, sds((width, HEAD_DIM), BF16)],
        scratch=[pltpu.VMEM((width, width), BF16)] * 2 + [pltpu.SemaphoreType.DMA((2,))],
        cost_estimate=cost(0.2),
        compiler_params=room(12),
        name="project_kv",
    )


def qu_kernel(normed_ref, w_ref, query_ref, slope_ref, gate_ref, wq, wu, sem):
    width = normed_ref.shape[1]
    copies = fetch(w_ref, (0, 3 * width), (wq, wu), sem)
    copies[0].wait()
    for low in range(0, width, 256):
        cols = slice(low, low + 256)
        query_ref[:, cols], slope_ref[:, cols] = swish_parts(dot(normed_ref[...], wq[:, cols]))
    copies[1].wait()
    for low in range(0, width, 256):
        cols = slice(low, low + 256)
        gate_ref[:, cols] = dot(normed_ref[...], wu[:, cols]).astype(BF16)


def project_qu(normed, weights):
    rows, width = normed.shape
    act = sds((rows, width), BF16)
    return run(
        qu_kernel,
        (normed, weights),
        in_specs=[vmem(), hbm()],
        out_specs=[vmem()] * 3,
        out_shape=[act, act, act],
        scratch=[pltpu.VMEM((width, width), BF16)] * 2 + [pltpu.SemaphoreType.DMA((2,))],
        cost_estimate=cost(0.2),
        compiler_params=room(12),
        name="project_qu",
    )


def distance_tables(seg_col, seg_row, dist_ref):
    rows = seg_col.shape[0]
    span = lax.broadcasted_iota(jnp.int32, (rows, rows), 0) - lax.broadcasted_iota(
        jnp.int32, (rows, rows), 1
    )
    allowed = (span >= 0) & (seg_col == seg_row)
    dist_ref[...] = jnp.where(allowed, span.astype(F32), FAR)


def attend_kernel(heads, first, q_ref, k_ref, v_ref, col_ref, row_ref, w_ref, out_ref, ahead, dist_ref, sem):
    copies = fetch(w_ref, (first,), (ahead,), sem)
    distance_tables(col_ref[...], row_ref[...], dist_ref)
    rows = q_ref.shape[0]
    half = rows // 2
    for head in range(heads):
        cols = slice(head * HEAD_DIM, (head + 1) * HEAD_DIM)
        for block in range(2):
            low, high = block * half, (block + 1) * half
            decay = jnp.exp(-slope_of(head) * dist_ref[low:high, :high])
            scores = (dot_nt(q_ref[low:high, cols], k_ref[:high, cols]) * decay).astype(BF16)
            out_ref[low:high, cols] = dot(scores, v_ref[:high, cols])
    copies[0].wait()


def attend_local(query, key, value, seg_col, seg_row, weights, first, part):
    rows, width = query.shape
    return run(
        functools.partial(attend_kernel, width // HEAD_DIM, first),
        (query, key, value, seg_col, seg_row, weights),
        in_specs=[vmem()] * 5 + [hbm()],
        out_specs=[vmem()] * 2,
        out_shape=[sds((rows, width), F32), sds((width, part), BF16)],
        scratch=[pltpu.VMEM((rows, rows), F32), pltpu.SemaphoreType.DMA((1,))],
        cost_estimate=cost(0.2),
        compiler_params=room(10),
        name="attend_local",
    )


def mix_kernel(heads, first, att_ref, q_ref, u_ref, x_ref, state_ref, dist_ref, w_ref, att_out, gated_out, hidden_out, normed_out, top_out, bottom_out, ahead, wo, sem):
    width = q_ref.shape[1]
    rows = q_ref.shape[0]
    copies = fetch(w_ref, (4 * width, first), (wo, ahead), sem)
    for head in range(heads):
        cols = slice(head * HEAD_DIM, (head + 1) * HEAD_DIM)
        weight = jnp.exp(-slope_of(head) * dist_ref[...])
        scaled = (q_ref[:, cols].astype(F32) * weight).astype(BF16)
        att_out[:, cols] = (att_ref[:, cols] + dot(scaled, state_ref[cols, :])).astype(BF16)
    copies[0].wait()
    for low in range(0, rows, 256):
        part = slice(low, low + 256)
        attended = att_out[part, :].astype(F32)
        gated = (attended * row_factor(attended) * u_ref[part, :].astype(F32)).astype(BF16)
        gated_out[part, :] = gated
        hidden = x_ref[part, :].astype(F32) + dot(gated, wo[...])
        hidden_out[part, :] = hidden
        normed = (hidden * row_factor(hidden)).astype(BF16)
        normed_out[part, :] = normed
        half_out, at = (top_out, low) if 2 * low < rows else (bottom_out, low - rows // 2)
        half_out[at : at + 256, :] = normed
    copies[1].wait()


def mix_top_kernel(heads, first, att_ref, q_ref, u_ref, x_ref, state_ref, dist_ref, w_ref, normed_out, ahead, att, wo, sem):
    width = q_ref.shape[1]
    rows = normed_out.shape[0]
    copies = fetch(w_ref, (4 * width, first), (wo, ahead), sem)
    for head in range(heads):
        cols = slice(head * HEAD_DIM, (head + 1) * HEAD_DIM)
        weight = jnp.exp(-slope_of(head) * dist_ref[:rows, :])
        scaled = (q_ref[:rows, cols].astype(F32) * weight).astype(BF16)
        att[:, cols] = (att_ref[:rows, cols] + dot(scaled, state_ref[cols, :])).astype(BF16)
    copies[0].wait()
    attended = att[...].astype(F32)
    gated = (attended * row_factor(attended) * u_ref[:rows, :].astype(F32)).astype(BF16)
    hidden = x_ref[:rows, :].astype(F32) + dot(gated, wo[...])
    normed_out[...] = (hidden * row_factor(hidden)).astype(BF16)
    copies[1].wait()


def mix_top(att, query, gate, tokens, state, cut_dist, weights, first, part):
    rows, width = query.shape
    return run(
        functools.partial(mix_top_kernel, width // HEAD_DIM, first),
        (att, query, gate, tokens, state, cut_dist, weights),
        in_specs=[vmem()] * 6 + [hbm()],
        out_specs=[vmem()] * 2,
        out_shape=[sds((rows // 2, width), BF16), sds((width, part), BF16)],
        scratch=[
            pltpu.VMEM((rows // 2, width), BF16),
            pltpu.VMEM((width, width), BF16),
            pltpu.SemaphoreType.DMA((2,)),
        ],
        cost_estimate=cost(0.2),
        compiler_params=room(12),
        name="mix_top",
    )


def mix_out(att, query, gate, tokens, state, cut_dist, weights, first, part, deps):
    rows, width = query.shape
    return run(
        functools.partial(mix_kernel, width // HEAD_DIM, first),
        (att, query, gate, tokens, state, cut_dist, weights),
        deps=deps,
        in_specs=[vmem()] * 6 + [hbm()],
        out_specs=[vmem()] * 7,
        out_shape=[sds((rows, width), kind) for kind in (BF16, BF16, F32, BF16)]
        + [sds((rows // 2, width), BF16)] * 2
        + [sds((width, part), BF16)],
        scratch=[pltpu.VMEM((width, width), BF16), pltpu.SemaphoreType.DMA((2,))],
        cost_estimate=cost(0.2),
        compiler_params=room(12),
        name="mix_out",
    )


def ff_kernel(grad_first, normed_ref, grad_ref, wg, wu, wd, acts_ref, back_ref):
    part = wg.shape[1]
    rows, width = normed_ref.shape
    for low in range(0, part, 256):
        cols = slice(low, min(low + 256, part))
        gate = dot(normed_ref[...], wg[:, cols])
        up = dot(normed_ref[...], wu[:, cols])
        d_hidden = dot(grad_ref[grad_first : grad_first + rows, :], wd[:, cols])
        for which, value in enumerate((d_hidden * up, d_hidden * gate, gate * up)):
            acts_ref[:, which * part + cols.start : which * part + cols.stop] = value.astype(BF16)
    for low in range(0, width, 256):
        block = slice(low, low + 256)
        back = dot_nt(acts_ref[:, :part], wg[block, :]) + dot_nt(acts_ref[:, part : 2 * part], wu[block, :])
        back_ref[:, block] = back.astype(back_ref.dtype)


def feed_forward(kind, normed, grad_first, grad, fetched, deps=()):
    rows, width = normed.shape
    part = fetched[0].shape[1]
    return run(
        functools.partial(ff_kernel, grad_first),
        (normed, grad, *fetched),
        deps=deps,
        in_specs=[vmem()] * 5,
        out_specs=[vmem()] * 2,
        out_shape=[sds((rows, 3 * part), BF16), sds((rows, width), kind)],
        cost_estimate=cost(0.2),
        compiler_params=room(22),
        name="feed_forward",
    )


def down_kernel(first, own_acts, other_acts, w_ref, own_ref, other_ref, wd, sem):
    part = wd.shape[1]
    width = own_ref.shape[1]
    copies = fetch(w_ref, (first + 2 * part,), (wd,), sem)
    copies[0].wait()
    for low in range(0, width, 256):
        block = slice(low, low + 256)
        own_ref[:, block] = dot_nt(own_acts[:, 2 * part :], wd[block, :])
        other_ref[:, block] = dot_nt(other_acts[:, 2 * part :], wd[block, :]).astype(BF16)


def down_project(first, part, own_acts, other_acts, weights, deps=()):
    width = weights.shape[0]
    return run(
        functools.partial(down_kernel, first),
        (own_acts, other_acts, weights),
        deps=deps,
        in_specs=[vmem()] * 2 + [hbm()],
        out_specs=[vmem()] * 2,
        out_shape=[sds((own_acts.shape[0], width), F32), sds((other_acts.shape[0], width), BF16)],
        scratch=[pltpu.VMEM((width, part), BF16), pltpu.SemaphoreType.DMA((1,))],
        cost_estimate=cost(0.2),
        compiler_params=room(12),
        name="down_project",
    )


def down_more_kernel(acts_ref, wd, out_ref):
    part = wd.shape[1]
    for low in range(0, out_ref.shape[1], 256):
        block = slice(low, low + 256)
        out_ref[:, block] = dot_nt(acts_ref[:, 2 * part :], wd[block, :]).astype(BF16)


def down_more(acts, wd):
    return run(
        down_more_kernel,
        (acts, wd),
        in_specs=[vmem()] * 2,
        out_specs=vmem(),
        out_shape=sds((acts.shape[0], wd.shape[0]), BF16),
        cost_estimate=cost(0.2),
        compiler_params=room(12),
        name="down_more",
    )


def add_kernel(hidden_ref, own_ref, top_ref, bottom_ref, out_ref):
    half = top_ref.shape[0]
    for rows, other in ((slice(0, half), top_ref), (slice(half, 2 * half), bottom_ref)):
        out_ref[rows, :] = (hidden_ref[rows, :] + own_ref[rows, :] + other[...].astype(F32)).astype(BF16)


def add_output(hidden, own, top, bottom, deps):
    return run(
        add_kernel,
        (hidden, own, top, bottom),
        deps=deps,
        in_specs=[vmem()] * 4,
        out_specs=vmem(),
        out_shape=sds(hidden.shape, BF16),
        cost_estimate=cost(1),
        compiler_params=room(8),
        name="add_output",
    )


def fold_kernel(kept_ref, late_ref, soon_ref, out_ref):
    half = late_ref.shape[0]
    out_ref[:half, :] = (kept_ref[:half, :].astype(F32) + late_ref[...].astype(F32)).astype(BF16)
    out_ref[half:, :] = (kept_ref[half:, :].astype(F32) + soon_ref[...].astype(F32)).astype(BF16)


def fold(kept, late, soon, deps):
    return run(
        fold_kernel,
        (kept, late, soon),
        deps=deps,
        in_specs=[vmem()] * 3,
        out_specs=vmem(),
        out_shape=sds(kept.shape, BF16),
        cost_estimate=cost(0.2),
        compiler_params=room(8),
        name="fold",
    )


def unmix_kernel(heads, hidden_ref, own_ref, top_ref, bottom_ref, grad_ref, u_ref, att_ref, q_ref, dist_ref, w_ref, d_hidden_out, d_mixer_out, d_att_out, state_out, wo, sem):
    rows, width = q_ref.shape
    copies = fetch(w_ref, (4 * width,), (wo,), sem)
    for low in range(0, rows, 256):
        part = slice(low, low + 256)
        hidden = hidden_ref[part, :]
        half_ref, at = (top_ref, low) if 2 * low < rows else (bottom_ref, low - rows // 2)
        upstream = own_ref[part, :] + half_ref[at : at + 256, :].astype(F32)
        d_hidden = grad_ref[part, :].astype(F32) + norm_back(hidden, row_factor(hidden), upstream)
        d_hidden_out[part, :] = d_hidden
        d_mixer_out[part, :width] = d_hidden.astype(BF16)
    copies[0].wait()
    for low in range(0, rows, 256):
        part = slice(low, low + 256)
        d_gated = dot_nt(d_mixer_out[part, :width], wo[...])
        attended = att_ref[part, :].astype(F32)
        factor = row_factor(attended)
        d_mixer_out[part, width:] = (d_gated * (attended * factor)).astype(BF16)
        d_att_out[part, :] = norm_back(attended, factor, d_gated * u_ref[part, :].astype(F32)).astype(BF16)
    for head in range(heads):
        cols = slice(head * HEAD_DIM, (head + 1) * HEAD_DIM)
        weight = jnp.exp(-slope_of(head) * dist_ref[...])
        scaled = (q_ref[:, cols].astype(F32) * weight).astype(BF16)
        state_out[cols, :] = dot_tn(scaled, d_att_out[:, cols]).astype(BF16)


def unmix(hidden, back_own, back_top, back_bottom, grad, gate, attended, query, cut_dist, weights, deps=()):
    rows, width = query.shape
    return run(
        functools.partial(unmix_kernel, width // HEAD_DIM),
        (hidden, back_own, back_top, back_bottom, grad, gate, attended, query, cut_dist, weights),
        deps=deps,
        in_specs=[vmem()] * 9 + [hbm()],
        out_specs=[vmem()] * 4,
        out_shape=[
            sds((rows, width), F32),
            sds((rows, 2 * width), BF16),
            sds((rows, width), BF16),
            sds((width, HEAD_DIM), BF16),
        ],
        scratch=[pltpu.VMEM((width, width), BF16), pltpu.SemaphoreType.DMA((1,))],
        cost_estimate=cost(60),
        compiler_params=room(14),
        name="unmix",
    )


def attend_back_kernel(heads, q_ref, k_ref, v_ref, d_ref, sq_ref, state_ref, cut_ref, col_ref, row_ref, dq_ref, dk_ref, dv_ref, dist_ref, turned_ref):
    rows = q_ref.shape[0]
    half = rows // 2
    distance_tables(col_ref[...], row_ref[...], dist_ref)
    turned_ref[...] = dist_ref[...].T
    for head in range(heads):
        cols = slice(head * HEAD_DIM, (head + 1) * HEAD_DIM)
        slope = slope_of(head)
        cut = jnp.exp(-slope * cut_ref[...])
        for block in range(2):
            low, high = block * half, (block + 1) * half
            decay = jnp.exp(-slope * dist_ref[low:high, :high])
            d_prod = (dot_nt(d_ref[low:high, cols], v_ref[:high, cols]) * decay).astype(BF16)
            d_query = dot(d_prod, k_ref[:high, cols])
            d_query += cut[low:high] * dot_nt(d_ref[low:high, cols], state_ref[cols, :])
            dq_ref[low:high, cols] = (d_query * sq_ref[low:high, cols].astype(F32)).astype(BF16)
        for block in range(2):
            low, high = block * half, (block + 1) * half
            decay = jnp.exp(-slope * turned_ref[low:high, low:])
            scores = (dot_nt(k_ref[low:high, cols], q_ref[low:, cols]) * decay).astype(BF16)
            dv_ref[low:high, cols] = dot(scores, d_ref[low:, cols])
            d_prod = (dot_nt(v_ref[low:high, cols], d_ref[low:, cols]) * decay).astype(BF16)
            dk_ref[low:high, cols] = dot(d_prod, q_ref[low:, cols])


def attend_back(query, key, value, d_att, q_slope, state, cut_dist, seg_col, seg_row, deps=()):
    rows, width = query.shape
    return run(
        functools.partial(attend_back_kernel, width // HEAD_DIM),
        (query, key, value, d_att, q_slope, state, cut_dist, seg_col, seg_row),
        deps=deps,
        in_specs=[vmem()] * 9,
        out_specs=[vmem()] * 3,
        out_shape=[sds((rows, width), kind) for kind in (BF16, F32, F32)],
        scratch=[pltpu.VMEM((rows, rows), F32)] * 2,
        cost_estimate=cost(0.2),
        compiler_params=room(12),
        name="attend_back",
    )


def join_kernel(heads, dq_ref, dk_ref, dv_ref, k_ref, v_ref, sk_ref, state_ref, cut_ref, out_ref):
    for head in range(heads):
        cols = slice(head * HEAD_DIM, (head + 1) * HEAD_DIM)
        cut = jnp.exp(-slope_of(head) * cut_ref[...])
        group = heads // 2 * HEAD_DIM
        at = head // (heads // 2) * 3 * group + head % (heads // 2) * HEAD_DIM
        out_ref[:, at : at + HEAD_DIM] = dq_ref[:, cols]
        d_key = dk_ref[:, cols] + cut * dot_nt(v_ref[:, cols], state_ref[cols, :])
        out_ref[:, at + group : at + group + HEAD_DIM] = (d_key * sk_ref[:, cols].astype(F32)).astype(BF16)
        d_value = dv_ref[:, cols] + cut * dot(k_ref[:, cols], state_ref[cols, :])
        out_ref[:, at + 2 * group : at + 2 * group + HEAD_DIM] = d_value.astype(BF16)


def join_back(dq, dk, dv, key, value, k_slope, state, cut_dist, deps=()):
    rows, width = key.shape
    return run(
        functools.partial(join_kernel, width // HEAD_DIM),
        (dq, dk, dv, key, value, k_slope, state, cut_dist),
        deps=deps,
        in_specs=[vmem()] * 8,
        out_specs=vmem(),
        out_shape=sds((rows, 3 * width), BF16),
        cost_estimate=cost(0.2),
        compiler_params=room(8),
        name="join_back",
    )


def input_kernel(dqkv_ref, dmix_ref, w_ref, dh_ref, x_ref, out_ref, *refs):
    bufs, sem = refs[:4], refs[4]
    rows, width = x_ref.shape
    half = width // 2
    copies = fetch(w_ref, [i * width for i in range(4)], bufs, sem)
    for copy in copies:
        copy.wait()
    for low in range(0, rows, 256):
        part = slice(low, low + 256)
        total = dot_nt(dmix_ref[part, width:], bufs[3][...])
        for i in range(3):
            for side in range(2):
                at = side * 3 * half + i * half
                total += dot_nt(dqkv_ref[part, at : at + half], bufs[i][:, side * half : (side + 1) * half])
        inputs = x_ref[part, :].astype(F32)
        out_ref[part, :] = dh_ref[part, :] + norm_back(inputs, row_factor(inputs), total)


def input_grad_of(dqkv, d_mixer, weights, d_hidden, tokens, deps=()):
    rows, width = tokens.shape
    return run(
        input_kernel,
        (dqkv, d_mixer, weights, d_hidden, tokens),
        deps=deps,
        in_specs=[vmem(), vmem(), hbm(), vmem(), vmem()],
        out_specs=vmem(),
        out_shape=sds((rows, width), F32),
        scratch=[pltpu.VMEM((width, width), BF16)] * 4
        + [pltpu.SemaphoreType.DMA((4,))],
        cost_estimate=cost(0.2),
        compiler_params=room(18),
        name="input_grad",
    )


def grad_kernel(jobs, wide, first, table, *refs):
    late_ref, soon_ref, keep_ref, turned = refs[-4:]
    rights = refs[max(job[0] + job[1] for job in jobs) : -4]
    width = turned.shape[0]
    half = width // 2
    rows = width // table.shape[0]
    loaded = None
    for block, job in enumerate(jobs):
        if job != loaded:
            loaded = job
            start = 0
            for source in refs[job[0] : job[0] + job[1]]:
                tokens = source.shape[0]
                for at in range(0, width, 128):
                    flat = source[:, at : at + 128].T
                    for sub in range(128 // rows):
                        place = pl.multiple_of(table[at // rows + sub] * rows, rows)
                        turned[pl.ds(place, rows), start : start + tokens] = flat[sub * rows : (sub + 1) * rows]
                start += tokens
        def columns(cols, source):
            right = jnp.concatenate([ref[:, source] for ref in rights], 0)
            keep_ref[:, cols] = dot(turned[:half, :], right).astype(BF16)
            sent = dot(turned[half:, :], right).astype(BF16)
            late_ref[:, cols] = sent[: half // 2]
            soon_ref[:, cols] = sent[half // 2 :]

        if wide * len(jobs) <= 2048:
            for low in range(block * wide, (block + 1) * wide, 256):
                columns(slice(low, low + 256), slice(first + low, first + low + 256))
            continue

        def body(j, carry, block=block, columns=columns):
            low = pl.multiple_of(block * wide + j * 256, 128)
            columns(pl.ds(low, 256), pl.ds(pl.multiple_of(first + low, 128), 256))
            return carry

        lax.fori_loop(0, wide // 256, body, 0)
        if wide % 256:
            low, high = (block + 1) * wide - wide % 256, (block + 1) * wide
            columns(slice(low, high), slice(first + low, first + high))


def places_of(axes):
    bits = lax.axis_size("zy").bit_length() - 1
    natural = list(range(bits - 1, -1, -1)) + ["core"] + (["seq"] if "seq" in axes else [])
    leaving = list(axes) + [axis for axis in natural if axis not in axes]
    owner = jnp.arange(2 ** len(natural), dtype=jnp.int32)
    place = jnp.zeros_like(owner)
    for rank, axis in enumerate(leaving):
        bit = (owner >> (len(natural) - 1 - natural.index(axis))) & 1
        if axis in axes:
            bit = bit ^ place_on(axis)
        place = place + (bit << (len(leaving) - 1 - rank))
    return place


def weight_grads(place, stacks, jobs, rights, span=None, deps=()):
    tokens, columns = sum(right.shape[0] for right in rights), rights[0].shape[1]
    if span is not None:
        columns = span[1] - span[0]
    wide = columns // len(jobs)
    width = stacks[0].shape[1]
    return run(
        functools.partial(grad_kernel, jobs, wide, 0 if span is None else span[0]),
        (place, *stacks, *rights),
        scalars=1,
        deps=deps,
        in_specs=[vmem()] * (len(stacks) + len(rights)),
        out_specs=[vmem()] * 3,
        out_shape=[sds((width // parts, columns), BF16) for parts in (4, 4, 2)],
        scratch=[pltpu.VMEM((width, tokens), BF16)],
        cost_estimate=cost(0.2),
        compiler_params=room(14 if columns > 3 * width else 12),
        name="weight_grads",
    )


def place_on(axis):
    if isinstance(axis, int):
        return (lax.axis_index("zy") >> axis) & 1
    return lax.axis_index(axis)


def swap(values, axis):
    if isinstance(axis, int):
        size = lax.axis_size("zy")
        return lax.ppermute(values, "zy", [(i, i ^ (1 << axis)) for i in range(size)])
    return lax.ppermute(values, axis, [(i, i ^ 1) for i in range(lax.axis_size(axis))])


def tie(value, *earlier):
    return lax.optimization_barrier((value, *earlier))[0]


class RowSums:
    def __init__(self, axes, late, soon, kept):
        self.axes, self.kept, self.sent = list(axes), kept, (soon, late)
        self.rows = kept.shape[0]
        self.terms = None

    def take(self, *earlier):
        axis = self.axes.pop(0)
        if self.terms is None:
            soon, late = (swap(each, axis) for each in self.sent)
            self.rows //= 2
            soon = tie(soon, *earlier)
            self.terms = [self.kept, late]
            self.sent = (self.kept[self.rows :].astype(F32) + soon.astype(F32)).astype(BF16)
            return self.sent
        got = swap(self.sent, axis)
        self.terms.append(tie(got, *earlier) if earlier else got)
        if not self.axes:
            return self.total(0, self.rows)
        self.rows //= 2
        self.sent = self.total(self.rows, 2 * self.rows)
        return self.sent

    def total(self, low, high):
        return functools.reduce(jnp.add, [t[low:high].astype(F32) for t in self.terms]).astype(BF16)


def mixer_grads_kernel(plane_ref, low_ref, low_other, high_ref, high_other, mix_ref, mix_other, query_ref, key_ref, value_ref, gate_ref, out_ref):
    rows = low_ref.shape[0]
    width = query_ref.shape[1]
    wide = width // 2
    own, other = (low_ref, high_ref, mix_ref), (low_other, high_other, mix_other)
    for plane in range(2):

        @pl.when(plane_ref[0] == plane)
        def _(plane=plane):
            for place, (low, high, mix) in ((plane, own), (1 - plane, other)):
                here = slice(place * rows, (place + 1) * rows)
                for i, ref in enumerate((query_ref, key_ref, value_ref)):
                    ref[here, :wide] = low[:, i * wide : (i + 1) * wide].astype(F32)
                    ref[here, wide:] = high[:, i * wide : (i + 1) * wide].astype(F32)
                out_ref[here, :] = mix[:, :width].astype(F32)
                gate_ref[here, :] = mix[:, width:].astype(F32)


def mixer_grads(plane, sums, width, deps):
    rows = 2 * sums[0].shape[0]
    arrays = [each for own in sums for each in (own, swap(own, "seq"))]
    return run(
        mixer_grads_kernel,
        (plane, *arrays),
        deps=deps,
        scalars=1,
        in_specs=[full(array.shape) for array in arrays],
        out_specs=[full((rows, width))] * 5,
        out_shape=[sds((rows, width), F32)] * 5,
        cost_estimate=cost(0.2),
        compiler_params=room(8),
        name="mixer_grads",
    )


def ff_grads_kernel(plane_ref, own_ref, other_ref, in_ref, down_ref):
    part = own_ref.shape[1] // 3
    for plane in range(2):

        @pl.when(plane_ref[0] == plane)
        def _(plane=plane):
            for place, ref in ((plane, own_ref), (1 - plane, other_ref)):
                for which, out in enumerate((in_ref, in_ref, down_ref)):
                    at = (place if which == 2 else 2 * which + place) * part
                    out[:, at : at + part] = ref[:, which * part : (which + 1) * part].astype(F32)


def ff_grads(plane, own, other):
    rows, columns = own.shape
    part = columns // 3
    return run(
        ff_grads_kernel,
        (plane, own, other),
        scalars=1,
        in_specs=[full(own.shape)] * 2,
        out_specs=[full((rows, 4 * part)), full((rows, 2 * part))],
        out_shape=[sds((rows, 4 * part), F32), sds((rows, 2 * part), F32)],
        cost_estimate=cost(0.2),
        compiler_params=room(10),
        name="ff_grads",
    )


def on_device(tokens, segments, w_query, w_key, w_value, w_gate, w_out, w_sglu_in, w_sglu_down, cotangent):
    rows, width = tokens.shape[1:]
    heads = width // HEAD_DIM
    planes = lax.axis_size("seq")
    plane = lax.axis_index("seq")
    ff = w_sglu_down.shape[1]
    part = ff // planes
    inputs, grad_tok = tokens[0], cotangent[0]
    bits = lax.axis_size("zy").bit_length() - 1
    zy = [0] + list(range(bits - 1, 0, -1))

    segs = lax.dynamic_slice_in_dim(segments[0], plane * rows, rows)
    edge = segments[0, rows - 1]
    places = jnp.arange(rows, dtype=jnp.int32)
    same = segs == edge
    from_cut = jnp.where(same, (places + 1).astype(F32), FAR)[:, None]
    to_cut = jnp.where(same, (rows - 1 - places).astype(F32), FAR)[:, None]
    seg_col, seg_row = segs[:, None], segs[None, :]

    shard = gather_shard(plane, part, (w_query, w_key, w_value, w_gate, w_out), w_sglu_in, w_sglu_down)
    weights = pltpu.with_memory_space_constraint(
        lax.all_gather(shard, ("zy", "core"), axis=0, tiled=True), pltpu.HBM
    )
    first = 5 * width

    low_axes = ["core", "seq"] + zy
    high_axes = low_axes
    ff_places, low_places, high_places = (places_of(axes) for axes in (["core"], low_axes, high_axes))

    grad_other = swap(grad_tok, "seq")
    x32 = inputs.astype(F32)
    normed_in = (x32 * row_factor(x32)).astype(BF16)

    key, k_slope, value, state = project_kv(
        normed_in, weights, to_cut, (grad_other, ff_places, low_places, high_places)
    )
    state = lax.ppermute(state, "seq", [(i, i + 1) for i in range(planes - 1)])
    query, q_slope, gate = project_qu(normed_in, weights)
    att, ahead_gate = attend_local(query, key, value, seg_col, seg_row, weights, first, part)
    mixer = (att, query, gate, inputs, state, from_cut, weights)
    top_rows, ahead_up = mix_top(*mixer, first + part, part)
    attended, gated, hidden, normed, _, bottom_rows, ahead_down = mix_out(
        *mixer, first + 2 * part, part, (top_rows,)
    )
    fetched = (ahead_gate, ahead_up, ahead_down)
    top, bottom = swap(top_rows, "seq"), swap(bottom_rows, "seq")
    half = rows // 2
    own_acts, back_own = feed_forward(F32, normed, 0, grad_tok, fetched)
    top_acts, back_top = feed_forward(BF16, top, 0, grad_other, fetched, (back_own,))
    back_top = swap(back_top, "seq")
    out_top = down_more(top_acts, fetched[2])
    bottom_acts, back_bottom = feed_forward(BF16, bottom, half, grad_other, fetched, (out_top,))
    back_bottom = swap(back_bottom, "seq")
    acts = (own_acts, top_acts, bottom_acts)

    late_ff, soon_ff, kept_ff = weight_grads(
        ff_places,
        (normed, top, bottom, grad_tok, grad_other),
        [(0, 3), (0, 3), (3, 2)],
        acts,
    )
    out_top = swap(tie(out_top, soon_ff), "seq")
    d_hidden, d_mixer, d_att, back_state = unmix(
        hidden, back_own, back_top, back_bottom, grad_tok, gate, attended, query, from_cut, weights, (soon_ff,)
    )
    back_state = lax.ppermute(back_state, "seq", [(i + 1, i) for i in range(planes - 1)])
    soon_ff, late_ff = (tie(swap(tie(each, back_top), "core"), d_mixer) for each in (soon_ff, late_ff))
    ff_part = fold(kept_ff, late_ff, soon_ff, (out_top,))
    ff_sum = lax.psum_scatter(ff_part, "zy", scatter_dimension=0, tiled=True)

    grads_mix = weight_grads(low_places, (gated, normed_in), [(0, 1), (1, 1)], (d_mixer,), None, (ff_part,))
    mixed = RowSums(low_axes, *grads_mix)
    latest = [grads_mix[0]]

    def step(*sums):
        for each in sums:
            latest[:] = [each.take(*latest)]
        return latest[0]

    dq, dk, dv = attend_back(
        query, key, value, d_att, q_slope, state, from_cut, seg_col, seg_row, (grads_mix[0],)
    )
    latest[:] = [dq, back_state]
    dqkv = join_back(dq, dk, dv, key, value, k_slope, back_state, to_cut, (step(mixed),))

    cut = heads // 2 * 3 * HEAD_DIM
    grads_low = weight_grads(low_places, (normed_in,), [(0, 1)], (dqkv,), (0, cut))
    low_heads = RowSums(low_axes, *grads_low)
    grads_high = weight_grads(high_places, (normed_in,), [(0, 1)], (dqkv,), (cut, 2 * cut), (grads_low[0],))
    high_heads = RowSums(high_axes, *grads_high)
    latest[:] = [grads_high[0]]
    out_own, out_bottom = down_project(first, part, own_acts, bottom_acts, weights, (latest[0],))
    latest[:] = [out_own]
    step(mixed, low_heads, high_heads)
    input_grad = input_grad_of(dqkv, d_mixer, weights, d_hidden, inputs, (latest[0],))
    latest[:] = [input_grad]
    out_bottom = swap(tie(out_bottom, step(mixed, low_heads, high_heads)), "seq")
    step(mixed, low_heads)
    output = add_output(hidden, out_own, out_top, out_bottom, (step(high_heads),))
    latest[:] = [output]
    ff_sum = tie(ff_sum, *latest)
    latest[:] = [ff_sum]
    while any(each.axes for each in (low_heads, high_heads, mixed)):
        for each in (mixed, low_heads, high_heads):
            if each.axes:
                step(each)
    low_sum, high_sum, mixed_sum = (each.total(0, each.rows) for each in (low_heads, high_heads, mixed))

    which = jnp.reshape(plane, (1,))
    grad_in, grad_down = ff_grads(which, ff_sum, swap(ff_sum, "seq"))
    *grads, grad_gate, grad_out = mixer_grads(which, (low_sum, high_sum, mixed_sum), width, (grad_down,))
    return (
        output[None],
        input_grad[None],
        *grads,
        grad_gate,
        grad_out,
        grad_in,
        grad_down,
    )


def solution(mesh):
    planes, group = mesh.devices.shape
    devices = mesh.devices.reshape(planes, group // 2, 2)
    split = Mesh(devices, ("seq", "zy", "core"))
    rows = ("zy", "core")
    tok = P(rows, "seq", None)
    mat = P(rows, None)
    return jax.shard_map(
        on_device,
        mesh=split,
        in_specs=(tok,) + (mat,) * 8 + (tok,),
        out_specs=(tok, tok) + (mat,) * 7,
        check_vma=False,
    )
```

```python
import functools

import jax
import jax.numpy as jnp
from jax import lax
from jax.experimental import pallas as pl
from jax.experimental.pallas import tpu as pltpu
from jax.sharding import Mesh
from jax.sharding import PartitionSpec as P

HEAD_DIM = 128
EPSILON = 1e-06
FAR = 1e9
F32 = jnp.float32
BF16 = jnp.bfloat16


def dot(left, right):
    return jnp.dot(left, right, preferred_element_type=F32)


def dot_nt(left, right):
    return lax.dot_general(left, right, (((1,), (1,)), ((), ())), preferred_element_type=F32)


def dot_tn(left, right):
    return lax.dot_general(left, right, (((0,), (0,)), ((), ())), preferred_element_type=F32)


def row_factor(values):
    return lax.rsqrt(jnp.mean(values * values, axis=-1, keepdims=True) + EPSILON)


def norm_back(values, factor, upstream):
    normed = values * factor
    return factor * (upstream - normed * jnp.mean(upstream * normed, axis=-1, keepdims=True))


def sds(shape, kind):
    return jax.ShapeDtypeStruct(shape, kind)


def full(shape):
    return pl.BlockSpec(shape, lambda *_: (0,) * len(shape))


def vmem():
    return pl.BlockSpec(memory_space=pltpu.VMEM)


def hbm():
    return pl.BlockSpec(memory_space=pltpu.HBM)


def fetch(w_ref, firsts, bufs, sem):
    copies = []
    for i, (first, buf) in enumerate(zip(firsts, bufs, strict=True)):
        copies.append(pltpu.make_async_copy(w_ref.at[:, first : first + buf.shape[1]], buf, sem.at[i]))
        copies[-1].start()
    return copies


def cost(micros):
    return pl.CostEstimate(flops=int(micros * 1.1e9), bytes_accessed=0, transcendentals=0)


def run(kernel, operands, in_specs, deps=(), scalars=0, grid=(1,), scratch=(), **options):
    given = len(operands)

    def body(*refs):
        kernel(*refs[:given], *refs[given + len(deps) :])

    return pl.pallas_call(
        body,
        grid_spec=pltpu.PrefetchScalarGridSpec(
            num_scalar_prefetch=scalars,
            grid=grid,
            in_specs=list(in_specs) + [pl.BlockSpec(memory_space=pl.ANY)] * len(deps),
            out_specs=options.pop("out_specs"),
            scratch_shapes=list(scratch),
        ),
        **options,
    )(*operands, *deps)


def room(mebibytes):
    return pltpu.CompilerParams(vmem_limit_bytes=mebibytes << 20)


def slope_of(head):
    return 0.25 * 2.0 ** (-0.5 * (head + 1))


def shard_kernel(plane_ref, *refs):
    out_ref = refs[-1]
    at = 0
    for ref in refs[:-1]:
        out_ref[:, at : at + ref.shape[1]] = ref[...]
        at += ref.shape[1]


def gather_shard(plane, part, mixer, w_in, w_down):
    rows = w_in.shape[0]
    planes = w_down.shape[1] // part
    wide = sum(w.shape[1] for w in mixer) + 3 * part
    return run(
        shard_kernel,
        (jnp.reshape(plane, (1,)), *mixer, w_in, w_in, w_down),
        scalars=1,
        in_specs=[pl.BlockSpec(w.shape, lambda i, p: (0, 0)) for w in mixer]
        + [
            pl.BlockSpec((rows, part), lambda i, p: (0, p[0])),
            pl.BlockSpec((rows, part), lambda i, p: (0, p[0] + planes)),
            pl.BlockSpec((rows, part), lambda i, p: (0, p[0])),
        ],
        out_specs=pl.BlockSpec((rows, wide), lambda i, p: (0, 0)),
        out_shape=sds((rows, wide), BF16),
        compiler_params=room(8),
        name="gather_shard",
    )


def swish_parts(pre):
    sig = jax.nn.sigmoid(pre)
    return (pre * sig).astype(BF16), (sig * (1.0 + pre * (1.0 - sig))).astype(BF16)


def kv_kernel(heads, normed_ref, w_ref, dist_ref, key_ref, slope_ref, value_ref, state_ref, wk, wv, sem):
    width = normed_ref.shape[1]
    copies = fetch(w_ref, (width, 2 * width), (wk, wv), sem)
    copies[0].wait()
    for low in range(0, width, 256):
        cols = slice(low, low + 256)
        key_ref[:, cols], slope_ref[:, cols] = swish_parts(dot(normed_ref[...], wk[:, cols]))
    copies[1].wait()
    for low in range(0, width, 256):
        cols = slice(low, low + 256)
        value_ref[:, cols] = dot(normed_ref[...], wv[:, cols]).astype(BF16)
    for head in range(heads):
        cols = slice(head * HEAD_DIM, (head + 1) * HEAD_DIM)
        weight = jnp.exp(-slope_of(head) * dist_ref[...])
        scaled = (key_ref[:, cols].astype(F32) * weight).astype(BF16)
        state_ref[cols, :] = dot_tn(scaled, value_ref[:, cols]).astype(BF16)


def project_kv(normed, weights, cut_dist, deps=()):
    rows, width = normed.shape
    heads = width // HEAD_DIM
    act = sds((rows, width), BF16)
    return run(
        functools.partial(kv_kernel, heads),
        (normed, weights, cut_dist),
        deps=deps,
        in_specs=[vmem(), hbm(), vmem()],
        out_specs=[vmem()] * 4,
        out_shape=[act, act, act, sds((width, HEAD_DIM), BF16)],
        scratch=[pltpu.VMEM((width, width), BF16)] * 2 + [pltpu.SemaphoreType.DMA((2,))],
        cost_estimate=cost(0.2),
        compiler_params=room(12),
        name="project_kv",
    )


def qu_kernel(normed_ref, w_ref, query_ref, slope_ref, gate_ref, wq, wu, sem):
    width = normed_ref.shape[1]
    copies = fetch(w_ref, (0, 3 * width), (wq, wu), sem)
    copies[0].wait()
    for low in range(0, width, 256):
        cols = slice(low, low + 256)
        query_ref[:, cols], slope_ref[:, cols] = swish_parts(dot(normed_ref[...], wq[:, cols]))
    copies[1].wait()
    for low in range(0, width, 256):
        cols = slice(low, low + 256)
        gate_ref[:, cols] = dot(normed_ref[...], wu[:, cols]).astype(BF16)


def project_qu(normed, weights):
    rows, width = normed.shape
    act = sds((rows, width), BF16)
    return run(
        qu_kernel,
        (normed, weights),
        in_specs=[vmem(), hbm()],
        out_specs=[vmem()] * 3,
        out_shape=[act, act, act],
        scratch=[pltpu.VMEM((width, width), BF16)] * 2 + [pltpu.SemaphoreType.DMA((2,))],
        cost_estimate=cost(0.2),
        compiler_params=room(12),
        name="project_qu",
    )


def distance_tables(seg_col, seg_row, dist_ref):
    rows = seg_col.shape[0]
    span = lax.broadcasted_iota(jnp.int32, (rows, rows), 0) - lax.broadcasted_iota(
        jnp.int32, (rows, rows), 1
    )
    allowed = (span >= 0) & (seg_col == seg_row)
    dist_ref[...] = jnp.where(allowed, span.astype(F32), FAR)


def attend_kernel(heads, first, q_ref, k_ref, v_ref, col_ref, row_ref, w_ref, out_ref, ahead, dist_ref, sem):
    copies = fetch(w_ref, (first,), (ahead,), sem)
    distance_tables(col_ref[...], row_ref[...], dist_ref)
    rows = q_ref.shape[0]
    half = rows // 2
    for head in range(heads):
        cols = slice(head * HEAD_DIM, (head + 1) * HEAD_DIM)
        for block in range(2):
            low, high = block * half, (block + 1) * half
            decay = jnp.exp(-slope_of(head) * dist_ref[low:high, :high])
            scores = (dot_nt(q_ref[low:high, cols], k_ref[:high, cols]) * decay).astype(BF16)
            out_ref[low:high, cols] = dot(scores, v_ref[:high, cols])
    copies[0].wait()


def attend_local(query, key, value, seg_col, seg_row, weights, first, part):
    rows, width = query.shape
    return run(
        functools.partial(attend_kernel, width // HEAD_DIM, first),
        (query, key, value, seg_col, seg_row, weights),
        in_specs=[vmem()] * 5 + [hbm()],
        out_specs=[vmem()] * 2,
        out_shape=[sds((rows, width), F32), sds((width, part), BF16)],
        scratch=[pltpu.VMEM((rows, rows), F32), pltpu.SemaphoreType.DMA((1,))],
        cost_estimate=cost(0.2),
        compiler_params=room(10),
        name="attend_local",
    )


def mix_kernel(heads, first, att_ref, q_ref, u_ref, x_ref, state_ref, dist_ref, w_ref, att_out, gated_out, hidden_out, normed_out, top_out, bottom_out, ahead, wo, sem):
    width = q_ref.shape[1]
    rows = q_ref.shape[0]
    copies = fetch(w_ref, (4 * width, first), (wo, ahead), sem)
    for head in range(heads):
        cols = slice(head * HEAD_DIM, (head + 1) * HEAD_DIM)
        weight = jnp.exp(-slope_of(head) * dist_ref[...])
        scaled = (q_ref[:, cols].astype(F32) * weight).astype(BF16)
        att_out[:, cols] = (att_ref[:, cols] + dot(scaled, state_ref[cols, :])).astype(BF16)
    copies[0].wait()
    for low in range(0, rows, 256):
        part = slice(low, low + 256)
        attended = att_out[part, :].astype(F32)
        gated = (attended * row_factor(attended) * u_ref[part, :].astype(F32)).astype(BF16)
        gated_out[part, :] = gated
        hidden = x_ref[part, :].astype(F32) + dot(gated, wo[...])
        hidden_out[part, :] = hidden
        normed = (hidden * row_factor(hidden)).astype(BF16)
        normed_out[part, :] = normed
        half_out, at = (top_out, low) if 2 * low < rows else (bottom_out, low - rows // 2)
        half_out[at : at + 256, :] = normed
    copies[1].wait()


def mix_top_kernel(heads, first, att_ref, q_ref, u_ref, x_ref, state_ref, dist_ref, w_ref, normed_out, ahead, att, wo, sem):
    width = q_ref.shape[1]
    rows = normed_out.shape[0]
    copies = fetch(w_ref, (4 * width, first), (wo, ahead), sem)
    for head in range(heads):
        cols = slice(head * HEAD_DIM, (head + 1) * HEAD_DIM)
        weight = jnp.exp(-slope_of(head) * dist_ref[:rows, :])
        scaled = (q_ref[:rows, cols].astype(F32) * weight).astype(BF16)
        att[:, cols] = (att_ref[:rows, cols] + dot(scaled, state_ref[cols, :])).astype(BF16)
    copies[0].wait()
    attended = att[...].astype(F32)
    gated = (attended * row_factor(attended) * u_ref[:rows, :].astype(F32)).astype(BF16)
    hidden = x_ref[:rows, :].astype(F32) + dot(gated, wo[...])
    normed_out[...] = (hidden * row_factor(hidden)).astype(BF16)
    copies[1].wait()


def mix_top(att, query, gate, tokens, state, cut_dist, weights, first, part):
    rows, width = query.shape
    return run(
        functools.partial(mix_top_kernel, width // HEAD_DIM, first),
        (att, query, gate, tokens, state, cut_dist, weights),
        in_specs=[vmem()] * 6 + [hbm()],
        out_specs=[vmem()] * 2,
        out_shape=[sds((rows // 2, width), BF16), sds((width, part), BF16)],
        scratch=[
            pltpu.VMEM((rows // 2, width), BF16),
            pltpu.VMEM((width, width), BF16),
            pltpu.SemaphoreType.DMA((2,)),
        ],
        cost_estimate=cost(0.2),
        compiler_params=room(12),
        name="mix_top",
    )


def mix_out(att, query, gate, tokens, state, cut_dist, weights, first, part, deps):
    rows, width = query.shape
    return run(
        functools.partial(mix_kernel, width // HEAD_DIM, first),
        (att, query, gate, tokens, state, cut_dist, weights),
        deps=deps,
        in_specs=[vmem()] * 6 + [hbm()],
        out_specs=[vmem()] * 7,
        out_shape=[sds((rows, width), kind) for kind in (BF16, BF16, F32, BF16)]
        + [sds((rows // 2, width), BF16)] * 2
        + [sds((width, part), BF16)],
        scratch=[pltpu.VMEM((width, width), BF16), pltpu.SemaphoreType.DMA((2,))],
        cost_estimate=cost(0.2),
        compiler_params=room(12),
        name="mix_out",
    )


def ff_kernel(grad_first, normed_ref, grad_ref, wg, wu, wd, acts_ref, back_ref):
    part = wg.shape[1]
    rows, width = normed_ref.shape
    for low in range(0, part, 256):
        cols = slice(low, min(low + 256, part))
        gate = dot(normed_ref[...], wg[:, cols])
        up = dot(normed_ref[...], wu[:, cols])
        d_hidden = dot(grad_ref[grad_first : grad_first + rows, :], wd[:, cols])
        for which, value in enumerate((d_hidden * up, d_hidden * gate, gate * up)):
            acts_ref[:, which * part + cols.start : which * part + cols.stop] = value.astype(BF16)
    for low in range(0, width, 256):
        block = slice(low, low + 256)
        back = dot_nt(acts_ref[:, :part], wg[block, :]) + dot_nt(acts_ref[:, part : 2 * part], wu[block, :])
        back_ref[:, block] = back.astype(back_ref.dtype)


def feed_forward(kind, normed, grad_first, grad, fetched, deps=()):
    rows, width = normed.shape
    part = fetched[0].shape[1]
    return run(
        functools.partial(ff_kernel, grad_first),
        (normed, grad, *fetched),
        deps=deps,
        in_specs=[vmem()] * 5,
        out_specs=[vmem()] * 2,
        out_shape=[sds((rows, 3 * part), BF16), sds((rows, width), kind)],
        cost_estimate=cost(0.2),
        compiler_params=room(22),
        name="feed_forward",
    )


def down_kernel(first, own_acts, other_acts, w_ref, own_ref, other_ref, wd, sem):
    part = wd.shape[1]
    width = own_ref.shape[1]
    copies = fetch(w_ref, (first + 2 * part,), (wd,), sem)
    copies[0].wait()
    for low in range(0, width, 256):
        block = slice(low, low + 256)
        own_ref[:, block] = dot_nt(own_acts[:, 2 * part :], wd[block, :])
        other_ref[:, block] = dot_nt(other_acts[:, 2 * part :], wd[block, :]).astype(BF16)


def down_project(first, part, own_acts, other_acts, weights, deps=()):
    width = weights.shape[0]
    return run(
        functools.partial(down_kernel, first),
        (own_acts, other_acts, weights),
        deps=deps,
        in_specs=[vmem()] * 2 + [hbm()],
        out_specs=[vmem()] * 2,
        out_shape=[sds((own_acts.shape[0], width), F32), sds((other_acts.shape[0], width), BF16)],
        scratch=[pltpu.VMEM((width, part), BF16), pltpu.SemaphoreType.DMA((1,))],
        cost_estimate=cost(0.2),
        compiler_params=room(12),
        name="down_project",
    )


def down_more_kernel(acts_ref, wd, out_ref):
    part = wd.shape[1]
    for low in range(0, out_ref.shape[1], 256):
        block = slice(low, low + 256)
        out_ref[:, block] = dot_nt(acts_ref[:, 2 * part :], wd[block, :]).astype(BF16)


def down_more(acts, wd):
    return run(
        down_more_kernel,
        (acts, wd),
        in_specs=[vmem()] * 2,
        out_specs=vmem(),
        out_shape=sds((acts.shape[0], wd.shape[0]), BF16),
        cost_estimate=cost(0.2),
        compiler_params=room(12),
        name="down_more",
    )


def add_kernel(hidden_ref, own_ref, top_ref, bottom_ref, out_ref):
    half = top_ref.shape[0]
    for rows, other in ((slice(0, half), top_ref), (slice(half, 2 * half), bottom_ref)):
        out_ref[rows, :] = (hidden_ref[rows, :] + own_ref[rows, :] + other[...].astype(F32)).astype(BF16)


def add_output(hidden, own, top, bottom, deps):
    return run(
        add_kernel,
        (hidden, own, top, bottom),
        deps=deps,
        in_specs=[vmem()] * 4,
        out_specs=vmem(),
        out_shape=sds(hidden.shape, BF16),
        cost_estimate=cost(1),
        compiler_params=room(8),
        name="add_output",
    )


def fold_kernel(kept_ref, late_ref, soon_ref, out_ref):
    half = late_ref.shape[0]
    out_ref[:half, :] = (kept_ref[:half, :].astype(F32) + late_ref[...].astype(F32)).astype(BF16)
    out_ref[half:, :] = (kept_ref[half:, :].astype(F32) + soon_ref[...].astype(F32)).astype(BF16)


def fold(kept, late, soon, deps):
    return run(
        fold_kernel,
        (kept, late, soon),
        deps=deps,
        in_specs=[vmem()] * 3,
        out_specs=vmem(),
        out_shape=sds(kept.shape, BF16),
        cost_estimate=cost(0.2),
        compiler_params=room(8),
        name="fold",
    )


def unmix_kernel(heads, hidden_ref, own_ref, top_ref, bottom_ref, grad_ref, u_ref, att_ref, q_ref, dist_ref, w_ref, d_hidden_out, d_mixer_out, d_att_out, state_out, wo, sem):
    rows, width = q_ref.shape
    copies = fetch(w_ref, (4 * width,), (wo,), sem)
    for low in range(0, rows, 256):
        part = slice(low, low + 256)
        hidden = hidden_ref[part, :]
        half_ref, at = (top_ref, low) if 2 * low < rows else (bottom_ref, low - rows // 2)
        upstream = own_ref[part, :] + half_ref[at : at + 256, :].astype(F32)
        d_hidden = grad_ref[part, :].astype(F32) + norm_back(hidden, row_factor(hidden), upstream)
        d_hidden_out[part, :] = d_hidden
        d_mixer_out[part, :width] = d_hidden.astype(BF16)
    copies[0].wait()
    for low in range(0, rows, 256):
        part = slice(low, low + 256)
        d_gated = dot_nt(d_mixer_out[part, :width], wo[...])
        attended = att_ref[part, :].astype(F32)
        factor = row_factor(attended)
        d_mixer_out[part, width:] = (d_gated * (attended * factor)).astype(BF16)
        d_att_out[part, :] = norm_back(attended, factor, d_gated * u_ref[part, :].astype(F32)).astype(BF16)
    for head in range(heads):
        cols = slice(head * HEAD_DIM, (head + 1) * HEAD_DIM)
        weight = jnp.exp(-slope_of(head) * dist_ref[...])
        scaled = (q_ref[:, cols].astype(F32) * weight).astype(BF16)
        state_out[cols, :] = dot_tn(scaled, d_att_out[:, cols]).astype(BF16)


def unmix(hidden, back_own, back_top, back_bottom, grad, gate, attended, query, cut_dist, weights, deps=()):
    rows, width = query.shape
    return run(
        functools.partial(unmix_kernel, width // HEAD_DIM),
        (hidden, back_own, back_top, back_bottom, grad, gate, attended, query, cut_dist, weights),
        deps=deps,
        in_specs=[vmem()] * 9 + [hbm()],
        out_specs=[vmem()] * 4,
        out_shape=[
            sds((rows, width), F32),
            sds((rows, 2 * width), BF16),
            sds((rows, width), BF16),
            sds((width, HEAD_DIM), BF16),
        ],
        scratch=[pltpu.VMEM((width, width), BF16), pltpu.SemaphoreType.DMA((1,))],
        cost_estimate=cost(60),
        compiler_params=room(14),
        name="unmix",
    )


def attend_back_kernel(heads, q_ref, k_ref, v_ref, d_ref, sq_ref, state_ref, cut_ref, col_ref, row_ref, dq_ref, dk_ref, dv_ref, dist_ref, turned_ref):
    rows = q_ref.shape[0]
    half = rows // 2
    distance_tables(col_ref[...], row_ref[...], dist_ref)
    turned_ref[...] = dist_ref[...].T
    for head in range(heads):
        cols = slice(head * HEAD_DIM, (head + 1) * HEAD_DIM)
        slope = slope_of(head)
        cut = jnp.exp(-slope * cut_ref[...])
        for block in range(2):
            low, high = block * half, (block + 1) * half
            decay = jnp.exp(-slope * dist_ref[low:high, :high])
            d_prod = (dot_nt(d_ref[low:high, cols], v_ref[:high, cols]) * decay).astype(BF16)
            d_query = dot(d_prod, k_ref[:high, cols])
            d_query += cut[low:high] * dot_nt(d_ref[low:high, cols], state_ref[cols, :])
            dq_ref[low:high, cols] = (d_query * sq_ref[low:high, cols].astype(F32)).astype(BF16)
        for block in range(2):
            low, high = block * half, (block + 1) * half
            decay = jnp.exp(-slope * turned_ref[low:high, low:])
            scores = (dot_nt(k_ref[low:high, cols], q_ref[low:, cols]) * decay).astype(BF16)
            dv_ref[low:high, cols] = dot(scores, d_ref[low:, cols])
            d_prod = (dot_nt(v_ref[low:high, cols], d_ref[low:, cols]) * decay).astype(BF16)
            dk_ref[low:high, cols] = dot(d_prod, q_ref[low:, cols])


def attend_back(query, key, value, d_att, q_slope, state, cut_dist, seg_col, seg_row, deps=()):
    rows, width = query.shape
    return run(
        functools.partial(attend_back_kernel, width // HEAD_DIM),
        (query, key, value, d_att, q_slope, state, cut_dist, seg_col, seg_row),
        deps=deps,
        in_specs=[vmem()] * 9,
        out_specs=[vmem()] * 3,
        out_shape=[sds((rows, width), kind) for kind in (BF16, F32, F32)],
        scratch=[pltpu.VMEM((rows, rows), F32)] * 2,
        cost_estimate=cost(0.2),
        compiler_params=room(12),
        name="attend_back",
    )


def join_kernel(heads, dq_ref, dk_ref, dv_ref, k_ref, v_ref, sk_ref, state_ref, cut_ref, out_ref):
    for head in range(heads):
        cols = slice(head * HEAD_DIM, (head + 1) * HEAD_DIM)
        cut = jnp.exp(-slope_of(head) * cut_ref[...])
        group = heads // 2 * HEAD_DIM
        at = head // (heads // 2) * 3 * group + head % (heads // 2) * HEAD_DIM
        out_ref[:, at : at + HEAD_DIM] = dq_ref[:, cols]
        d_key = dk_ref[:, cols] + cut * dot_nt(v_ref[:, cols], state_ref[cols, :])
        out_ref[:, at + group : at + group + HEAD_DIM] = (d_key * sk_ref[:, cols].astype(F32)).astype(BF16)
        d_value = dv_ref[:, cols] + cut * dot(k_ref[:, cols], state_ref[cols, :])
        out_ref[:, at + 2 * group : at + 2 * group + HEAD_DIM] = d_value.astype(BF16)


def join_back(dq, dk, dv, key, value, k_slope, state, cut_dist, deps=()):
    rows, width = key.shape
    return run(
        functools.partial(join_kernel, width // HEAD_DIM),
        (dq, dk, dv, key, value, k_slope, state, cut_dist),
        deps=deps,
        in_specs=[vmem()] * 8,
        out_specs=vmem(),
        out_shape=sds((rows, 3 * width), BF16),
        cost_estimate=cost(0.2),
        compiler_params=room(8),
        name="join_back",
    )


def input_kernel(dqkv_ref, dmix_ref, w_ref, dh_ref, x_ref, out_ref, *refs):
    bufs, sem = refs[:4], refs[4]
    rows, width = x_ref.shape
    half = width // 2
    copies = fetch(w_ref, [i * width for i in range(4)], bufs, sem)
    for copy in copies:
        copy.wait()
    for low in range(0, rows, 256):
        part = slice(low, low + 256)
        total = dot_nt(dmix_ref[part, width:], bufs[3][...])
        for i in range(3):
            for side in range(2):
                at = side * 3 * half + i * half
                total += dot_nt(dqkv_ref[part, at : at + half], bufs[i][:, side * half : (side + 1) * half])
        inputs = x_ref[part, :].astype(F32)
        out_ref[part, :] = dh_ref[part, :] + norm_back(inputs, row_factor(inputs), total)


def input_grad_of(dqkv, d_mixer, weights, d_hidden, tokens, deps=()):
    rows, width = tokens.shape
    return run(
        input_kernel,
        (dqkv, d_mixer, weights, d_hidden, tokens),
        deps=deps,
        in_specs=[vmem(), vmem(), hbm(), vmem(), vmem()],
        out_specs=vmem(),
        out_shape=sds((rows, width), F32),
        scratch=[pltpu.VMEM((width, width), BF16)] * 4
        + [pltpu.SemaphoreType.DMA((4,))],
        cost_estimate=cost(0.2),
        compiler_params=room(18),
        name="input_grad",
    )


def grad_kernel(jobs, wide, first, table, *refs):
    late_ref, soon_ref, keep_ref, turned = refs[-4:]
    rights = refs[max(job[0] + job[1] for job in jobs) : -4]
    width = turned.shape[0]
    half = width // 2
    rows = width // table.shape[0]
    loaded = None
    for block, job in enumerate(jobs):
        if job != loaded:
            loaded = job
            start = 0
            for source in refs[job[0] : job[0] + job[1]]:
                tokens = source.shape[0]
                for at in range(0, width, 128):
                    flat = source[:, at : at + 128].T
                    for sub in range(128 // rows):
                        place = pl.multiple_of(table[at // rows + sub] * rows, rows)
                        turned[pl.ds(place, rows), start : start + tokens] = flat[sub * rows : (sub + 1) * rows]
                start += tokens
        def columns(cols, source):
            right = jnp.concatenate([ref[:, source] for ref in rights], 0)
            keep_ref[:, cols] = dot(turned[:half, :], right).astype(BF16)
            sent = dot(turned[half:, :], right).astype(BF16)
            late_ref[:, cols] = sent[: half // 2]
            soon_ref[:, cols] = sent[half // 2 :]

        if wide * len(jobs) <= 2048:
            for low in range(block * wide, (block + 1) * wide, 256):
                columns(slice(low, low + 256), slice(first + low, first + low + 256))
            continue

        def body(j, carry, block=block, columns=columns):
            low = pl.multiple_of(block * wide + j * 512, 128)
            columns(pl.ds(low, 512), pl.ds(pl.multiple_of(first + low, 128), 512))
            return carry

        lax.fori_loop(0, wide // 512, body, 0)
        if wide % 512:
            low, high = (block + 1) * wide - wide % 512, (block + 1) * wide
            columns(slice(low, high), slice(first + low, first + high))


def places_of(axes):
    bits = lax.axis_size("zy").bit_length() - 1
    natural = list(range(bits - 1, -1, -1)) + ["core"] + (["seq"] if "seq" in axes else [])
    leaving = list(axes) + [axis for axis in natural if axis not in axes]
    owner = jnp.arange(2 ** len(natural), dtype=jnp.int32)
    place = jnp.zeros_like(owner)
    for rank, axis in enumerate(leaving):
        bit = (owner >> (len(natural) - 1 - natural.index(axis))) & 1
        if axis in axes:
            bit = bit ^ place_on(axis)
        place = place + (bit << (len(leaving) - 1 - rank))
    return place


def weight_grads(place, stacks, jobs, rights, span=None, deps=()):
    tokens, columns = sum(right.shape[0] for right in rights), rights[0].shape[1]
    if span is not None:
        columns = span[1] - span[0]
    wide = columns // len(jobs)
    width = stacks[0].shape[1]
    return run(
        functools.partial(grad_kernel, jobs, wide, 0 if span is None else span[0]),
        (place, *stacks, *rights),
        scalars=1,
        deps=deps,
        in_specs=[vmem()] * (len(stacks) + len(rights)),
        out_specs=[vmem()] * 3,
        out_shape=[sds((width // parts, columns), BF16) for parts in (4, 4, 2)],
        scratch=[pltpu.VMEM((width, tokens), BF16)],
        cost_estimate=cost(0.2),
        compiler_params=room(24 if columns > 3 * width else 12),
        name="weight_grads",
    )


def place_on(axis):
    if isinstance(axis, int):
        return (lax.axis_index("zy") >> axis) & 1
    return lax.axis_index(axis)


def swap(values, axis):
    if isinstance(axis, int):
        size = lax.axis_size("zy")
        return lax.ppermute(values, "zy", [(i, i ^ (1 << axis)) for i in range(size)])
    return lax.ppermute(values, axis, [(i, i ^ 1) for i in range(lax.axis_size(axis))])


def tie(value, *earlier):
    return lax.optimization_barrier((value, *earlier))[0]


class RowSums:
    def __init__(self, axes, late, soon, kept):
        self.axes, self.kept, self.sent = list(axes), kept, (soon, late)
        self.rows = kept.shape[0]
        self.terms = None

    def take(self, *earlier):
        axis = self.axes.pop(0)
        if self.terms is None:
            soon, late = (swap(each, axis) for each in self.sent)
            self.rows //= 2
            soon = tie(soon, *earlier)
            self.terms = [self.kept, late]
            self.sent = (self.kept[self.rows :].astype(F32) + soon.astype(F32)).astype(BF16)
            return self.sent
        got = swap(self.sent, axis)
        self.terms.append(tie(got, *earlier) if earlier else got)
        if not self.axes:
            return self.total(0, self.rows)
        self.rows //= 2
        self.sent = self.total(self.rows, 2 * self.rows)
        return self.sent

    def total(self, low, high):
        return functools.reduce(jnp.add, [t[low:high].astype(F32) for t in self.terms]).astype(BF16)


def mixer_grads_kernel(plane_ref, low_ref, low_other, high_ref, high_other, mix_ref, mix_other, query_ref, key_ref, value_ref, gate_ref, out_ref):
    rows = low_ref.shape[0]
    width = query_ref.shape[1]
    wide = width // 2
    own, other = (low_ref, high_ref, mix_ref), (low_other, high_other, mix_other)
    for plane in range(2):

        @pl.when(plane_ref[0] == plane)
        def _(plane=plane):
            for place, (low, high, mix) in ((plane, own), (1 - plane, other)):
                here = slice(place * rows, (place + 1) * rows)
                for i, ref in enumerate((query_ref, key_ref, value_ref)):
                    ref[here, :wide] = low[:, i * wide : (i + 1) * wide].astype(F32)
                    ref[here, wide:] = high[:, i * wide : (i + 1) * wide].astype(F32)
                out_ref[here, :] = mix[:, :width].astype(F32)
                gate_ref[here, :] = mix[:, width:].astype(F32)


def mixer_grads(plane, sums, width, deps):
    rows = 2 * sums[0].shape[0]
    arrays = [each for own in sums for each in (own, swap(own, "seq"))]
    return run(
        mixer_grads_kernel,
        (plane, *arrays),
        deps=deps,
        scalars=1,
        in_specs=[full(array.shape) for array in arrays],
        out_specs=[full((rows, width))] * 5,
        out_shape=[sds((rows, width), F32)] * 5,
        cost_estimate=cost(0.2),
        compiler_params=room(8),
        name="mixer_grads",
    )


def ff_grads_kernel(plane_ref, own_ref, other_ref, in_ref, down_ref):
    part = own_ref.shape[1] // 3
    for plane in range(2):

        @pl.when(plane_ref[0] == plane)
        def _(plane=plane):
            for place, ref in ((plane, own_ref), (1 - plane, other_ref)):
                for which, out in enumerate((in_ref, in_ref, down_ref)):
                    at = (place if which == 2 else 2 * which + place) * part
                    out[:, at : at + part] = ref[:, which * part : (which + 1) * part].astype(F32)


def ff_grads(plane, own, other):
    rows, columns = own.shape
    part = columns // 3
    return run(
        ff_grads_kernel,
        (plane, own, other),
        scalars=1,
        in_specs=[full(own.shape)] * 2,
        out_specs=[full((rows, 4 * part)), full((rows, 2 * part))],
        out_shape=[sds((rows, 4 * part), F32), sds((rows, 2 * part), F32)],
        cost_estimate=cost(0.2),
        compiler_params=room(10),
        name="ff_grads",
    )


def on_device(tokens, segments, w_query, w_key, w_value, w_gate, w_out, w_sglu_in, w_sglu_down, cotangent):
    rows, width = tokens.shape[1:]
    heads = width // HEAD_DIM
    planes = lax.axis_size("seq")
    plane = lax.axis_index("seq")
    ff = w_sglu_down.shape[1]
    part = ff // planes
    inputs, grad_tok = tokens[0], cotangent[0]
    bits = lax.axis_size("zy").bit_length() - 1
    zy = [0] + list(range(bits - 1, 0, -1))

    segs = lax.dynamic_slice_in_dim(segments[0], plane * rows, rows)
    edge = segments[0, rows - 1]
    places = jnp.arange(rows, dtype=jnp.int32)
    same = segs == edge
    from_cut = jnp.where(same, (places + 1).astype(F32), FAR)[:, None]
    to_cut = jnp.where(same, (rows - 1 - places).astype(F32), FAR)[:, None]
    seg_col, seg_row = segs[:, None], segs[None, :]

    shard = gather_shard(plane, part, (w_query, w_key, w_value, w_gate, w_out), w_sglu_in, w_sglu_down)
    weights = pltpu.with_memory_space_constraint(
        lax.all_gather(shard, ("zy", "core"), axis=0, tiled=True), pltpu.HBM
    )
    first = 5 * width

    low_axes = ["core", "seq"] + zy
    high_axes = low_axes
    ff_places, low_places, high_places = (places_of(axes) for axes in (["core"], low_axes, high_axes))

    grad_other = swap(grad_tok, "seq")
    x32 = inputs.astype(F32)
    normed_in = (x32 * row_factor(x32)).astype(BF16)

    key, k_slope, value, state = project_kv(
        normed_in, weights, to_cut, (grad_other, ff_places, low_places, high_places)
    )
    state = lax.ppermute(state, "seq", [(i, i + 1) for i in range(planes - 1)])
    query, q_slope, gate = project_qu(normed_in, weights)
    att, ahead_gate = attend_local(query, key, value, seg_col, seg_row, weights, first, part)
    mixer = (att, query, gate, inputs, state, from_cut, weights)
    top_rows, ahead_up = mix_top(*mixer, first + part, part)
    attended, gated, hidden, normed, _, bottom_rows, ahead_down = mix_out(
        *mixer, first + 2 * part, part, (top_rows,)
    )
    fetched = (ahead_gate, ahead_up, ahead_down)
    top, bottom = swap(top_rows, "seq"), swap(bottom_rows, "seq")
    half = rows // 2
    own_acts, back_own = feed_forward(F32, normed, 0, grad_tok, fetched)
    top_acts, back_top = feed_forward(BF16, top, 0, grad_other, fetched, (back_own,))
    back_top = swap(back_top, "seq")
    out_top = down_more(top_acts, fetched[2])
    bottom_acts, back_bottom = feed_forward(BF16, bottom, half, grad_other, fetched, (out_top,))
    back_bottom = swap(back_bottom, "seq")
    acts = (own_acts, top_acts, bottom_acts)

    late_ff, soon_ff, kept_ff = weight_grads(
        ff_places,
        (normed, top, bottom, grad_tok, grad_other),
        [(0, 3), (0, 3), (3, 2)],
        acts,
    )
    out_top = swap(tie(out_top, soon_ff), "seq")
    d_hidden, d_mixer, d_att, back_state = unmix(
        hidden, back_own, back_top, back_bottom, grad_tok, gate, attended, query, from_cut, weights, (soon_ff,)
    )
    back_state = lax.ppermute(back_state, "seq", [(i + 1, i) for i in range(planes - 1)])
    soon_ff, late_ff = (tie(swap(tie(each, back_top), "core"), d_mixer) for each in (soon_ff, late_ff))
    ff_part = fold(kept_ff, late_ff, soon_ff, (out_top,))
    ff_sum = lax.psum_scatter(ff_part, "zy", scatter_dimension=0, tiled=True)

    grads_mix = weight_grads(low_places, (gated, normed_in), [(0, 1), (1, 1)], (d_mixer,), None, (ff_part,))
    mixed = RowSums(low_axes, *grads_mix)
    latest = [grads_mix[0]]

    def step(*sums):
        for each in sums:
            latest[:] = [each.take(*latest)]
        return latest[0]

    dq, dk, dv = attend_back(
        query, key, value, d_att, q_slope, state, from_cut, seg_col, seg_row, (grads_mix[0],)
    )
    latest[:] = [dq, back_state]
    dqkv = join_back(dq, dk, dv, key, value, k_slope, back_state, to_cut, (step(mixed),))

    cut = heads // 2 * 3 * HEAD_DIM
    grads_low = weight_grads(low_places, (normed_in,), [(0, 1)], (dqkv,), (0, cut))
    low_heads = RowSums(low_axes, *grads_low)
    grads_high = weight_grads(high_places, (normed_in,), [(0, 1)], (dqkv,), (cut, 2 * cut), (grads_low[0],))
    high_heads = RowSums(high_axes, *grads_high)
    latest[:] = [grads_high[0]]
    out_own, out_bottom = down_project(first, part, own_acts, bottom_acts, weights, (latest[0],))
    latest[:] = [out_own]
    step(mixed, low_heads, high_heads)
    input_grad = input_grad_of(dqkv, d_mixer, weights, d_hidden, inputs, (latest[0],))
    latest[:] = [input_grad]
    out_bottom = swap(tie(out_bottom, step(mixed, low_heads, high_heads)), "seq")
    step(mixed, low_heads)
    output = add_output(hidden, out_own, out_top, out_bottom, (step(high_heads),))
    latest[:] = [output]
    ff_sum = tie(ff_sum, *latest)
    latest[:] = [ff_sum]
    while any(each.axes for each in (low_heads, high_heads, mixed)):
        for each in (mixed, low_heads, high_heads):
            if each.axes:
                step(each)
    low_sum, high_sum, mixed_sum = (each.total(0, each.rows) for each in (low_heads, high_heads, mixed))

    which = jnp.reshape(plane, (1,))
    grad_in, grad_down = ff_grads(which, ff_sum, swap(ff_sum, "seq"))
    *grads, grad_gate, grad_out = mixer_grads(which, (low_sum, high_sum, mixed_sum), width, (grad_down,))
    return (
        output[None],
        input_grad[None],
        *grads,
        grad_gate,
        grad_out,
        grad_in,
        grad_down,
    )


def solution(mesh):
    planes, group = mesh.devices.shape
    devices = mesh.devices.reshape(planes, group // 2, 2)
    split = Mesh(devices, ("seq", "zy", "core"))
    rows = ("zy", "core")
    tok = P(rows, "seq", None)
    mat = P(rows, None)
    return jax.shard_map(
        on_device,
        mesh=split,
        in_specs=(tok,) + (mat,) * 8 + (tok,),
        out_specs=(tok, tok) + (mat,) * 7,
        check_vma=False,
    )
```
